128 devices in a mesh: resp: 32 (over x, z, y_lo), head: 4 (over y_hi, core).
Axes of the slice: x: 4, y: 4 (y_hi: 2, y_lo: 2; y = y_hi * 2 + y_lo), z: 4, core: 2. Of those that a mesh axis runs over, the one named last changes fastest.
Arguments:
- queries: bfloat16 [32, 512, 5120], P('resp', None, 'head'), may hold values from -8 to 8
- resp_keys: bfloat16 [32, 512, 1024], P('resp', None, 'head'), may hold values from -6 to 6
- resp_values: bfloat16 [32, 512, 1024], P('resp', None, 'head'), may hold values from -6 to 6
- prompt_keys: bfloat16 [1024, 1024], P(('resp', 'head')), may hold values from -8 to 8
- prompt_values: bfloat16 [1024, 1024], P(('resp', 'head')), may hold values from -6 to 6
- lengths: int32 [32], P('resp'), may hold values from 64 to 512, as said below
- loss_mask: int32 [32, 512], P('resp'), may hold values 0 or 1
- out_grad: bfloat16 [32, 512, 5120], P('resp', None, 'head'), may hold values from -6 to 6
Outputs:
- attended: bfloat16 [32, 512, 5120], P('resp', None, 'head')
- query_grad: bfloat16 [32, 512, 5120], P('resp', None, 'head')
- key_grad: bfloat16 [32, 512, 1024], P('resp', None, 'head')
- value_grad: bfloat16 [32, 512, 1024], P('resp', None, 'head')
- prompt_key_grad: float32 [1024, 1024], P(('resp', 'head'))
- prompt_value_grad: float32 [1024, 1024], P(('resp', 'head'))
The draws below stay inside these ranges and needn't reach their ends.
Inputs may be any that keep to these rules, and one draw needn't show every extreme that they name: `lengths`: the longest response has exactly 512 live positions.
All inputs are finite; a program needn't handle non-finite values. No bound on the sum of `loss_mask` on one device may be relied on, other than what follows from the above.
Results may differ from the reference program's by a relative error of at most 0.035.
Values may be sent and summed in bfloat16 or wider, within the bound.
A program may use at most 128 MiB of HBM per device.

```python
import jax
import jax.numpy as jnp
from jax import lax

Q_HEADS = 40
KV_HEADS = 8
HEAD_DIM = 128
LMAX = 512
RESPONSES = 32
PROMPT = 1024


def draw_queries(key, part):
    row_width = Q_HEADS * HEAD_DIM
    values = jnp.clip(jax.random.normal(key, (RESPONSES, LMAX, row_width), jnp.float32), -6.0, 6.0)
    return values.astype(jnp.bfloat16)


def draw_prompt_keys(key, part):
    row_width = KV_HEADS * HEAD_DIM
    values = jnp.clip(jax.random.normal(key, (PROMPT, row_width), jnp.float32), -6.0, 6.0)
    return values.astype(jnp.bfloat16)


def draw_lengths(key, part):
    drawn = jax.random.randint(key, (RESPONSES,), LMAX // 8, LMAX + 1)
    longest = jax.random.randint(jax.random.fold_in(key, 3), (), 0, RESPONSES)
    return drawn.at[longest].set(LMAX).astype(jnp.int32)


def set_ends(entries, rng, low, high):
    index_at = [jax.random.randint(jax.random.fold_in(rng, axis), (), 0, length) for axis, length in enumerate(entries.shape)]
    widest = entries.shape.index(max(entries.shape))
    next_to = index_at[:widest] + [(index_at[widest] + 1) % entries.shape[widest]] + index_at[widest + 1:]
    return entries.at[tuple(index_at)].set(low).at[tuple(next_to)].set(high)


def shard_levels(key, extent, split, smallest, largest):
    gain = 1.0
    for dim, shards_of in split:
        draws = jax.random.uniform(jax.random.fold_in(jax.random.fold_in(key, 6), dim), (shards_of,), jnp.float32, smallest / len(split), largest / len(split))
        gain = gain * jnp.repeat(jnp.exp(draws), extent[dim] // shards_of).reshape((-1,) + (1,) * (len(extent) - 1 - dim))
    return gain


def bell_draw(rng, extent, scale, most, shards=(), held_as=jnp.bfloat16):
    entries = scale * jax.random.normal(rng, extent, jnp.float32)
    if shards:
        entries = entries * shard_levels(rng, extent, shards, -0.22, 0.18)
    return jnp.clip(entries, -most, most).astype(held_as)


def setup_inputs(seed: int = 0) -> dict:
    key_of = jax.random.split(jax.random.key(seed), 9)
    return {
        "queries": draw_queries(jax.random.fold_in(key_of[8], 71), 0),
        "resp_keys": bell_draw(key_of[1], (RESPONSES, LMAX, KV_HEADS * HEAD_DIM), 1.0, 6.0, ((0, 32), (2, 4))),
        "resp_values": bell_draw(key_of[2], (RESPONSES, LMAX, KV_HEADS * HEAD_DIM), 1.0, 6.0, ((0, 32), (2, 4))),
        "prompt_keys": draw_prompt_keys(jax.random.fold_in(key_of[8], 71), 0),
        "prompt_values": bell_draw(key_of[4], (PROMPT, KV_HEADS * HEAD_DIM), 1.0, 6.0, ((0, 128),)),
        "lengths": draw_lengths(jax.random.fold_in(key_of[8], 71), 0),
        "loss_mask": set_ends((jax.random.randint(key_of[6], (RESPONSES, LMAX), 0, 4) < 3).astype(jnp.int32), jax.random.fold_in(key_of[6], 1), 0, 1),
        "out_grad": bell_draw(key_of[7], (RESPONSES, LMAX, Q_HEADS * HEAD_DIM), 1.0, 6.0, ((0, 32), (2, 4))),
    }


def reference(queries, resp_keys, resp_values, prompt_keys, prompt_values, lengths, loss_mask, out_grad):
    group_size = Q_HEADS // KV_HEADS
    score_scale = HEAD_DIM ** -0.5
    prompt_key3 = prompt_keys.astype(jnp.float32).reshape(PROMPT, KV_HEADS, HEAD_DIM)
    prompt_value3 = prompt_values.astype(jnp.float32).reshape(PROMPT, KV_HEADS, HEAD_DIM)
    positions = jnp.arange(LMAX)

    def per_response(totals_now, inputs):
        key_total, value_total = totals_now
        query_row, key_row, value_row, length, keep_row, grad_row = inputs
        query_five = query_row.astype(jnp.float32).reshape(LMAX, KV_HEADS, group_size, HEAD_DIM)
        own_key = key_row.astype(jnp.float32).reshape(LMAX, KV_HEADS, HEAD_DIM)
        own_value = value_row.astype(jnp.float32).reshape(LMAX, KV_HEADS, HEAD_DIM)
        prompt_scores = jnp.einsum('tkgd,jkd->kgtj', query_five, prompt_key3) * score_scale
        own_scores = jnp.einsum('tkgd,jkd->kgtj', query_five, own_key) * score_scale
        allowed = (positions[None, :] <= positions[:, None]) & (positions[None, :] < length)
        own_scores = jnp.where(allowed, own_scores, -jnp.inf)
        row_top = jnp.maximum(prompt_scores.max(-1), own_scores.max(-1))
        row_total = jnp.exp(prompt_scores - row_top[..., None]).sum(-1) + jnp.exp(own_scores - row_top[..., None]).sum(-1)
        log_total = row_top + jnp.log(row_total)
        prompt_prob = jnp.exp(prompt_scores - log_total[..., None])
        own_prob = jnp.exp(own_scores - log_total[..., None])
        prompt_weight = lax.optimization_barrier(prompt_prob.astype(jnp.bfloat16)).astype(jnp.float32)
        own_weight = lax.optimization_barrier(own_prob.astype(jnp.bfloat16)).astype(jnp.float32)
        live_rows = positions < length
        attended = jnp.einsum('kgtj,jkd->tkgd', prompt_weight, prompt_value3) + jnp.einsum('kgtj,jkd->tkgd', own_weight, own_value)
        attended = jnp.where(live_rows[:, None, None, None], attended, 0.0)
        attended_low = attended.astype(jnp.bfloat16)
        attended_back = lax.optimization_barrier(attended_low).astype(jnp.float32)
        grad_factor = (keep_row * live_rows.astype(jnp.int32)).astype(jnp.float32)
        grad_five = grad_row.astype(jnp.float32).reshape(LMAX, KV_HEADS, group_size, HEAD_DIM) * grad_factor[:, None, None, None]
        row_delta = jnp.einsum('tkgd,tkgd->kgt', grad_five, attended_back)
        prompt_dprob = jnp.einsum('tkgd,jkd->kgtj', grad_five, prompt_value3)
        own_dprob = jnp.einsum('tkgd,jkd->kgtj', grad_five, own_value)
        prompt_ds = lax.optimization_barrier((prompt_prob * (prompt_dprob - row_delta[..., None]) * score_scale).astype(jnp.bfloat16)).astype(jnp.float32)
        own_ds = lax.optimization_barrier((own_prob * (own_dprob - row_delta[..., None]) * score_scale).astype(jnp.bfloat16)).astype(jnp.float32)
        query_grad = jnp.einsum('kgtj,jkd->tkgd', prompt_ds, prompt_key3) + jnp.einsum('kgtj,jkd->tkgd', own_ds, own_key)
        key_grad = jnp.einsum('kgtj,tkgd->jkd', own_ds, query_five)
        value_grad = jnp.einsum('kgtj,tkgd->jkd', own_weight, grad_five)
        key_total = key_total + jnp.einsum('kgtj,tkgd->jkd', prompt_ds, query_five)
        value_total = value_total + jnp.einsum('kgtj,tkgd->jkd', prompt_weight, grad_five)
        results = (attended_low.reshape(LMAX, Q_HEADS * HEAD_DIM),
                   query_grad.astype(jnp.bfloat16).reshape(LMAX, Q_HEADS * HEAD_DIM),
                   key_grad.astype(jnp.bfloat16).reshape(LMAX, KV_HEADS * HEAD_DIM),
                   value_grad.astype(jnp.bfloat16).reshape(LMAX, KV_HEADS * HEAD_DIM))
        return (key_total, value_total), results

    zero_total = jnp.zeros((PROMPT, KV_HEADS, HEAD_DIM), jnp.float32)
    totals_end, stacked = lax.scan(per_response, (zero_total, zero_total),
                                   (queries, resp_keys, resp_values, lengths, loss_mask, out_grad))
    attended, query_grad, key_grad, value_grad = stacked
    prompt_key_grad = totals_end[0].reshape(PROMPT, KV_HEADS * HEAD_DIM)
    prompt_value_grad = totals_end[1].reshape(PROMPT, KV_HEADS * HEAD_DIM)
    return (attended, query_grad, key_grad, value_grad, prompt_key_grad, prompt_value_grad)
```

```python
import jax
import jax.numpy as jnp
from jax import lax
from jax.sharding import PartitionSpec as P

HEAD_DIM = 128


def respond(
    query_row, key_row, value_row, length, keep_row, grad_row, prompt_key3, prompt_value3, kv_count
):
    steps_len = query_row.shape[0]
    group_size = query_row.shape[1] // (kv_count * HEAD_DIM)
    score_scale = HEAD_DIM ** (-0.5)
    positions = jnp.arange(steps_len)
    query_five = query_row.reshape(steps_len, kv_count, group_size, HEAD_DIM)
    own_key = key_row.reshape(steps_len, kv_count, HEAD_DIM)
    own_value = value_row.reshape(steps_len, kv_count, HEAD_DIM)
    prompt_scores = (
        jnp.einsum("tkgd,jkd->kgtj", query_five, prompt_key3, preferred_element_type=jnp.float32)
        * score_scale
    )
    own_scores = (
        jnp.einsum("tkgd,jkd->kgtj", query_five, own_key, preferred_element_type=jnp.float32)
        * score_scale
    )
    allowed = (positions[None, :] <= positions[:, None]) & (positions[None, :] < length)
    own_scores = jnp.where(allowed, own_scores, -jnp.inf)
    row_top = jnp.maximum(prompt_scores.max(-1), own_scores.max(-1))
    row_total = jnp.exp(prompt_scores - row_top[..., None]).sum(-1) + jnp.exp(
        own_scores - row_top[..., None]
    ).sum(-1)
    log_total = row_top + jnp.log(row_total)
    prompt_prob = jnp.exp(prompt_scores - log_total[..., None])
    own_prob = jnp.exp(own_scores - log_total[..., None])
    prompt_weight = prompt_prob.astype(jnp.bfloat16)
    own_weight = own_prob.astype(jnp.bfloat16)
    live_rows = positions < length
    attended = jnp.einsum(
        "kgtj,jkd->tkgd", prompt_weight, prompt_value3, preferred_element_type=jnp.float32
    ) + jnp.einsum("kgtj,jkd->tkgd", own_weight, own_value, preferred_element_type=jnp.float32)
    attended = jnp.where(live_rows[:, None, None, None], attended, 0.0).astype(jnp.bfloat16)
    grad_factor = (keep_row * live_rows.astype(jnp.int32)).astype(jnp.bfloat16)
    grad_five = (
        grad_row.reshape(steps_len, kv_count, group_size, HEAD_DIM)
        * grad_factor[:, None, None, None]
    )
    row_delta = jnp.einsum(
        "tkgd,tkgd->kgt", grad_five, attended, preferred_element_type=jnp.float32
    )
    prompt_dprob = jnp.einsum(
        "tkgd,jkd->kgtj", grad_five, prompt_value3, preferred_element_type=jnp.float32
    )
    own_dprob = jnp.einsum(
        "tkgd,jkd->kgtj", grad_five, own_value, preferred_element_type=jnp.float32
    )
    prompt_ds = (prompt_prob * (prompt_dprob - row_delta[..., None]) * score_scale).astype(
        jnp.bfloat16
    )
    own_ds = (own_prob * (own_dprob - row_delta[..., None]) * score_scale).astype(jnp.bfloat16)
    query_grad = jnp.einsum(
        "kgtj,jkd->tkgd", prompt_ds, prompt_key3, preferred_element_type=jnp.float32
    ) + jnp.einsum("kgtj,jkd->tkgd", own_ds, own_key, preferred_element_type=jnp.float32)
    key_grad = jnp.einsum("kgtj,tkgd->jkd", own_ds, query_five, preferred_element_type=jnp.float32)
    value_grad = jnp.einsum(
        "kgtj,tkgd->jkd", own_weight, grad_five, preferred_element_type=jnp.float32
    )
    return (
        attended.reshape(query_row.shape),
        query_grad.astype(jnp.bfloat16).reshape(query_row.shape),
        key_grad.astype(jnp.bfloat16).reshape(key_row.shape),
        value_grad.astype(jnp.bfloat16).reshape(key_row.shape),
        prompt_ds,
        prompt_weight,
        grad_five,
    )


def per_device(
    queries, resp_keys, resp_values, prompt_keys, prompt_values, lengths, loss_mask, out_grad
):
    kv_width = resp_keys.shape[2]
    kv_count = kv_width // HEAD_DIM
    rows_here = prompt_keys.shape[0]
    groups = lax.axis_size("head")
    devices = lax.axis_size("resp") * groups
    both = jnp.concatenate(
        [prompt_keys.reshape(rows_here, groups, kv_width), prompt_values.reshape(rows_here, groups, kv_width)],
        2,
    ).transpose(1, 0, 2)
    outgoing = jnp.broadcast_to(both[None], (devices // groups,) + both.shape).reshape(
        devices, rows_here, 2 * kv_width
    )
    gathered = lax.all_to_all(outgoing, ("resp", "head"), split_axis=0, concat_axis=0, tiled=True)
    gathered = gathered.reshape(devices * rows_here, 2 * kv_width)
    group_keys = gathered[:, :kv_width]
    group_values = gathered[:, kv_width:]
    prompt_rows = group_keys.shape[0]
    prompt_key3 = group_keys.reshape(prompt_rows, kv_count, HEAD_DIM)
    prompt_value3 = group_values.reshape(prompt_rows, kv_count, HEAD_DIM)

    def one_response(inputs):
        query_row, key_row, value_row, length, keep_row, grad_row = inputs
        return respond(
            query_row,
            key_row,
            value_row,
            length,
            keep_row,
            grad_row,
            prompt_key3,
            prompt_value3,
            kv_count,
        )

    results = lax.map(one_response, (queries, resp_keys, resp_values, lengths, loss_mask, out_grad))
    attended, query_grad, key_grad, value_grad, prompt_ds, prompt_weight, grad_all = results
    query_all = queries.reshape(queries.shape[0], queries.shape[1], kv_count, -1, HEAD_DIM)
    key_part = jnp.einsum(
        "rkgtj,rtkgd->jkd", prompt_ds, query_all, preferred_element_type=jnp.float32
    )
    value_part = jnp.einsum(
        "rkgtj,rtkgd->jkd", prompt_weight, grad_all, preferred_element_type=jnp.float32
    )
    both_parts = jnp.concatenate(
        [key_part.reshape(prompt_rows, kv_width), value_part.reshape(prompt_rows, kv_width)], 1
    )
    arrived = lax.all_to_all(
        both_parts.reshape(devices, rows_here, 2 * kv_width),
        ("resp", "head"),
        split_axis=0,
        concat_axis=0,
        tiled=True,
    )
    summed = arrived.reshape(devices // groups, groups, rows_here, 2 * kv_width).sum(0)
    summed = summed.transpose(1, 0, 2)
    prompt_key_grad = summed[:, :, :kv_width].reshape(rows_here, groups * kv_width)
    prompt_value_grad = summed[:, :, kv_width:].reshape(rows_here, groups * kv_width)
    return (attended, query_grad, key_grad, value_grad, prompt_key_grad, prompt_value_grad)


def solution(mesh):
    placed = (
        P("resp", None, "head"),
        P("resp", None, "head"),
        P("resp", None, "head"),
        P(("resp", "head"), None),
        P(("resp", "head"), None),
        P("resp"),
        P("resp", None),
        P("resp", None, "head"),
    )
    return jax.shard_map(
        per_device,
        mesh=mesh,
        in_specs=placed,
        out_specs=(
            P("resp", None, "head"),
            P("resp", None, "head"),
            P("resp", None, "head"),
            P("resp", None, "head"),
            P(("resp", "head"), None),
            P(("resp", "head"), None),
        ),
        check_vma=False,
    )
```

```python
import functools

import jax
import jax.numpy as jnp
from jax import lax
from jax.experimental import pallas as pl
from jax.experimental.pallas import tpu as pltpu
from jax.sharding import PartitionSpec as P

HEAD_DIM = 128
NT = (((1,), (1,)), ((), ()))
TN = (((0,), (0,)), ((), ()))


def attention_kernel(
    length_ref, q_ref, do_ref, kp_ref, vp_ref, ko_ref, vo_ref, keep_ref,
    att_ref, dq_ref, dko_ref, dvo_ref, pg_ref, dko_acc, dvo_acc,
):
    f32, bf16 = jnp.float32, jnp.bfloat16
    k = pl.program_id(0)
    g = pl.program_id(1)
    scale = HEAD_DIM ** (-0.5)
    length = length_ref[0]
    steps = q_ref.shape[0]
    q = q_ref[...]
    kp = kp_ref[...]
    ko = ko_ref[...]
    vp = vp_ref[...]
    vo = vo_ref[...]
    sp = lax.dot_general(q, kp, NT, preferred_element_type=f32) * scale
    so = lax.dot_general(q, ko, NT, preferred_element_type=f32) * scale
    t = lax.broadcasted_iota(jnp.int32, (steps, 1), 0)
    j = lax.broadcasted_iota(jnp.int32, (1, steps), 1)
    allowed = (j <= t) & (j < length)
    so = jnp.where(allowed, so, -jnp.inf)
    top = jnp.maximum(sp.max(-1, keepdims=True), so.max(-1, keepdims=True))
    total = jnp.exp(sp - top).sum(-1, keepdims=True) + jnp.exp(so - top).sum(-1, keepdims=True)
    log_total = top + jnp.log(total)
    pp = jnp.exp(sp - log_total)
    po = jnp.exp(so - log_total)
    wp = pp.astype(bf16)
    wo = po.astype(bf16)
    live = t < length
    out = jnp.dot(wp, vp, preferred_element_type=f32) + jnp.dot(wo, vo, preferred_element_type=f32)
    att = jnp.where(live, out, 0.0).astype(bf16)
    att_ref[...] = att
    factor = (keep_ref[...] * live.astype(jnp.int32)).astype(bf16)
    do = do_ref[...] * factor
    delta = (do.astype(f32) * att.astype(f32)).sum(-1, keepdims=True)
    dpp = lax.dot_general(do, vp, NT, preferred_element_type=f32)
    dpo = lax.dot_general(do, vo, NT, preferred_element_type=f32)
    dsp = (pp * (dpp - delta) * scale).astype(bf16)
    dso = (po * (dpo - delta) * scale).astype(bf16)
    dq = jnp.dot(dsp, kp, preferred_element_type=f32) + jnp.dot(dso, ko, preferred_element_type=f32)
    dq_ref[...] = dq.astype(bf16)
    dkp = lax.dot_general(dsp, q, TN, preferred_element_type=f32)
    dvp = lax.dot_general(wp, do, TN, preferred_element_type=f32)
    dko = lax.dot_general(dso, q, TN, preferred_element_type=f32)
    dvo = lax.dot_general(wo, do, TN, preferred_element_type=f32)
    width = HEAD_DIM
    kcol = pl.ds(pl.multiple_of(k * width, width), width)
    vcol = pl.ds(pl.multiple_of((k + pl.num_programs(0)) * width, width), width)

    @pl.when(g == 0)
    def _():
        dko_acc[...] = dko
        dvo_acc[...] = dvo
        pg_ref[:, kcol] = dkp
        pg_ref[:, vcol] = dvp

    @pl.when(g > 0)
    def _():
        dko_acc[...] += dko
        dvo_acc[...] += dvo
        pg_ref[:, kcol] += dkp
        pg_ref[:, vcol] += dvp

    @pl.when(g == pl.num_programs(1) - 1)
    def _():
        dko_ref[...] = dko_acc[...].astype(bf16)
        dvo_ref[...] = dvo_acc[...].astype(bf16)


def attend(length, queries, out_grad, prompt_kv, keys, values, keep, kv_count):
    steps, width = queries.shape
    group_size = width // (kv_count * HEAD_DIM)
    prompt_rows = prompt_kv.shape[0]
    head_block = lambda k, g, n: (0, k * group_size + g)
    kv_block = lambda k, g, n: (0, k)
    bf16, f32 = jnp.bfloat16, jnp.float32
    return pl.pallas_call(
        attention_kernel,
        out_shape=(
            jax.ShapeDtypeStruct((steps, width), bf16),
            jax.ShapeDtypeStruct((steps, width), bf16),
            jax.ShapeDtypeStruct(keys.shape, bf16),
            jax.ShapeDtypeStruct(keys.shape, bf16),
            jax.ShapeDtypeStruct((prompt_rows, 2 * kv_count * HEAD_DIM), f32),
        ),
        grid_spec=pltpu.PrefetchScalarGridSpec(
            num_scalar_prefetch=1,
            grid=(kv_count, group_size),
            in_specs=[
                pl.BlockSpec((steps, HEAD_DIM), head_block),
                pl.BlockSpec((steps, HEAD_DIM), head_block),
                pl.BlockSpec((prompt_rows, HEAD_DIM), kv_block),
                pl.BlockSpec((prompt_rows, HEAD_DIM), lambda k, g, n: (0, k + kv_count)),
                pl.BlockSpec((steps, HEAD_DIM), kv_block),
                pl.BlockSpec((steps, HEAD_DIM), kv_block),
                pl.BlockSpec((steps, 1), lambda k, g, n: (0, 0)),
            ],
            out_specs=[
                pl.BlockSpec((steps, HEAD_DIM), head_block),
                pl.BlockSpec((steps, HEAD_DIM), head_block),
                pl.BlockSpec((steps, HEAD_DIM), kv_block),
                pl.BlockSpec((steps, HEAD_DIM), kv_block),
                pl.BlockSpec((prompt_rows, 2 * kv_count * HEAD_DIM), lambda k, g, n: (0, 0)),
            ],
            scratch_shapes=[pltpu.VMEM((steps, HEAD_DIM), f32)] * 2,
        ),
        compiler_params=pltpu.CompilerParams(
            dimension_semantics=("arbitrary", "arbitrary"),
            vmem_limit_bytes=60 * 1024 * 1024,
        ),
    )(length, queries, out_grad, prompt_kv, prompt_kv, keys, values, keep)


def per_device(
    queries, resp_keys, resp_values, prompt_keys, prompt_values, lengths, loss_mask, out_grad
):
    kv_width = resp_keys.shape[2]
    kv_count = kv_width // HEAD_DIM
    rows_here = prompt_keys.shape[0]
    groups = lax.axis_size("head")
    devices = lax.axis_size("resp") * groups
    both = jnp.concatenate(
        [prompt_keys.reshape(rows_here, groups, kv_width), prompt_values.reshape(rows_here, groups, kv_width)],
        2,
    ).transpose(1, 0, 2)
    outgoing = jnp.broadcast_to(both[None], (devices // groups,) + both.shape).reshape(
        devices, rows_here, 2 * kv_width
    )
    gathered = lax.all_to_all(outgoing, ("resp", "head"), split_axis=0, concat_axis=0, tiled=True)
    prompt_kv = gathered.reshape(devices * rows_here, 2 * kv_width)

    steps = queries.shape[1]
    att, dq, dk, dv, prompt_parts = attend(
        lengths,
        queries.reshape(steps, -1),
        out_grad.reshape(steps, -1),
        prompt_kv,
        resp_keys.reshape(steps, kv_width),
        resp_values.reshape(steps, kv_width),
        loss_mask.reshape(steps, 1),
        kv_count,
    )
    arrived = lax.all_to_all(
        prompt_parts.reshape(devices, rows_here, 2 * kv_width),
        ("resp", "head"),
        split_axis=0,
        concat_axis=0,
        tiled=True,
    )
    summed = arrived.reshape(devices // groups, groups, rows_here, 2 * kv_width).sum(0)
    summed = summed.transpose(1, 0, 2)
    prompt_key_grad = summed[:, :, :kv_width].reshape(rows_here, groups * kv_width)
    prompt_value_grad = summed[:, :, kv_width:].reshape(rows_here, groups * kv_width)
    return (
        att.reshape(queries.shape),
        dq.reshape(queries.shape),
        dk.reshape(resp_keys.shape),
        dv.reshape(resp_keys.shape),
        prompt_key_grad,
        prompt_value_grad,
    )


def solution(mesh):
    placed = (
        P("resp", None, "head"),
        P("resp", None, "head"),
        P("resp", None, "head"),
        P(("resp", "head"), None),
        P(("resp", "head"), None),
        P("resp"),
        P("resp", None),
        P("resp", None, "head"),
    )
    return jax.shard_map(
        per_device,
        mesh=mesh,
        in_specs=placed,
        out_specs=(
            P("resp", None, "head"),
            P("resp", None, "head"),
            P("resp", None, "head"),
            P("resp", None, "head"),
            P(("resp", "head"), None),
            P(("resp", "head"), None),
        ),
        check_vma=False,
    )
```

```python
import functools

import jax
import jax.numpy as jnp
from jax import lax
from jax.experimental import pallas as pl
from jax.experimental.pallas import tpu as pltpu
from jax.sharding import PartitionSpec as P

HEAD_DIM = 128
NT = (((1,), (1,)), ((), ()))
TN = (((0,), (0,)), ((), ()))


def attention_kernel(
    length_ref, q_ref, do_ref, kp_ref, vp_ref, ko_ref, vo_ref, keep_ref,
    att_ref, dq_ref, dko_ref, dvo_ref, pg_ref, dko_acc, dvo_acc,
):
    f32, bf16 = jnp.float32, jnp.bfloat16
    k = pl.program_id(0)
    g = pl.program_id(1)
    scale = HEAD_DIM ** (-0.5)
    length = length_ref[0]
    steps = q_ref.shape[0]
    q = q_ref[...]
    kp = kp_ref[...]
    ko = ko_ref[...]
    vp = vp_ref[...]
    vo = vo_ref[...]
    sp = lax.dot_general(q, kp, NT, preferred_element_type=f32) * scale
    so = lax.dot_general(q, ko, NT, preferred_element_type=f32) * scale
    t = lax.broadcasted_iota(jnp.int32, (steps, 1), 0)
    j = lax.broadcasted_iota(jnp.int32, (1, steps), 1)
    allowed = (j <= t) & (j < length)
    so = jnp.where(allowed, so, -jnp.inf)
    top = jnp.maximum(sp.max(-1, keepdims=True), so.max(-1, keepdims=True))
    total = jnp.exp(sp - top).sum(-1, keepdims=True) + jnp.exp(so - top).sum(-1, keepdims=True)
    log_total = top + jnp.log(total)
    pp = jnp.exp(sp - log_total)
    po = jnp.exp(so - log_total)
    wp = pp.astype(bf16)
    wo = po.astype(bf16)
    live = t < length
    out = jnp.dot(wp, vp, preferred_element_type=f32) + jnp.dot(wo, vo, preferred_element_type=f32)
    att = jnp.where(live, out, 0.0).astype(bf16)
    att_ref[...] = att
    factor = (keep_ref[...] * live.astype(jnp.int32)).astype(bf16)
    do = do_ref[...] * factor
    delta = (do.astype(f32) * att.astype(f32)).sum(-1, keepdims=True)
    dpp = lax.dot_general(do, vp, NT, preferred_element_type=f32)
    dpo = lax.dot_general(do, vo, NT, preferred_element_type=f32)
    dsp = (pp * (dpp - delta) * scale).astype(bf16)
    dso = (po * (dpo - delta) * scale).astype(bf16)
    dq = jnp.dot(dsp, kp, preferred_element_type=f32) + jnp.dot(dso, ko, preferred_element_type=f32)
    dq_ref[...] = dq.astype(bf16)
    dkp = lax.dot_general(dsp, q, TN, preferred_element_type=f32)
    dvp = lax.dot_general(wp, do, TN, preferred_element_type=f32)
    dko = lax.dot_general(dso, q, TN, preferred_element_type=f32)
    dvo = lax.dot_general(wo, do, TN, preferred_element_type=f32)
    width = HEAD_DIM
    kcol = pl.ds(pl.multiple_of(k * width, width), width)
    vcol = pl.ds(pl.multiple_of((k + pl.num_programs(0)) * width, width), width)

    @pl.when(g == 0)
    def _():
        dko_acc[...] = dko
        dvo_acc[...] = dvo
        pg_ref[:, kcol] = dkp
        pg_ref[:, vcol] = dvp

    @pl.when(g > 0)
    def _():
        dko_acc[...] += dko
        dvo_acc[...] += dvo
        pg_ref[:, kcol] += dkp
        pg_ref[:, vcol] += dvp

    @pl.when(g == pl.num_programs(1) - 1)
    def _():
        dko_ref[...] = dko_acc[...].astype(bf16)
        dvo_ref[...] = dvo_acc[...].astype(bf16)


def attend(length, queries, out_grad, prompt_kv, keys, values, keep, kv_count):
    steps, width = queries.shape
    group_size = width // (kv_count * HEAD_DIM)
    prompt_rows = prompt_kv.shape[0]
    head_block = lambda k, g, n: (0, k * group_size + g)
    kv_block = lambda k, g, n: (0, k)
    bf16, f32 = jnp.bfloat16, jnp.float32
    return pl.pallas_call(
        attention_kernel,
        out_shape=(
            jax.ShapeDtypeStruct((steps, width), bf16),
            jax.ShapeDtypeStruct((steps, width), bf16),
            jax.ShapeDtypeStruct(keys.shape, bf16),
            jax.ShapeDtypeStruct(keys.shape, bf16),
            jax.ShapeDtypeStruct((prompt_rows, 2 * kv_count * HEAD_DIM), f32),
        ),
        grid_spec=pltpu.PrefetchScalarGridSpec(
            num_scalar_prefetch=1,
            grid=(kv_count, group_size),
            in_specs=[
                pl.BlockSpec((steps, HEAD_DIM), head_block),
                pl.BlockSpec((steps, HEAD_DIM), head_block),
                pl.BlockSpec((prompt_rows, HEAD_DIM), kv_block),
                pl.BlockSpec((prompt_rows, HEAD_DIM), lambda k, g, n: (0, k + kv_count)),
                pl.BlockSpec((steps, HEAD_DIM), kv_block),
                pl.BlockSpec((steps, HEAD_DIM), kv_block),
                pl.BlockSpec((steps, 1), lambda k, g, n: (0, 0)),
            ],
            out_specs=[
                pl.BlockSpec((steps, HEAD_DIM), head_block),
                pl.BlockSpec((steps, HEAD_DIM), head_block),
                pl.BlockSpec((steps, HEAD_DIM), kv_block),
                pl.BlockSpec((steps, HEAD_DIM), kv_block),
                pl.BlockSpec((prompt_rows, 2 * kv_count * HEAD_DIM), lambda k, g, n: (0, 0)),
            ],
            scratch_shapes=[pltpu.VMEM((steps, HEAD_DIM), f32)] * 2,
        ),
        compiler_params=pltpu.CompilerParams(
            dimension_semantics=("arbitrary", "arbitrary"),
            vmem_limit_bytes=60 * 1024 * 1024,
        ),
    )(length, queries, out_grad, prompt_kv, prompt_kv, keys, values, keep)


def per_device(
    queries, resp_keys, resp_values, prompt_keys, prompt_values, lengths, loss_mask, out_grad
):
    kv_width = resp_keys.shape[2]
    kv_count = kv_width // HEAD_DIM
    rows_here = prompt_keys.shape[0]
    groups = lax.axis_size("head")
    devices = lax.axis_size("resp") * groups
    both = jnp.concatenate(
        [prompt_keys.reshape(rows_here, groups, kv_width), prompt_values.reshape(rows_here, groups, kv_width)],
        2,
    ).transpose(1, 0, 2)
    outgoing = jnp.broadcast_to(both[None], (devices // groups,) + both.shape).reshape(
        devices, rows_here, 2 * kv_width
    )
    gathered = lax.all_to_all(outgoing, ("resp", "head"), split_axis=0, concat_axis=0, tiled=True)
    prompt_kv = gathered.reshape(devices * rows_here, 2 * kv_width)

    steps = queries.shape[1]
    att, dq, dk, dv, prompt_parts = attend(
        lengths,
        queries.reshape(steps, -1),
        out_grad.reshape(steps, -1),
        prompt_kv,
        resp_keys.reshape(steps, kv_width),
        resp_values.reshape(steps, kv_width),
        loss_mask.reshape(steps, 1),
        kv_count,
    )
    arrived = lax.all_to_all(
        prompt_parts.astype(jnp.bfloat16).reshape(devices, rows_here, 2 * kv_width),
        ("resp", "head"),
        split_axis=0,
        concat_axis=0,
        tiled=True,
    )
    summed = arrived.astype(jnp.float32).reshape(devices // groups, groups, rows_here, 2 * kv_width).sum(0)
    summed = summed.transpose(1, 0, 2)
    prompt_key_grad = summed[:, :, :kv_width].reshape(rows_here, groups * kv_width)
    prompt_value_grad = summed[:, :, kv_width:].reshape(rows_here, groups * kv_width)
    return (
        att.reshape(queries.shape),
        dq.reshape(queries.shape),
        dk.reshape(resp_keys.shape),
        dv.reshape(resp_keys.shape),
        prompt_key_grad,
        prompt_value_grad,
    )


def solution(mesh):
    placed = (
        P("resp", None, "head"),
        P("resp", None, "head"),
        P("resp", None, "head"),
        P(("resp", "head"), None),
        P(("resp", "head"), None),
        P("resp"),
        P("resp", None),
        P("resp", None, "head"),
    )
    return jax.shard_map(
        per_device,
        mesh=mesh,
        in_specs=placed,
        out_specs=(
            P("resp", None, "head"),
            P("resp", None, "head"),
            P("resp", None, "head"),
            P("resp", None, "head"),
            P(("resp", "head"), None),
            P(("resp", "head"), None),
        ),
        check_vma=False,
    )
```

```python
import functools

import jax
import jax.numpy as jnp
from jax import lax
from jax.experimental import pallas as pl
from jax.experimental.pallas import tpu as pltpu
from jax.sharding import PartitionSpec as P

HEAD_DIM = 128
NT = (((1,), (1,)), ((), ()))
TN = (((0,), (0,)), ((), ()))


def attention_kernel(
    n_alias, length_ref, q_ref, do_ref, kp_ref, vp_ref, ko_ref, vo_ref, keep_ref, *rest
):
    att_ref, dq_ref, dko_ref, dvo_ref, pg_ref, dko_acc, dvo_acc = rest[n_alias:]
    f32, bf16 = jnp.float32, jnp.bfloat16
    g = pl.program_id(0)
    scale = HEAD_DIM ** (-0.5)
    length = length_ref[0]
    steps = q_ref.shape[0]
    q = q_ref[...]
    kp = kp_ref[...]
    ko = ko_ref[...]
    vp = vp_ref[...]
    vo = vo_ref[...]
    sp = lax.dot_general(q, kp, NT, preferred_element_type=f32) * scale
    so = lax.dot_general(q, ko, NT, preferred_element_type=f32) * scale
    t = lax.broadcasted_iota(jnp.int32, (steps, 1), 0)
    j = lax.broadcasted_iota(jnp.int32, (1, steps), 1)
    allowed = (j <= t) & (j < length)
    so = jnp.where(allowed, so, -jnp.inf)
    top = jnp.maximum(sp.max(-1, keepdims=True), so.max(-1, keepdims=True))
    total = jnp.exp(sp - top).sum(-1, keepdims=True) + jnp.exp(so - top).sum(-1, keepdims=True)
    log_total = top + jnp.log(total)
    pp = jnp.exp(sp - log_total)
    po = jnp.exp(so - log_total)
    wp = pp.astype(bf16)
    wo = po.astype(bf16)
    live = t < length
    out = jnp.dot(wp, vp, preferred_element_type=f32) + jnp.dot(wo, vo, preferred_element_type=f32)
    att = jnp.where(live, out, 0.0).astype(bf16)
    att_ref[...] = att
    factor = (keep_ref[...] * live.astype(jnp.int32)).astype(bf16)
    do = do_ref[...] * factor
    delta = (do.astype(f32) * att.astype(f32)).sum(-1, keepdims=True)
    dpp = lax.dot_general(do, vp, NT, preferred_element_type=f32)
    dpo = lax.dot_general(do, vo, NT, preferred_element_type=f32)
    dsp = (pp * (dpp - delta) * scale).astype(bf16)
    dso = (po * (dpo - delta) * scale).astype(bf16)
    dq = jnp.dot(dsp, kp, preferred_element_type=f32) + jnp.dot(dso, ko, preferred_element_type=f32)
    dq_ref[...] = dq.astype(bf16)
    dkp = lax.dot_general(dsp, q, TN, preferred_element_type=f32)
    dvp = lax.dot_general(wp, do, TN, preferred_element_type=f32)
    dko = lax.dot_general(dso, q, TN, preferred_element_type=f32)
    dvo = lax.dot_general(wo, do, TN, preferred_element_type=f32)
    kcol = slice(0, HEAD_DIM)
    vcol = slice(HEAD_DIM, 2 * HEAD_DIM)

    @pl.when(g == 0)
    def _():
        dko_acc[...] = dko
        dvo_acc[...] = dvo
        pg_ref[:, kcol] = dkp
        pg_ref[:, vcol] = dvp

    @pl.when(g > 0)
    def _():
        dko_acc[...] += dko
        dvo_acc[...] += dvo
        pg_ref[:, kcol] += dkp
        pg_ref[:, vcol] += dvp

    @pl.when(g == pl.num_programs(0) - 1)
    def _():
        dko_ref[...] = dko_acc[...].astype(bf16)
        dvo_ref[...] = dvo_acc[...].astype(bf16)


def attend(k, length, queries, out_grad, prompt_kv, keys, values, keep, kv_count, earlier):
    steps, width = queries.shape
    group_size = width // (kv_count * HEAD_DIM)
    prompt_rows = prompt_kv.shape[0]
    head_block = lambda g, n: (0, k * group_size + g)
    kv_block = lambda g, n: (0, k)
    bf16, f32 = jnp.bfloat16, jnp.float32
    n_alias = len(earlier)
    heads_flops = 2 * steps * (prompt_rows + steps) * HEAD_DIM * 6 * group_size
    return pl.pallas_call(
        functools.partial(attention_kernel, n_alias),
        out_shape=(
            jax.ShapeDtypeStruct((steps, width), bf16),
            jax.ShapeDtypeStruct((steps, width), bf16),
            jax.ShapeDtypeStruct(keys.shape, bf16),
            jax.ShapeDtypeStruct(keys.shape, bf16),
            jax.ShapeDtypeStruct((prompt_rows, 2 * HEAD_DIM), f32),
        ),
        grid_spec=pltpu.PrefetchScalarGridSpec(
            num_scalar_prefetch=1,
            grid=(group_size,),
            in_specs=[
                pl.BlockSpec((steps, HEAD_DIM), head_block),
                pl.BlockSpec((steps, HEAD_DIM), head_block),
                pl.BlockSpec((prompt_rows, HEAD_DIM), lambda g, n: (0, 0)),
                pl.BlockSpec((prompt_rows, HEAD_DIM), lambda g, n: (0, 1)),
                pl.BlockSpec((steps, HEAD_DIM), kv_block),
                pl.BlockSpec((steps, HEAD_DIM), kv_block),
                pl.BlockSpec((steps, 1), lambda g, n: (0, 0)),
            ]
            + [pl.BlockSpec(memory_space=pl.ANY)] * n_alias,
            out_specs=[
                pl.BlockSpec((steps, HEAD_DIM), head_block),
                pl.BlockSpec((steps, HEAD_DIM), head_block),
                pl.BlockSpec((steps, HEAD_DIM), kv_block),
                pl.BlockSpec((steps, HEAD_DIM), kv_block),
                pl.BlockSpec((prompt_rows, 2 * HEAD_DIM), lambda g, n: (0, 0)),
            ],
            scratch_shapes=[pltpu.VMEM((steps, HEAD_DIM), f32)] * 2,
        ),
        input_output_aliases={8 + i: i for i in range(n_alias)},
        compiler_params=pltpu.CompilerParams(
            dimension_semantics=("arbitrary",),
            vmem_limit_bytes=60 * 1024 * 1024,
        ),
        cost_estimate=pl.CostEstimate(
            flops=heads_flops,
            transcendentals=steps * (prompt_rows + steps) * group_size,
            bytes_accessed=4 * steps * width // kv_count + 4 * prompt_rows * HEAD_DIM * 4,
        ),
    )(length, queries, out_grad, prompt_kv, prompt_kv, keys, values, keep, *earlier)


def per_device(
    queries, resp_keys, resp_values, prompt_keys, prompt_values, lengths, loss_mask, out_grad
):
    kv_width = resp_keys.shape[2]
    kv_count = kv_width // HEAD_DIM
    rows_here = prompt_keys.shape[0]
    groups = lax.axis_size("head")
    devices = lax.axis_size("resp") * groups
    steps = queries.shape[1]
    queries2 = queries.reshape(steps, -1)
    out_grad2 = out_grad.reshape(steps, -1)
    keys2 = resp_keys.reshape(steps, kv_width)
    values2 = resp_values.reshape(steps, kv_width)
    keep = loss_mask.reshape(steps, 1)
    both = jnp.stack(
        [
            prompt_keys.reshape(rows_here, groups, kv_count, HEAD_DIM),
            prompt_values.reshape(rows_here, groups, kv_count, HEAD_DIM),
        ],
        3,
    )
    earlier = ()
    grads = []
    for k in range(kv_count):
        mine = both[:, :, k].transpose(1, 0, 2, 3).reshape(groups, rows_here, 2 * HEAD_DIM)
        outgoing = jnp.broadcast_to(mine[None], (devices // groups,) + mine.shape).reshape(
            devices, rows_here, 2 * HEAD_DIM
        )
        gathered = lax.all_to_all(outgoing, ("resp", "head"), split_axis=0, concat_axis=0, tiled=True)
        prompt_kv = gathered.reshape(devices * rows_here, 2 * HEAD_DIM)
        *earlier, prompt_parts = attend(
            k, lengths, queries2, out_grad2, prompt_kv, keys2, values2, keep, kv_count, tuple(earlier)
        )
        arrived = lax.all_to_all(
            prompt_parts.astype(jnp.bfloat16).reshape(devices, rows_here, 2 * HEAD_DIM),
            ("resp", "head"),
            split_axis=0,
            concat_axis=0,
            tiled=True,
        )
        grads.append(
            arrived.astype(jnp.float32).reshape(devices // groups, groups, rows_here, 2, HEAD_DIM).sum(0)
        )
    att, dq, dk, dv = earlier
    summed = jnp.stack(grads, 3).transpose(2, 1, 0, 3, 4)
    prompt_key_grad = summed[0].reshape(rows_here, groups * kv_width)
    prompt_value_grad = summed[1].reshape(rows_here, groups * kv_width)
    return (
        att.reshape(queries.shape),
        dq.reshape(queries.shape),
        dk.reshape(resp_keys.shape),
        dv.reshape(resp_keys.shape),
        prompt_key_grad,
        prompt_value_grad,
    )


def solution(mesh):
    placed = (
        P("resp", None, "head"),
        P("resp", None, "head"),
        P("resp", None, "head"),
        P(("resp", "head"), None),
        P(("resp", "head"), None),
        P("resp"),
        P("resp", None),
        P("resp", None, "head"),
    )
    return jax.shard_map(
        per_device,
        mesh=mesh,
        in_specs=placed,
        out_specs=(
            P("resp", None, "head"),
            P("resp", None, "head"),
            P("resp", None, "head"),
            P("resp", None, "head"),
            P(("resp", "head"), None),
            P(("resp", "head"), None),
        ),
        check_vma=False,
    )
```

```python
import functools

import jax
import jax.numpy as jnp
from jax import lax
from jax.experimental import pallas as pl
from jax.experimental.pallas import tpu as pltpu
from jax.sharding import PartitionSpec as P

HEAD_DIM = 128
NT = (((1,), (1,)), ((), ()))
TN = (((0,), (0,)), ((), ()))


def attention_kernel(
    length_ref, q_ref, do_ref, kp_ref, vp_ref, ko_ref, vo_ref, keep_ref,
    att_ref, dq_ref, dko_ref, dvo_ref, pg_ref, dko_acc, dvo_acc,
):
    f32, bf16 = jnp.float32, jnp.bfloat16
    k = pl.program_id(0)
    g = pl.program_id(1)
    scale = HEAD_DIM ** (-0.5)
    length = length_ref[0]
    steps = q_ref.shape[0]
    q = q_ref[...]
    kp = kp_ref[...]
    ko = ko_ref[...]
    vp = vp_ref[...]
    vo = vo_ref[...]
    sp = lax.dot_general(q, kp, NT, preferred_element_type=f32) * scale
    so = lax.dot_general(q, ko, NT, preferred_element_type=f32) * scale
    t = lax.broadcasted_iota(jnp.int32, (steps, 1), 0)
    j = lax.broadcasted_iota(jnp.int32, (1, steps), 1)
    allowed = (j <= t) & (j < length)
    so = jnp.where(allowed, so, -jnp.inf)
    top = jnp.maximum(sp.max(-1, keepdims=True), so.max(-1, keepdims=True))
    ep = jnp.exp(sp - top)
    eo = jnp.exp(so - top)
    inverse = 1.0 / (ep.sum(-1, keepdims=True) + eo.sum(-1, keepdims=True))
    pp = ep * inverse
    po = eo * inverse
    wp = pp.astype(bf16)
    wo = po.astype(bf16)
    live = t < length
    out = jnp.dot(wp, vp, preferred_element_type=f32) + jnp.dot(wo, vo, preferred_element_type=f32)
    att = jnp.where(live, out, 0.0).astype(bf16)
    att_ref[...] = att
    factor = (keep_ref[...] * live.astype(jnp.int32)).astype(bf16)
    do = do_ref[...] * factor
    delta = (do.astype(f32) * att.astype(f32)).sum(-1, keepdims=True)
    dpp = lax.dot_general(do, vp, NT, preferred_element_type=f32)
    dpo = lax.dot_general(do, vo, NT, preferred_element_type=f32)
    dsp = (pp * (dpp - delta)).astype(bf16)
    dso = (po * (dpo - delta)).astype(bf16)
    dq = jnp.dot(dsp, kp, preferred_element_type=f32) + jnp.dot(dso, ko, preferred_element_type=f32)
    dq_ref[...] = (dq * scale).astype(bf16)
    dkp = lax.dot_general(dsp, q, TN, preferred_element_type=f32) * scale
    dvp = lax.dot_general(wp, do, TN, preferred_element_type=f32)
    dko = lax.dot_general(dso, q, TN, preferred_element_type=f32) * scale
    dvo = lax.dot_general(wo, do, TN, preferred_element_type=f32)
    width = HEAD_DIM
    kcol = pl.ds(pl.multiple_of(k * width, width), width)
    vcol = pl.ds(pl.multiple_of((k + pl.num_programs(0)) * width, width), width)

    @pl.when(g == 0)
    def _():
        dko_acc[...] = dko
        dvo_acc[...] = dvo
        pg_ref[:, kcol] = dkp
        pg_ref[:, vcol] = dvp

    @pl.when(g > 0)
    def _():
        dko_acc[...] += dko
        dvo_acc[...] += dvo
        pg_ref[:, kcol] += dkp
        pg_ref[:, vcol] += dvp

    @pl.when(g == pl.num_programs(1) - 1)
    def _():
        dko_ref[...] = dko_acc[...].astype(bf16)
        dvo_ref[...] = dvo_acc[...].astype(bf16)


def attend(length, queries, out_grad, prompt_kv, keys, values, keep, kv_count):
    steps, width = queries.shape
    group_size = width // (kv_count * HEAD_DIM)
    prompt_rows = prompt_kv.shape[0]
    head_block = lambda k, g, n: (0, k * group_size + g)
    kv_block = lambda k, g, n: (0, k)
    bf16, f32 = jnp.bfloat16, jnp.float32
    return pl.pallas_call(
        attention_kernel,
        out_shape=(
            jax.ShapeDtypeStruct((steps, width), bf16),
            jax.ShapeDtypeStruct((steps, width), bf16),
            jax.ShapeDtypeStruct(keys.shape, bf16),
            jax.ShapeDtypeStruct(keys.shape, bf16),
            jax.ShapeDtypeStruct((prompt_rows, 2 * kv_count * HEAD_DIM), f32),
        ),
        grid_spec=pltpu.PrefetchScalarGridSpec(
            num_scalar_prefetch=1,
            grid=(kv_count, group_size),
            in_specs=[
                pl.BlockSpec((steps, HEAD_DIM), head_block),
                pl.BlockSpec((steps, HEAD_DIM), head_block),
                pl.BlockSpec((prompt_rows, HEAD_DIM), kv_block),
                pl.BlockSpec((prompt_rows, HEAD_DIM), lambda k, g, n: (0, k + kv_count)),
                pl.BlockSpec((steps, HEAD_DIM), kv_block),
                pl.BlockSpec((steps, HEAD_DIM), kv_block),
                pl.BlockSpec((steps, 1), lambda k, g, n: (0, 0)),
            ],
            out_specs=[
                pl.BlockSpec((steps, HEAD_DIM), head_block),
                pl.BlockSpec((steps, HEAD_DIM), head_block),
                pl.BlockSpec((steps, HEAD_DIM), kv_block),
                pl.BlockSpec((steps, HEAD_DIM), kv_block),
                pl.BlockSpec((prompt_rows, 2 * kv_count * HEAD_DIM), lambda k, g, n: (0, 0)),
            ],
            scratch_shapes=[pltpu.VMEM((steps, HEAD_DIM), f32)] * 2,
        ),
        compiler_params=pltpu.CompilerParams(
            dimension_semantics=("arbitrary", "arbitrary"),
            vmem_limit_bytes=60 * 1024 * 1024,
        ),
    )(length, queries, out_grad, prompt_kv, prompt_kv, keys, values, keep)


def per_device(
    queries, resp_keys, resp_values, prompt_keys, prompt_values, lengths, loss_mask, out_grad
):
    kv_width = resp_keys.shape[2]
    kv_count = kv_width // HEAD_DIM
    rows_here = prompt_keys.shape[0]
    groups = lax.axis_size("head")
    devices = lax.axis_size("resp") * groups
    both = jnp.concatenate(
        [prompt_keys.reshape(rows_here, groups, kv_width), prompt_values.reshape(rows_here, groups, kv_width)],
        2,
    ).transpose(1, 0, 2)
    outgoing = jnp.broadcast_to(both[None], (devices // groups,) + both.shape).reshape(
        devices, rows_here, 2 * kv_width
    )
    gathered = lax.all_to_all(outgoing, ("resp", "head"), split_axis=0, concat_axis=0, tiled=True)
    prompt_kv = gathered.reshape(devices * rows_here, 2 * kv_width)

    steps = queries.shape[1]
    att, dq, dk, dv, prompt_parts = attend(
        lengths,
        queries.reshape(steps, -1),
        out_grad.reshape(steps, -1),
        prompt_kv,
        resp_keys.reshape(steps, kv_width),
        resp_values.reshape(steps, kv_width),
        loss_mask.reshape(steps, 1),
        kv_count,
    )
    arrived = lax.all_to_all(
        prompt_parts.astype(jnp.bfloat16).reshape(devices, rows_here, 2 * kv_width),
        ("resp", "head"),
        split_axis=0,
        concat_axis=0,
        tiled=True,
    )
    summed = arrived.astype(jnp.float32).reshape(devices // groups, groups, rows_here, 2 * kv_width).sum(0)
    summed = summed.transpose(1, 0, 2)
    prompt_key_grad = summed[:, :, :kv_width].reshape(rows_here, groups * kv_width)
    prompt_value_grad = summed[:, :, kv_width:].reshape(rows_here, groups * kv_width)
    return (
        att.reshape(queries.shape),
        dq.reshape(queries.shape),
        dk.reshape(resp_keys.shape),
        dv.reshape(resp_keys.shape),
        prompt_key_grad,
        prompt_value_grad,
    )


def solution(mesh):
    placed = (
        P("resp", None, "head"),
        P("resp", None, "head"),
        P("resp", None, "head"),
        P(("resp", "head"), None),
        P(("resp", "head"), None),
        P("resp"),
        P("resp", None),
        P("resp", None, "head"),
    )
    return jax.shard_map(
        per_device,
        mesh=mesh,
        in_specs=placed,
        out_specs=(
            P("resp", None, "head"),
            P("resp", None, "head"),
            P("resp", None, "head"),
            P("resp", None, "head"),
            P(("resp", "head"), None),
            P(("resp", "head"), None),
        ),
        check_vma=False,
    )
```

```python
import functools

import jax
import jax.numpy as jnp
from jax import lax
from jax.experimental import pallas as pl
from jax.experimental.pallas import tpu as pltpu
from jax.sharding import PartitionSpec as P

HEAD_DIM = 128
NT = (((1,), (1,)), ((), ()))
TN = (((0,), (0,)), ((), ()))


def attention_kernel(
    length_ref, q_ref, do_ref, kp_ref, vp_ref, ko_ref, vo_ref, keep_col_ref,
    att_ref, dq_ref, dko_ref, dvo_ref, pg_ref, dko_acc, dvo_acc,
):
    f32, bf16 = jnp.float32, jnp.bfloat16
    k = pl.program_id(0)
    g = pl.program_id(1)
    scale = HEAD_DIM ** (-0.5)
    length = length_ref[0]
    steps = q_ref.shape[0]
    q = q_ref[...]
    kp = kp_ref[...]
    ko = ko_ref[...]
    vp = vp_ref[...]
    vo = vo_ref[...]
    sp = lax.dot_general(kp, q, NT, preferred_element_type=f32) * scale
    so = lax.dot_general(ko, q, NT, preferred_element_type=f32) * scale
    j = lax.broadcasted_iota(jnp.int32, (steps, 1), 0)
    t = lax.broadcasted_iota(jnp.int32, (1, steps), 1)
    allowed = (j <= t) & (j < length)
    so = jnp.where(allowed, so, -jnp.inf)
    top = jnp.maximum(sp.max(0, keepdims=True), so.max(0, keepdims=True))
    ep = jnp.exp(sp - top)
    eo = jnp.exp(so - top)
    inverse = 1.0 / (ep.sum(0, keepdims=True) + eo.sum(0, keepdims=True))
    pp = ep * inverse
    po = eo * inverse
    wp = pp.astype(bf16)
    wo = po.astype(bf16)
    live = t < length
    out = lax.dot_general(vp, wp, TN, preferred_element_type=f32) + lax.dot_general(
        vo, wo, TN, preferred_element_type=f32
    )
    att = jnp.where(live, out, 0.0).astype(bf16).astype(f32)
    att_ref[...] = att.T.astype(bf16)
    live_col = lax.broadcasted_iota(jnp.int32, (steps, 1), 0) < length
    factor = (keep_col_ref[...] * live_col.astype(jnp.int32)).astype(bf16)
    do = do_ref[...] * factor
    delta = (do.astype(f32).T * att).sum(0, keepdims=True)
    dpp = lax.dot_general(vp, do, NT, preferred_element_type=f32)
    dpo = lax.dot_general(vo, do, NT, preferred_element_type=f32)
    dsp = (pp * (dpp - delta)).astype(bf16)
    dso = (po * (dpo - delta)).astype(bf16)
    dq = lax.dot_general(kp, dsp, TN, preferred_element_type=f32) + lax.dot_general(
        ko, dso, TN, preferred_element_type=f32
    )
    dq_ref[...] = (dq * scale).T.astype(bf16)
    dkp = jnp.dot(dsp, q, preferred_element_type=f32) * scale
    dvp = jnp.dot(wp, do, preferred_element_type=f32)
    dko = jnp.dot(dso, q, preferred_element_type=f32) * scale
    dvo = jnp.dot(wo, do, preferred_element_type=f32)
    width = HEAD_DIM
    kcol = pl.ds(pl.multiple_of(k * width, width), width)
    vcol = pl.ds(pl.multiple_of((k + pl.num_programs(0)) * width, width), width)

    @pl.when(g == 0)
    def _():
        dko_acc[...] = dko
        dvo_acc[...] = dvo
        pg_ref[:, kcol] = dkp
        pg_ref[:, vcol] = dvp

    @pl.when(g > 0)
    def _():
        dko_acc[...] += dko
        dvo_acc[...] += dvo
        pg_ref[:, kcol] += dkp
        pg_ref[:, vcol] += dvp

    @pl.when(g == pl.num_programs(1) - 1)
    def _():
        dko_ref[...] = dko_acc[...].astype(bf16)
        dvo_ref[...] = dvo_acc[...].astype(bf16)


def attend(length, queries, out_grad, prompt_kv, keys, values, keep, kv_count):
    steps, width = queries.shape
    group_size = width // (kv_count * HEAD_DIM)
    prompt_rows = prompt_kv.shape[0]
    head_block = lambda k, g, n: (0, k * group_size + g)
    kv_block = lambda k, g, n: (0, k)
    bf16, f32 = jnp.bfloat16, jnp.float32
    return pl.pallas_call(
        attention_kernel,
        out_shape=(
            jax.ShapeDtypeStruct((steps, width), bf16),
            jax.ShapeDtypeStruct((steps, width), bf16),
            jax.ShapeDtypeStruct(keys.shape, bf16),
            jax.ShapeDtypeStruct(keys.shape, bf16),
            jax.ShapeDtypeStruct((prompt_rows, 2 * kv_count * HEAD_DIM), f32),
        ),
        grid_spec=pltpu.PrefetchScalarGridSpec(
            num_scalar_prefetch=1,
            grid=(kv_count, group_size),
            in_specs=[
                pl.BlockSpec((steps, HEAD_DIM), head_block),
                pl.BlockSpec((steps, HEAD_DIM), head_block),
                pl.BlockSpec((prompt_rows, HEAD_DIM), kv_block),
                pl.BlockSpec((prompt_rows, HEAD_DIM), lambda k, g, n: (0, k + kv_count)),
                pl.BlockSpec((steps, HEAD_DIM), kv_block),
                pl.BlockSpec((steps, HEAD_DIM), kv_block),
                pl.BlockSpec((steps, 1), lambda k, g, n: (0, 0)),
            ],
            out_specs=[
                pl.BlockSpec((steps, HEAD_DIM), head_block),
                pl.BlockSpec((steps, HEAD_DIM), head_block),
                pl.BlockSpec((steps, HEAD_DIM), kv_block),
                pl.BlockSpec((steps, HEAD_DIM), kv_block),
                pl.BlockSpec((prompt_rows, 2 * kv_count * HEAD_DIM), lambda k, g, n: (0, 0)),
            ],
            scratch_shapes=[pltpu.VMEM((steps, HEAD_DIM), f32)] * 2,
        ),
        compiler_params=pltpu.CompilerParams(
            dimension_semantics=("arbitrary", "arbitrary"),
            vmem_limit_bytes=60 * 1024 * 1024,
        ),
    )(length, queries, out_grad, prompt_kv, prompt_kv, keys, values, keep)


def per_device(
    queries, resp_keys, resp_values, prompt_keys, prompt_values, lengths, loss_mask, out_grad
):
    kv_width = resp_keys.shape[2]
    kv_count = kv_width // HEAD_DIM
    rows_here = prompt_keys.shape[0]
    groups = lax.axis_size("head")
    devices = lax.axis_size("resp") * groups
    both = jnp.concatenate(
        [prompt_keys.reshape(rows_here, groups, kv_width), prompt_values.reshape(rows_here, groups, kv_width)],
        2,
    ).transpose(1, 0, 2)
    outgoing = jnp.broadcast_to(both[None], (devices // groups,) + both.shape).reshape(
        devices, rows_here, 2 * kv_width
    )
    gathered = lax.all_to_all(outgoing, ("resp", "head"), split_axis=0, concat_axis=0, tiled=True)
    prompt_kv = gathered.reshape(devices * rows_here, 2 * kv_width)

    steps = queries.shape[1]
    att, dq, dk, dv, prompt_parts = attend(
        lengths,
        queries.reshape(steps, -1),
        out_grad.reshape(steps, -1),
        prompt_kv,
        resp_keys.reshape(steps, kv_width),
        resp_values.reshape(steps, kv_width),
        loss_mask.reshape(steps, 1),
        kv_count,
    )
    arrived = lax.all_to_all(
        prompt_parts.astype(jnp.bfloat16).reshape(devices, rows_here, 2 * kv_width),
        ("resp", "head"),
        split_axis=0,
        concat_axis=0,
        tiled=True,
    )
    summed = arrived.astype(jnp.float32).reshape(devices // groups, groups, rows_here, 2 * kv_width).sum(0)
    summed = summed.transpose(1, 0, 2)
    prompt_key_grad = summed[:, :, :kv_width].reshape(rows_here, groups * kv_width)
    prompt_value_grad = summed[:, :, kv_width:].reshape(rows_here, groups * kv_width)
    return (
        att.reshape(queries.shape),
        dq.reshape(queries.shape),
        dk.reshape(resp_keys.shape),
        dv.reshape(resp_keys.shape),
        prompt_key_grad,
        prompt_value_grad,
    )


def solution(mesh):
    placed = (
        P("resp", None, "head"),
        P("resp", None, "head"),
        P("resp", None, "head"),
        P(("resp", "head"), None),
        P(("resp", "head"), None),
        P("resp"),
        P("resp", None),
        P("resp", None, "head"),
    )
    return jax.shard_map(
        per_device,
        mesh=mesh,
        in_specs=placed,
        out_specs=(
            P("resp", None, "head"),
            P("resp", None, "head"),
            P("resp", None, "head"),
            P("resp", None, "head"),
            P(("resp", "head"), None),
            P(("resp", "head"), None),
        ),
        check_vma=False,
    )
```

```python
import functools

import jax
import jax.numpy as jnp
from jax import lax
from jax.experimental import pallas as pl
from jax.experimental.pallas import tpu as pltpu
from jax.sharding import PartitionSpec as P

HEAD_DIM = 128
NT = (((1,), (1,)), ((), ()))
TN = (((0,), (0,)), ((), ()))


def attention_kernel(
    length_ref, q_ref, do_ref, kp_ref, vp_ref, ko_ref, vo_ref, keep_col_ref,
    att_ref, dq_ref, dko_ref, dvo_ref, pg_ref, dko_acc, dvo_acc,
):
    f32, bf16 = jnp.float32, jnp.bfloat16
    k = pl.program_id(0)
    g = pl.program_id(1)
    scale = HEAD_DIM ** (-0.5)
    length = length_ref[0]
    steps = q_ref.shape[0]
    q = q_ref[...]
    kp = kp_ref[...]
    ko = ko_ref[...]
    vp = vp_ref[...]
    vo = vo_ref[...]
    sp = lax.dot_general(kp, q, NT, preferred_element_type=f32) * scale
    so = lax.dot_general(ko, q, NT, preferred_element_type=f32) * scale
    j = lax.broadcasted_iota(jnp.int32, (steps, 1), 0)
    t = lax.broadcasted_iota(jnp.int32, (1, steps), 1)
    allowed = (j <= t) & (j < length)
    so = jnp.where(allowed, so, -jnp.inf)
    top = jnp.maximum(sp.max(0, keepdims=True), so.max(0, keepdims=True))
    ep = jnp.exp(sp - top)
    eo = jnp.exp(so - top)
    inverse = 1.0 / (ep.sum(0, keepdims=True) + eo.sum(0, keepdims=True))
    pp = ep * inverse
    po = eo * inverse
    wp = pp.astype(bf16)
    wo = po.astype(bf16)
    live = t < length
    out = lax.dot_general(vp, wp, TN, preferred_element_type=f32) + lax.dot_general(
        vo, wo, TN, preferred_element_type=f32
    )
    att = jnp.where(live, out, 0.0).astype(bf16).astype(f32)
    att_ref[...] = att.T.astype(bf16)
    live_col = lax.broadcasted_iota(jnp.int32, (steps, 1), 0) < length
    factor = (keep_col_ref[...] * live_col.astype(jnp.int32)).astype(bf16)
    do = do_ref[...] * factor
    delta = (do.astype(f32).T * att).sum(0, keepdims=True)
    dpp = lax.dot_general(vp, do, NT, preferred_element_type=f32)
    dpo = lax.dot_general(vo, do, NT, preferred_element_type=f32)
    dsp = (pp * (dpp - delta)).astype(bf16)
    dso = (po * (dpo - delta)).astype(bf16)
    dq = lax.dot_general(kp, dsp, TN, preferred_element_type=f32) + lax.dot_general(
        ko, dso, TN, preferred_element_type=f32
    )
    dq_ref[...] = (dq * scale).T.astype(bf16)
    dkp = jnp.dot(dsp, q, preferred_element_type=f32) * scale
    dvp = jnp.dot(wp, do, preferred_element_type=f32)
    dko = jnp.dot(dso, q, preferred_element_type=f32) * scale
    dvo = jnp.dot(wo, do, preferred_element_type=f32)
    width = HEAD_DIM
    kcol = pl.ds(pl.multiple_of(k * width, width), width)
    vcol = pl.ds(pl.multiple_of((k + pl.num_programs(0)) * width, width), width)

    @pl.when(g == 0)
    def _():
        dko_acc[...] = dko
        dvo_acc[...] = dvo
        pg_ref[:, kcol] = dkp
        pg_ref[:, vcol] = dvp

    @pl.when(g > 0)
    def _():
        dko_acc[...] += dko
        dvo_acc[...] += dvo
        pg_ref[:, kcol] += dkp
        pg_ref[:, vcol] += dvp

    @pl.when(g == pl.num_programs(1) - 1)
    def _():
        dko_ref[...] = dko_acc[...].astype(bf16)
        dvo_ref[...] = dvo_acc[...].astype(bf16)


def attend(length, queries, out_grad, prompt_kv, keys, values, keep, kv_count):
    steps, width = queries.shape
    group_size = width // (kv_count * HEAD_DIM)
    prompt_rows = prompt_kv.shape[0]
    head_block = lambda k, g, n: (0, k * group_size + g)
    kv_block = lambda k, g, n: (0, k)
    bf16, f32 = jnp.bfloat16, jnp.float32
    return pl.pallas_call(
        attention_kernel,
        out_shape=(
            jax.ShapeDtypeStruct((steps, width), bf16),
            jax.ShapeDtypeStruct((steps, width), bf16),
            jax.ShapeDtypeStruct(keys.shape, bf16),
            jax.ShapeDtypeStruct(keys.shape, bf16),
            jax.ShapeDtypeStruct((prompt_rows, 2 * kv_count * HEAD_DIM), f32),
        ),
        grid_spec=pltpu.PrefetchScalarGridSpec(
            num_scalar_prefetch=1,
            grid=(kv_count, group_size),
            in_specs=[
                pl.BlockSpec((steps, HEAD_DIM), head_block),
                pl.BlockSpec((steps, HEAD_DIM), head_block),
                pl.BlockSpec((prompt_rows, HEAD_DIM), kv_block),
                pl.BlockSpec((prompt_rows, HEAD_DIM), lambda k, g, n: (0, k + kv_count)),
                pl.BlockSpec((steps, HEAD_DIM), kv_block),
                pl.BlockSpec((steps, HEAD_DIM), kv_block),
                pl.BlockSpec((steps, 1), lambda k, g, n: (0, 0)),
            ],
            out_specs=[
                pl.BlockSpec((steps, HEAD_DIM), head_block),
                pl.BlockSpec((steps, HEAD_DIM), head_block),
                pl.BlockSpec((steps, HEAD_DIM), kv_block),
                pl.BlockSpec((steps, HEAD_DIM), kv_block),
                pl.BlockSpec((prompt_rows, 2 * kv_count * HEAD_DIM), lambda k, g, n: (0, 0)),
            ],
            scratch_shapes=[pltpu.VMEM((steps, HEAD_DIM), f32)] * 2,
        ),
        compiler_params=pltpu.CompilerParams(
            dimension_semantics=("arbitrary", "arbitrary"),
            vmem_limit_bytes=60 * 1024 * 1024,
        ),
    )(length, queries, out_grad, prompt_kv, prompt_kv, keys, values, keep)


def exchange_kernel(n_head, x_ref, o_ref, send_sem, recv_sem):
    count = x_ref.shape[0]
    me = lax.axis_index("resp") * n_head + lax.axis_index("head")
    barrier = pltpu.get_barrier_semaphore()

    def where(d):
        return (d // n_head, d % n_head)

    def greet(d, carry):
        @pl.when(d != me)
        def _():
            pl.semaphore_signal(barrier, 1, device_id=where(d), device_id_type=pl.DeviceIdType.MESH)

        return carry

    lax.fori_loop(0, count, greet, 0)
    pl.semaphore_wait(barrier, count - 1)

    def send(d):
        return pltpu.make_async_remote_copy(
            src_ref=x_ref.at[d],
            dst_ref=o_ref.at[me],
            send_sem=send_sem.at[d],
            recv_sem=recv_sem.at[me],
            device_id=where(d),
            device_id_type=pl.DeviceIdType.MESH,
        )

    def start(d, carry):
        @pl.when(d != me)
        def _():
            send(d).start()

        return carry

    lax.fori_loop(0, count, start, 0)
    o_ref[me] = x_ref[me]

    def finish(d, carry):
        @pl.when(d != me)
        def _():
            send(d).wait_send()
            pltpu.make_async_remote_copy(
                src_ref=x_ref.at[d],
                dst_ref=o_ref.at[d],
                send_sem=send_sem.at[d],
                recv_sem=recv_sem.at[d],
                device_id=where(d),
                device_id_type=pl.DeviceIdType.MESH,
            ).wait_recv()

        return carry

    lax.fori_loop(0, count, finish, 0)


def exchange(x, n_head, collective_id):
    count = x.shape[0]
    return pl.pallas_call(
        functools.partial(exchange_kernel, n_head),
        out_shape=jax.ShapeDtypeStruct(x.shape, x.dtype),
        in_specs=[pl.BlockSpec(memory_space=pltpu.VMEM)],
        out_specs=pl.BlockSpec(memory_space=pltpu.VMEM),
        scratch_shapes=[pltpu.SemaphoreType.DMA((count,)), pltpu.SemaphoreType.DMA((count,))],
        compiler_params=pltpu.CompilerParams(collective_id=collective_id, has_side_effects=True),
    )(x)


def per_device(
    queries, resp_keys, resp_values, prompt_keys, prompt_values, lengths, loss_mask, out_grad
):
    kv_width = resp_keys.shape[2]
    kv_count = kv_width // HEAD_DIM
    rows_here = prompt_keys.shape[0]
    groups = lax.axis_size("head")
    devices = lax.axis_size("resp") * groups
    both = jnp.concatenate(
        [prompt_keys.reshape(rows_here, groups, kv_width), prompt_values.reshape(rows_here, groups, kv_width)],
        2,
    ).transpose(1, 0, 2)
    outgoing = jnp.broadcast_to(both[None], (devices // groups,) + both.shape).reshape(
        devices, rows_here, 2 * kv_width
    )
    gathered = exchange(outgoing, groups, 0)
    prompt_kv = gathered.reshape(devices * rows_here, 2 * kv_width)

    steps = queries.shape[1]
    att, dq, dk, dv, prompt_parts = attend(
        lengths,
        queries.reshape(steps, -1),
        out_grad.reshape(steps, -1),
        prompt_kv,
        resp_keys.reshape(steps, kv_width),
        resp_values.reshape(steps, kv_width),
        loss_mask.reshape(steps, 1),
        kv_count,
    )
    arrived = exchange(
        prompt_parts.astype(jnp.bfloat16).reshape(devices, rows_here, 2 * kv_width), groups, 1
    )
    summed = arrived.astype(jnp.float32).reshape(devices // groups, groups, rows_here, 2 * kv_width).sum(0)
    summed = summed.transpose(1, 0, 2)
    prompt_key_grad = summed[:, :, :kv_width].reshape(rows_here, groups * kv_width)
    prompt_value_grad = summed[:, :, kv_width:].reshape(rows_here, groups * kv_width)
    return (
        att.reshape(queries.shape),
        dq.reshape(queries.shape),
        dk.reshape(resp_keys.shape),
        dv.reshape(resp_keys.shape),
        prompt_key_grad,
        prompt_value_grad,
    )


def solution(mesh):
    placed = (
        P("resp", None, "head"),
        P("resp", None, "head"),
        P("resp", None, "head"),
        P(("resp", "head"), None),
        P(("resp", "head"), None),
        P("resp"),
        P("resp", None),
        P("resp", None, "head"),
    )
    return jax.shard_map(
        per_device,
        mesh=mesh,
        in_specs=placed,
        out_specs=(
            P("resp", None, "head"),
            P("resp", None, "head"),
            P("resp", None, "head"),
            P("resp", None, "head"),
            P(("resp", "head"), None),
            P(("resp", "head"), None),
        ),
        check_vma=False,
    )
```

```python
import functools

import jax
import jax.numpy as jnp
from jax import lax
from jax.experimental import pallas as pl
from jax.experimental.pallas import tpu as pltpu
from jax.sharding import PartitionSpec as P

HEAD_DIM = 128
NT = (((1,), (1,)), ((), ()))
TN = (((0,), (0,)), ((), ()))


def attention_kernel(
    length_ref, q_ref, do_ref, kp_ref, vp_ref, ko_ref, vo_ref, keep_col_ref,
    att_ref, dq_ref, dko_ref, dvo_ref, pg_ref, dko_acc, dvo_acc,
):
    f32, bf16 = jnp.float32, jnp.bfloat16
    k = pl.program_id(0)
    g = pl.program_id(1)
    scale = HEAD_DIM ** (-0.5)
    length = length_ref[0]
    steps = q_ref.shape[0]
    q = q_ref[...]
    kp = kp_ref[...]
    ko = ko_ref[...]
    vp = vp_ref[...]
    vo = vo_ref[...]
    sp = lax.dot_general(kp, q, NT, preferred_element_type=f32) * scale
    so = lax.dot_general(ko, q, NT, preferred_element_type=f32) * scale
    j = lax.broadcasted_iota(jnp.int32, (steps, 1), 0)
    t = lax.broadcasted_iota(jnp.int32, (1, steps), 1)
    allowed = (j <= t) & (j < length)
    so = jnp.where(allowed, so, -jnp.inf)
    top = jnp.maximum(sp.max(0, keepdims=True), so.max(0, keepdims=True))
    ep = jnp.exp(sp - top)
    eo = jnp.exp(so - top)
    inverse = 1.0 / (ep.sum(0, keepdims=True) + eo.sum(0, keepdims=True))
    pp = ep * inverse
    po = eo * inverse
    wp = pp.astype(bf16)
    wo = po.astype(bf16)
    live = t < length
    out = lax.dot_general(vp, wp, TN, preferred_element_type=f32) + lax.dot_general(
        vo, wo, TN, preferred_element_type=f32
    )
    att = jnp.where(live, out, 0.0).astype(bf16).astype(f32)
    att_ref[...] = att.T.astype(bf16)
    live_col = lax.broadcasted_iota(jnp.int32, (steps, 1), 0) < length
    factor = (keep_col_ref[...] * live_col.astype(jnp.int32)).astype(bf16)
    do = do_ref[...] * factor
    delta = (do.astype(f32).T * att).sum(0, keepdims=True)
    dpp = lax.dot_general(vp, do, NT, preferred_element_type=f32)
    dpo = lax.dot_general(vo, do, NT, preferred_element_type=f32)
    dsp = (pp * (dpp - delta)).astype(bf16)
    dso = (po * (dpo - delta)).astype(bf16)
    dq = lax.dot_general(kp, dsp, TN, preferred_element_type=f32) + lax.dot_general(
        ko, dso, TN, preferred_element_type=f32
    )
    dq_ref[...] = (dq * scale).T.astype(bf16)
    dkp = jnp.dot(dsp, q, preferred_element_type=f32) * scale
    dvp = jnp.dot(wp, do, preferred_element_type=f32)
    dko = jnp.dot(dso, q, preferred_element_type=f32) * scale
    dvo = jnp.dot(wo, do, preferred_element_type=f32)
    width = HEAD_DIM
    kcol = pl.ds(pl.multiple_of(k * width, width), width)
    vcol = pl.ds(pl.multiple_of((k + pl.num_programs(0)) * width, width), width)

    @pl.when(g == 0)
    def _():
        dko_acc[...] = dko
        dvo_acc[...] = dvo
        pg_ref[:, kcol] = dkp
        pg_ref[:, vcol] = dvp

    @pl.when(g > 0)
    def _():
        dko_acc[...] += dko
        dvo_acc[...] += dvo
        pg_ref[:, kcol] += dkp
        pg_ref[:, vcol] += dvp

    @pl.when(g == pl.num_programs(1) - 1)
    def _():
        dko_ref[...] = dko_acc[...].astype(bf16)
        dvo_ref[...] = dvo_acc[...].astype(bf16)


def attend(length, queries, out_grad, prompt_kv, keys, values, keep, kv_count):
    steps, width = queries.shape
    group_size = width // (kv_count * HEAD_DIM)
    prompt_rows = prompt_kv.shape[0]
    head_block = lambda k, g, n: (0, k * group_size + g)
    kv_block = lambda k, g, n: (0, k)
    bf16, f32 = jnp.bfloat16, jnp.float32
    return pl.pallas_call(
        attention_kernel,
        out_shape=(
            jax.ShapeDtypeStruct((steps, width), bf16),
            jax.ShapeDtypeStruct((steps, width), bf16),
            jax.ShapeDtypeStruct(keys.shape, bf16),
            jax.ShapeDtypeStruct(keys.shape, bf16),
            jax.ShapeDtypeStruct((prompt_rows, 2 * kv_count * HEAD_DIM), f32),
        ),
        grid_spec=pltpu.PrefetchScalarGridSpec(
            num_scalar_prefetch=1,
            grid=(kv_count, group_size),
            in_specs=[
                pl.BlockSpec((steps, HEAD_DIM), head_block),
                pl.BlockSpec((steps, HEAD_DIM), head_block),
                pl.BlockSpec((prompt_rows, HEAD_DIM), kv_block),
                pl.BlockSpec((prompt_rows, HEAD_DIM), lambda k, g, n: (0, k + kv_count)),
                pl.BlockSpec((steps, HEAD_DIM), kv_block),
                pl.BlockSpec((steps, HEAD_DIM), kv_block),
                pl.BlockSpec((steps, 1), lambda k, g, n: (0, 0)),
            ],
            out_specs=[
                pl.BlockSpec((steps, HEAD_DIM), head_block),
                pl.BlockSpec((steps, HEAD_DIM), head_block),
                pl.BlockSpec((steps, HEAD_DIM), kv_block),
                pl.BlockSpec((steps, HEAD_DIM), kv_block),
                pl.BlockSpec((prompt_rows, 2 * kv_count * HEAD_DIM), lambda k, g, n: (0, 0)),
            ],
            scratch_shapes=[pltpu.VMEM((steps, HEAD_DIM), f32)] * 2,
        ),
        compiler_params=pltpu.CompilerParams(
            dimension_semantics=("arbitrary", "arbitrary"),
            vmem_limit_bytes=60 * 1024 * 1024,
        ),
    )(length, queries, out_grad, prompt_kv, prompt_kv, keys, values, keep)


def exchange_kernel(axis, same, x_ref, o_ref, send_sem, recv_sem):
    count = o_ref.shape[0]
    axes = ("resp", "head")
    me = lax.axis_index(axes[axis])
    here = tuple(lax.axis_index(a) for a in axes)
    barrier = pltpu.get_barrier_semaphore()

    def where(d):
        return here[:axis] + (d,) + here[axis + 1 :]

    def block(d):
        return x_ref if same else x_ref.at[d]

    def greet(d, carry):
        @pl.when(d != me)
        def _():
            pl.semaphore_signal(barrier, 1, device_id=where(d), device_id_type=pl.DeviceIdType.MESH)

        return carry

    lax.fori_loop(0, count, greet, 0)
    pl.semaphore_wait(barrier, count - 1)

    def send(d):
        return pltpu.make_async_remote_copy(
            src_ref=block(d),
            dst_ref=o_ref.at[me],
            send_sem=send_sem.at[d],
            recv_sem=recv_sem.at[me],
            device_id=where(d),
            device_id_type=pl.DeviceIdType.MESH,
        )

    def start(d, carry):
        @pl.when(d != me)
        def _():
            send(d).start()

        return carry

    lax.fori_loop(0, count, start, 0)
    o_ref[me] = block(me)[...]

    def finish(d, carry):
        @pl.when(d != me)
        def _():
            send(d).wait_send()
            pltpu.make_async_remote_copy(
                src_ref=block(d),
                dst_ref=o_ref.at[d],
                send_sem=send_sem.at[d],
                recv_sem=recv_sem.at[d],
                device_id=where(d),
                device_id_type=pl.DeviceIdType.MESH,
            ).wait_recv()

        return carry

    lax.fori_loop(0, count, finish, 0)


def exchange(x, axis, count, collective_id, same=False):
    shape = ((count,) + x.shape) if same else x.shape
    return pl.pallas_call(
        functools.partial(exchange_kernel, axis, same),
        out_shape=jax.ShapeDtypeStruct(shape, x.dtype),
        in_specs=[pl.BlockSpec(memory_space=pltpu.VMEM)],
        out_specs=pl.BlockSpec(memory_space=pltpu.VMEM),
        scratch_shapes=[pltpu.SemaphoreType.DMA((count,)), pltpu.SemaphoreType.DMA((count,))],
        compiler_params=pltpu.CompilerParams(collective_id=collective_id, has_side_effects=True),
    )(x)


def per_device(
    queries, resp_keys, resp_values, prompt_keys, prompt_values, lengths, loss_mask, out_grad
):
    kv_width = resp_keys.shape[2]
    kv_count = kv_width // HEAD_DIM
    rows_here = prompt_keys.shape[0]
    groups = lax.axis_size("head")
    devices = lax.axis_size("resp") * groups
    both = jnp.concatenate(
        [prompt_keys.reshape(rows_here, groups, kv_width), prompt_values.reshape(rows_here, groups, kv_width)],
        2,
    ).transpose(1, 0, 2)
    responses = devices // groups
    mine = exchange(both, 1, groups, 0)
    gathered = exchange(mine, 0, responses, 1, same=True)
    prompt_kv = gathered.reshape(devices * rows_here, 2 * kv_width)

    steps = queries.shape[1]
    att, dq, dk, dv, prompt_parts = attend(
        lengths,
        queries.reshape(steps, -1),
        out_grad.reshape(steps, -1),
        prompt_kv,
        resp_keys.reshape(steps, kv_width),
        resp_values.reshape(steps, kv_width),
        loss_mask.reshape(steps, 1),
        kv_count,
    )
    arrived = exchange(
        prompt_parts.astype(jnp.bfloat16).reshape(responses, groups * rows_here, 2 * kv_width), 0, responses, 2
    )
    partial = arrived.astype(jnp.float32).sum(0).astype(jnp.bfloat16)
    summed = exchange(partial.reshape(groups, rows_here, 2 * kv_width), 1, groups, 3).astype(jnp.float32)
    summed = summed.transpose(1, 0, 2)
    prompt_key_grad = summed[:, :, :kv_width].reshape(rows_here, groups * kv_width)
    prompt_value_grad = summed[:, :, kv_width:].reshape(rows_here, groups * kv_width)
    return (
        att.reshape(queries.shape),
        dq.reshape(queries.shape),
        dk.reshape(resp_keys.shape),
        dv.reshape(resp_keys.shape),
        prompt_key_grad,
        prompt_value_grad,
    )


def solution(mesh):
    placed = (
        P("resp", None, "head"),
        P("resp", None, "head"),
        P("resp", None, "head"),
        P(("resp", "head"), None),
        P(("resp", "head"), None),
        P("resp"),
        P("resp", None),
        P("resp", None, "head"),
    )
    return jax.shard_map(
        per_device,
        mesh=mesh,
        in_specs=placed,
        out_specs=(
            P("resp", None, "head"),
            P("resp", None, "head"),
            P("resp", None, "head"),
            P("resp", None, "head"),
            P(("resp", "head"), None),
            P(("resp", "head"), None),
        ),
        check_vma=False,
    )
```

```python
import functools

import jax
import jax.numpy as jnp
from jax import lax
from jax.experimental import pallas as pl
from jax.experimental.pallas import tpu as pltpu
from jax.sharding import PartitionSpec as P

HEAD_DIM = 128
NT = (((1,), (1,)), ((), ()))
TN = (((0,), (0,)), ((), ()))


def attention_kernel(
    n_head, length_ref, q_ref, do_ref, kp_ref, vp_ref, ko_ref, vo_ref, keep_col_ref,
    att_ref, dq_ref, dko_ref, dvo_ref, recv_ref, dko_acc, dvo_acc, pg_ref, sbuf, rbuf, ssem, rsem,
):
    f32, bf16 = jnp.float32, jnp.bfloat16
    k = pl.program_id(0)
    g = pl.program_id(1)
    scale = HEAD_DIM ** (-0.5)
    length = length_ref[0]
    steps = q_ref.shape[0]
    q = q_ref[...]
    kp = kp_ref[...]
    ko = ko_ref[...]
    vp = vp_ref[...]
    vo = vo_ref[...]
    sp = lax.dot_general(kp, q, NT, preferred_element_type=f32) * scale
    so = lax.dot_general(ko, q, NT, preferred_element_type=f32) * scale
    j = lax.broadcasted_iota(jnp.int32, (steps, 1), 0)
    t = lax.broadcasted_iota(jnp.int32, (1, steps), 1)
    allowed = (j <= t) & (j < length)
    so = jnp.where(allowed, so, -jnp.inf)
    top = jnp.maximum(sp.max(0, keepdims=True), so.max(0, keepdims=True))
    ep = jnp.exp(sp - top)
    eo = jnp.exp(so - top)
    inverse = 1.0 / (ep.sum(0, keepdims=True) + eo.sum(0, keepdims=True))
    pp = ep * inverse
    po = eo * inverse
    wp = pp.astype(bf16)
    wo = po.astype(bf16)
    live = t < length
    out = lax.dot_general(vp, wp, TN, preferred_element_type=f32) + lax.dot_general(
        vo, wo, TN, preferred_element_type=f32
    )
    att = jnp.where(live, out, 0.0).astype(bf16).astype(f32)
    att_ref[...] = att.T.astype(bf16)
    live_col = lax.broadcasted_iota(jnp.int32, (steps, 1), 0) < length
    factor = (keep_col_ref[...] * live_col.astype(jnp.int32)).astype(bf16)
    do = do_ref[...] * factor
    delta = (do.astype(f32).T * att).sum(0, keepdims=True)
    dpp = lax.dot_general(vp, do, NT, preferred_element_type=f32)
    dpo = lax.dot_general(vo, do, NT, preferred_element_type=f32)
    dsp = (pp * (dpp - delta)).astype(bf16)
    dso = (po * (dpo - delta)).astype(bf16)
    dq = lax.dot_general(kp, dsp, TN, preferred_element_type=f32) + lax.dot_general(
        ko, dso, TN, preferred_element_type=f32
    )
    dq_ref[...] = (dq * scale).T.astype(bf16)
    dkp = jnp.dot(dsp, q, preferred_element_type=f32) * scale
    dvp = jnp.dot(wp, do, preferred_element_type=f32)
    dko = jnp.dot(dso, q, preferred_element_type=f32) * scale
    dvo = jnp.dot(wo, do, preferred_element_type=f32)
    width = HEAD_DIM
    last_g = g == pl.num_programs(1) - 1
    count = sbuf.shape[1]
    me = lax.axis_index("resp") * n_head + lax.axis_index("head")

    def where(d):
        return (d // n_head, d % n_head)

    @pl.when((k == 0) & (g == 0))
    def _():
        barrier = pltpu.get_barrier_semaphore()

        def greet(d, carry):
            @pl.when(d != me)
            def _():
                pl.semaphore_signal(barrier, 1, device_id=where(d), device_id_type=pl.DeviceIdType.MESH)

            return carry

        lax.fori_loop(0, count, greet, 0)
        pl.semaphore_wait(barrier, count - 1)

    @pl.when(g == 0)
    def _():
        dko_acc[...] = dko
        dvo_acc[...] = dvo
        pg_ref[:, :width] = dkp
        pg_ref[:, width:] = dvp

    @pl.when(g > 0)
    def _():
        dko_acc[...] += dko
        dvo_acc[...] += dvo
        pg_ref[:, :width] += dkp
        pg_ref[:, width:] += dvp

    def send(kk, d):
        return pltpu.make_async_remote_copy(
            src_ref=sbuf.at[kk, d],
            dst_ref=rbuf.at[kk, me],
            send_sem=ssem.at[kk, d],
            recv_sem=rsem.at[kk, me],
            device_id=where(d),
            device_id_type=pl.DeviceIdType.MESH,
        )

    @pl.when(last_g)
    def _():
        dko_ref[...] = dko_acc[...].astype(bf16)
        dvo_ref[...] = dvo_acc[...].astype(bf16)
        rows = sbuf.shape[2]

        def stage(d, carry):
            sbuf[k, d] = pg_ref[pl.ds(pl.multiple_of(d * rows, rows), rows), :].astype(bf16)
            return carry

        lax.fori_loop(0, count, stage, 0)

        def start(d, carry):
            @pl.when(d != me)
            def _():
                send(k, d).start()

            return carry

        lax.fori_loop(0, count, start, 0)
        rbuf[k, me] = sbuf[k, me]

    @pl.when(last_g & (k == pl.num_programs(0) - 1))
    def _():
        for kk in range(sbuf.shape[0]):

            def finish(d, carry):
                @pl.when(d != me)
                def _():
                    send(kk, d).wait_send()
                    pltpu.make_async_remote_copy(
                        src_ref=sbuf.at[kk, d],
                        dst_ref=rbuf.at[kk, d],
                        send_sem=ssem.at[kk, d],
                        recv_sem=rsem.at[kk, d],
                        device_id=where(d),
                        device_id_type=pl.DeviceIdType.MESH,
                    ).wait_recv()

                return carry

            lax.fori_loop(0, count, finish, 0)
        recv_ref[...] = rbuf[...]


def attend(length, queries, out_grad, prompt_kv, keys, values, keep, kv_count, n_head, devices):
    steps, width = queries.shape
    group_size = width // (kv_count * HEAD_DIM)
    prompt_rows = prompt_kv.shape[0]
    head_block = lambda k, g, n: (0, k * group_size + g)
    kv_block = lambda k, g, n: (0, k)
    bf16, f32 = jnp.bfloat16, jnp.float32
    return pl.pallas_call(
        functools.partial(attention_kernel, n_head),
        out_shape=(
            jax.ShapeDtypeStruct((steps, width), bf16),
            jax.ShapeDtypeStruct((steps, width), bf16),
            jax.ShapeDtypeStruct(keys.shape, bf16),
            jax.ShapeDtypeStruct(keys.shape, bf16),
            jax.ShapeDtypeStruct((kv_count, devices, prompt_rows // devices, 2 * HEAD_DIM), bf16),
        ),
        grid_spec=pltpu.PrefetchScalarGridSpec(
            num_scalar_prefetch=1,
            grid=(kv_count, group_size),
            in_specs=[
                pl.BlockSpec((steps, HEAD_DIM), head_block),
                pl.BlockSpec((steps, HEAD_DIM), head_block),
                pl.BlockSpec((prompt_rows, HEAD_DIM), kv_block),
                pl.BlockSpec((prompt_rows, HEAD_DIM), lambda k, g, n: (0, k + kv_count)),
                pl.BlockSpec((steps, HEAD_DIM), kv_block),
                pl.BlockSpec((steps, HEAD_DIM), kv_block),
                pl.BlockSpec((steps, 1), lambda k, g, n: (0, 0)),
            ],
            out_specs=[
                pl.BlockSpec((steps, HEAD_DIM), head_block),
                pl.BlockSpec((steps, HEAD_DIM), head_block),
                pl.BlockSpec((steps, HEAD_DIM), kv_block),
                pl.BlockSpec((steps, HEAD_DIM), kv_block),
                pl.BlockSpec(
                    (kv_count, devices, prompt_rows // devices, 2 * HEAD_DIM), lambda k, g, n: (0, 0, 0, 0)
                ),
            ],
            scratch_shapes=[pltpu.VMEM((steps, HEAD_DIM), f32)] * 2
            + [pltpu.VMEM((prompt_rows, 2 * HEAD_DIM), f32)]
            + [pltpu.VMEM((kv_count, devices, prompt_rows // devices, 2 * HEAD_DIM), bf16)] * 2
            + [pltpu.SemaphoreType.DMA((kv_count, devices))] * 2,
        ),
        compiler_params=pltpu.CompilerParams(
            dimension_semantics=("arbitrary", "arbitrary"),
            vmem_limit_bytes=60 * 1024 * 1024,
            collective_id=0,
            has_side_effects=True,
        ),
    )(length, queries, out_grad, prompt_kv, prompt_kv, keys, values, keep)


def per_device(
    queries, resp_keys, resp_values, prompt_keys, prompt_values, lengths, loss_mask, out_grad
):
    kv_width = resp_keys.shape[2]
    kv_count = kv_width // HEAD_DIM
    rows_here = prompt_keys.shape[0]
    groups = lax.axis_size("head")
    devices = lax.axis_size("resp") * groups
    both = jnp.concatenate(
        [prompt_keys.reshape(rows_here, groups, kv_width), prompt_values.reshape(rows_here, groups, kv_width)],
        2,
    ).transpose(1, 0, 2)
    outgoing = jnp.broadcast_to(both[None], (devices // groups,) + both.shape).reshape(
        devices, rows_here, 2 * kv_width
    )
    gathered = lax.all_to_all(outgoing, ("resp", "head"), split_axis=0, concat_axis=0, tiled=True)
    prompt_kv = gathered.reshape(devices * rows_here, 2 * kv_width)

    steps = queries.shape[1]
    att, dq, dk, dv, arrived = attend(
        lengths,
        queries.reshape(steps, -1),
        out_grad.reshape(steps, -1),
        prompt_kv,
        resp_keys.reshape(steps, kv_width),
        resp_values.reshape(steps, kv_width),
        loss_mask.reshape(steps, 1),
        kv_count,
        groups,
        devices,
    )
    summed = arrived.astype(jnp.float32).reshape(kv_count, devices // groups, groups, rows_here, 2, HEAD_DIM)
    summed = summed.sum(1).transpose(3, 2, 1, 0, 4)
    prompt_key_grad = summed[0].reshape(rows_here, groups * kv_width)
    prompt_value_grad = summed[1].reshape(rows_here, groups * kv_width)
    return (
        att.reshape(queries.shape),
        dq.reshape(queries.shape),
        dk.reshape(resp_keys.shape),
        dv.reshape(resp_keys.shape),
        prompt_key_grad,
        prompt_value_grad,
    )


def solution(mesh):
    placed = (
        P("resp", None, "head"),
        P("resp", None, "head"),
        P("resp", None, "head"),
        P(("resp", "head"), None),
        P(("resp", "head"), None),
        P("resp"),
        P("resp", None),
        P("resp", None, "head"),
    )
    return jax.shard_map(
        per_device,
        mesh=mesh,
        in_specs=placed,
        out_specs=(
            P("resp", None, "head"),
            P("resp", None, "head"),
            P("resp", None, "head"),
            P("resp", None, "head"),
            P(("resp", "head"), None),
            P(("resp", "head"), None),
        ),
        check_vma=False,
    )
```

```python
import functools

import jax
import jax.numpy as jnp
from jax import lax
from jax.experimental import pallas as pl
from jax.experimental.pallas import tpu as pltpu
from jax.sharding import PartitionSpec as P

HEAD_DIM = 128
NT = (((1,), (1,)), ((), ()))
TN = (((0,), (0,)), ((), ()))


def attention_kernel(
    length_ref, q_ref, do_ref, kp_ref, vp_ref, ko_ref, vo_ref, keep_col_ref,
    att_ref, dq_ref, dko_ref, dvo_ref, pg_ref, dko_acc, dvo_acc,
):
    f32, bf16 = jnp.float32, jnp.bfloat16
    k = pl.program_id(0)
    g = pl.program_id(1)
    part = pl.program_id(2)
    parts = pl.num_programs(2)
    scale = HEAD_DIM ** (-0.5)
    length = length_ref[0]
    rows = q_ref.shape[0]
    width = HEAD_DIM
    kcol = pl.ds(pl.multiple_of(k * width, width), width)
    vcol = pl.ds(pl.multiple_of((k + pl.num_programs(0)) * width, width), width)

    @pl.when((g == 0) & (part == 0))
    def _():
        dko_acc[...] = jnp.zeros_like(dko_acc)
        dvo_acc[...] = jnp.zeros_like(dvo_acc)
        pg_ref[:, kcol] = jnp.zeros((pg_ref.shape[0], width), f32)
        pg_ref[:, vcol] = jnp.zeros((pg_ref.shape[0], width), f32)

    def compute(first):
        own = first + rows
        q = q_ref[...]
        kp = kp_ref[...]
        ko = ko_ref[:own, :]
        vp = vp_ref[...]
        vo = vo_ref[:own, :]
        sp = lax.dot_general(kp, q, NT, preferred_element_type=f32) * scale
        so = lax.dot_general(ko, q, NT, preferred_element_type=f32) * scale
        j = lax.broadcasted_iota(jnp.int32, (own, 1), 0)
        t = first + lax.broadcasted_iota(jnp.int32, (1, rows), 1)
        allowed = (j <= t) & (j < length)
        so = jnp.where(allowed, so, -jnp.inf)
        top = jnp.maximum(sp.max(0, keepdims=True), so.max(0, keepdims=True))
        ep = jnp.exp(sp - top)
        eo = jnp.exp(so - top)
        inverse = 1.0 / (ep.sum(0, keepdims=True) + eo.sum(0, keepdims=True))
        pp = ep * inverse
        po = eo * inverse
        wp = pp.astype(bf16)
        wo = po.astype(bf16)
        live = t < length
        out = lax.dot_general(vp, wp, TN, preferred_element_type=f32) + lax.dot_general(
            vo, wo, TN, preferred_element_type=f32
        )
        att = jnp.where(live, out, 0.0).astype(bf16).astype(f32)
        att_ref[...] = att.T.astype(bf16)
        live_col = first + lax.broadcasted_iota(jnp.int32, (rows, 1), 0) < length
        factor = (keep_col_ref[...] * live_col.astype(jnp.int32)).astype(bf16)
        do = do_ref[...] * factor
        delta = (do.astype(f32).T * att).sum(0, keepdims=True)
        dpp = lax.dot_general(vp, do, NT, preferred_element_type=f32)
        dpo = lax.dot_general(vo, do, NT, preferred_element_type=f32)
        dsp = (pp * (dpp - delta)).astype(bf16)
        dso = (po * (dpo - delta)).astype(bf16)
        dq = lax.dot_general(kp, dsp, TN, preferred_element_type=f32) + lax.dot_general(
            ko, dso, TN, preferred_element_type=f32
        )
        dq_ref[...] = (dq * scale).T.astype(bf16)
        pg_ref[:, kcol] += jnp.dot(dsp, q, preferred_element_type=f32) * scale
        pg_ref[:, vcol] += jnp.dot(wp, do, preferred_element_type=f32)
        dko_acc[:own, :] += jnp.dot(dso, q, preferred_element_type=f32) * scale
        dvo_acc[:own, :] += jnp.dot(wo, do, preferred_element_type=f32)

    for index in range(ko_ref.shape[0] // rows):

        @pl.when(part == index)
        def _():
            compute(index * rows)

    @pl.when((g == pl.num_programs(1) - 1) & (part == parts - 1))
    def _():
        dko_ref[...] = dko_acc[...].astype(bf16)
        dvo_ref[...] = dvo_acc[...].astype(bf16)


def attend(length, queries, out_grad, prompt_kv, keys, values, keep, kv_count):
    steps, width = queries.shape
    group_size = width // (kv_count * HEAD_DIM)
    prompt_rows = prompt_kv.shape[0]
    parts = 2
    rows = steps // parts
    head_block = lambda k, g, i, n: (i, k * group_size + g)
    kv_block = lambda k, g, i, n: (0, k)
    bf16, f32 = jnp.bfloat16, jnp.float32
    return pl.pallas_call(
        attention_kernel,
        out_shape=(
            jax.ShapeDtypeStruct((steps, width), bf16),
            jax.ShapeDtypeStruct((steps, width), bf16),
            jax.ShapeDtypeStruct(keys.shape, bf16),
            jax.ShapeDtypeStruct(keys.shape, bf16),
            jax.ShapeDtypeStruct((prompt_rows, 2 * kv_count * HEAD_DIM), f32),
        ),
        grid_spec=pltpu.PrefetchScalarGridSpec(
            num_scalar_prefetch=1,
            grid=(kv_count, group_size, parts),
            in_specs=[
                pl.BlockSpec((rows, HEAD_DIM), head_block),
                pl.BlockSpec((rows, HEAD_DIM), head_block),
                pl.BlockSpec((prompt_rows, HEAD_DIM), kv_block),
                pl.BlockSpec((prompt_rows, HEAD_DIM), lambda k, g, i, n: (0, k + kv_count)),
                pl.BlockSpec((steps, HEAD_DIM), kv_block),
                pl.BlockSpec((steps, HEAD_DIM), kv_block),
                pl.BlockSpec((rows, 1), lambda k, g, i, n: (i, 0)),
            ],
            out_specs=[
                pl.BlockSpec((rows, HEAD_DIM), head_block),
                pl.BlockSpec((rows, HEAD_DIM), head_block),
                pl.BlockSpec((steps, HEAD_DIM), kv_block),
                pl.BlockSpec((steps, HEAD_DIM), kv_block),
                pl.BlockSpec((prompt_rows, 2 * kv_count * HEAD_DIM), lambda k, g, i, n: (0, 0)),
            ],
            scratch_shapes=[pltpu.VMEM((steps, HEAD_DIM), f32)] * 2,
        ),
        compiler_params=pltpu.CompilerParams(
            dimension_semantics=("arbitrary", "arbitrary", "arbitrary"),
            vmem_limit_bytes=60 * 1024 * 1024,
        ),
    )(length, queries, out_grad, prompt_kv, prompt_kv, keys, values, keep)


def per_device(
    queries, resp_keys, resp_values, prompt_keys, prompt_values, lengths, loss_mask, out_grad
):
    kv_width = resp_keys.shape[2]
    kv_count = kv_width // HEAD_DIM
    rows_here = prompt_keys.shape[0]
    groups = lax.axis_size("head")
    devices = lax.axis_size("resp") * groups
    both = jnp.concatenate(
        [prompt_keys.reshape(rows_here, groups, kv_width), prompt_values.reshape(rows_here, groups, kv_width)],
        2,
    ).transpose(1, 0, 2)
    outgoing = jnp.broadcast_to(both[None], (devices // groups,) + both.shape).reshape(
        devices, rows_here, 2 * kv_width
    )
    gathered = lax.all_to_all(outgoing, ("resp", "head"), split_axis=0, concat_axis=0, tiled=True)
    prompt_kv = gathered.reshape(devices * rows_here, 2 * kv_width)

    steps = queries.shape[1]
    att, dq, dk, dv, prompt_parts = attend(
        lengths,
        queries.reshape(steps, -1),
        out_grad.reshape(steps, -1),
        prompt_kv,
        resp_keys.reshape(steps, kv_width),
        resp_values.reshape(steps, kv_width),
        loss_mask.reshape(steps, 1),
        kv_count,
    )
    arrived = lax.all_to_all(
        prompt_parts.astype(jnp.bfloat16).reshape(devices, rows_here, 2 * kv_width),
        ("resp", "head"),
        split_axis=0,
        concat_axis=0,
        tiled=True,
    )
    summed = arrived.astype(jnp.float32).reshape(devices // groups, groups, rows_here, 2 * kv_width).sum(0)
    summed = summed.transpose(1, 0, 2)
    prompt_key_grad = summed[:, :, :kv_width].reshape(rows_here, groups * kv_width)
    prompt_value_grad = summed[:, :, kv_width:].reshape(rows_here, groups * kv_width)
    return (
        att.reshape(queries.shape),
        dq.reshape(queries.shape),
        dk.reshape(resp_keys.shape),
        dv.reshape(resp_keys.shape),
        prompt_key_grad,
        prompt_value_grad,
    )


def solution(mesh):
    placed = (
        P("resp", None, "head"),
        P("resp", None, "head"),
        P("resp", None, "head"),
        P(("resp", "head"), None),
        P(("resp", "head"), None),
        P("resp"),
        P("resp", None),
        P("resp", None, "head"),
    )
    return jax.shard_map(
        per_device,
        mesh=mesh,
        in_specs=placed,
        out_specs=(
            P("resp", None, "head"),
            P("resp", None, "head"),
            P("resp", None, "head"),
            P("resp", None, "head"),
            P(("resp", "head"), None),
            P(("resp", "head"), None),
        ),
        check_vma=False,
    )
```

```python
import functools

import jax
import jax.numpy as jnp
from jax import lax
from jax.experimental import pallas as pl
from jax.experimental.pallas import tpu as pltpu
from jax.sharding import PartitionSpec as P

HEAD_DIM = 128
NT = (((1,), (1,)), ((), ()))
TN = (((0,), (0,)), ((), ()))


def attention_kernel(
    length_ref, q_ref, qt_ref, do_ref, dot_ref, kp_ref, kpt_ref, vp_ref, vpt_ref,
    ko_ref, kot_ref, vo_ref, vot_ref, keep_col_ref, keep_row_ref,
    att_ref, dq_ref, dko_ref, dvo_ref, pg_ref, dko_acc, dvo_acc,
):
    f32, bf16 = jnp.float32, jnp.bfloat16
    k = pl.program_id(0)
    g = pl.program_id(1)
    scale = HEAD_DIM ** (-0.5)
    length = length_ref[0]
    steps = q_ref.shape[0]
    q = q_ref[...]
    qt = qt_ref[...]
    kp = kp_ref[...]
    ko = ko_ref[...]
    vp = vp_ref[...]
    vo = vo_ref[...]
    sp = jnp.dot(kp, qt, preferred_element_type=f32) * scale
    so = jnp.dot(ko, qt, preferred_element_type=f32) * scale
    j = lax.broadcasted_iota(jnp.int32, (steps, 1), 0)
    t = lax.broadcasted_iota(jnp.int32, (1, steps), 1)
    allowed = (j <= t) & (j < length)
    so = jnp.where(allowed, so, -jnp.inf)
    top = jnp.maximum(sp.max(0, keepdims=True), so.max(0, keepdims=True))
    ep = jnp.exp(sp - top)
    eo = jnp.exp(so - top)
    inverse = 1.0 / (ep.sum(0, keepdims=True) + eo.sum(0, keepdims=True))
    pp = ep * inverse
    po = eo * inverse
    wp = pp.astype(bf16)
    wo = po.astype(bf16)
    live = t < length
    out = jnp.dot(vpt_ref[...], wp, preferred_element_type=f32) + jnp.dot(
        vot_ref[...], wo, preferred_element_type=f32
    )
    att = jnp.where(live, out, 0.0).astype(bf16).astype(f32)
    att_ref[...] = att.T.astype(bf16)
    live_col = lax.broadcasted_iota(jnp.int32, (steps, 1), 0) < length
    do = do_ref[...] * (keep_col_ref[...] * live_col.astype(jnp.int32)).astype(bf16)
    dot = dot_ref[...] * (keep_row_ref[...] * live.astype(jnp.int32)).astype(bf16)
    delta = (dot.astype(f32) * att).sum(0, keepdims=True)
    dpp = jnp.dot(vp, dot, preferred_element_type=f32)
    dpo = jnp.dot(vo, dot, preferred_element_type=f32)
    dsp = (pp * (dpp - delta)).astype(bf16)
    dso = (po * (dpo - delta)).astype(bf16)
    dq = jnp.dot(kpt_ref[...], dsp, preferred_element_type=f32) + jnp.dot(
        kot_ref[...], dso, preferred_element_type=f32
    )
    dq_ref[...] = (dq * scale).T.astype(bf16)
    dkp = jnp.dot(dsp, q, preferred_element_type=f32) * scale
    dvp = jnp.dot(wp, do, preferred_element_type=f32)
    dko = jnp.dot(dso, q, preferred_element_type=f32) * scale
    dvo = jnp.dot(wo, do, preferred_element_type=f32)
    width = HEAD_DIM
    kcol = pl.ds(pl.multiple_of(k * width, width), width)
    vcol = pl.ds(pl.multiple_of((k + pl.num_programs(0)) * width, width), width)

    @pl.when(g == 0)
    def _():
        dko_acc[...] = dko
        dvo_acc[...] = dvo
        pg_ref[:, kcol] = dkp
        pg_ref[:, vcol] = dvp

    @pl.when(g > 0)
    def _():
        dko_acc[...] += dko
        dvo_acc[...] += dvo
        pg_ref[:, kcol] += dkp
        pg_ref[:, vcol] += dvp

    @pl.when(g == pl.num_programs(1) - 1)
    def _():
        dko_ref[...] = dko_acc[...].astype(bf16)
        dvo_ref[...] = dvo_acc[...].astype(bf16)


def attend(length, queries, out_grad, prompt_kv, keys, values, keep, kv_count):
    steps, width = queries.shape
    group_size = width // (kv_count * HEAD_DIM)
    prompt_rows = prompt_kv.shape[0]
    head_block = lambda k, g, n: (0, k * group_size + g)
    kv_block = lambda k, g, n: (0, k)
    bf16, f32 = jnp.bfloat16, jnp.float32
    return pl.pallas_call(
        attention_kernel,
        out_shape=(
            jax.ShapeDtypeStruct((steps, width), bf16),
            jax.ShapeDtypeStruct((steps, width), bf16),
            jax.ShapeDtypeStruct(keys.shape, bf16),
            jax.ShapeDtypeStruct(keys.shape, bf16),
            jax.ShapeDtypeStruct((prompt_rows, 2 * kv_count * HEAD_DIM), f32),
        ),
        grid_spec=pltpu.PrefetchScalarGridSpec(
            num_scalar_prefetch=1,
            grid=(kv_count, group_size),
            in_specs=[
                pl.BlockSpec((steps, HEAD_DIM), head_block),
                pl.BlockSpec((HEAD_DIM, steps), lambda k, g, n: (k * group_size + g, 0)),
                pl.BlockSpec((steps, HEAD_DIM), head_block),
                pl.BlockSpec((HEAD_DIM, steps), lambda k, g, n: (k * group_size + g, 0)),
                pl.BlockSpec((prompt_rows, HEAD_DIM), kv_block),
                pl.BlockSpec((HEAD_DIM, prompt_rows), lambda k, g, n: (k, 0)),
                pl.BlockSpec((prompt_rows, HEAD_DIM), lambda k, g, n: (0, k + kv_count)),
                pl.BlockSpec((HEAD_DIM, prompt_rows), lambda k, g, n: (k + kv_count, 0)),
                pl.BlockSpec((steps, HEAD_DIM), kv_block),
                pl.BlockSpec((HEAD_DIM, steps), lambda k, g, n: (k, 0)),
                pl.BlockSpec((steps, HEAD_DIM), kv_block),
                pl.BlockSpec((HEAD_DIM, steps), lambda k, g, n: (k, 0)),
                pl.BlockSpec((steps, 1), lambda k, g, n: (0, 0)),
                pl.BlockSpec((1, steps), lambda k, g, n: (0, 0)),
            ],
            out_specs=[
                pl.BlockSpec((steps, HEAD_DIM), head_block),
                pl.BlockSpec((steps, HEAD_DIM), head_block),
                pl.BlockSpec((steps, HEAD_DIM), kv_block),
                pl.BlockSpec((steps, HEAD_DIM), kv_block),
                pl.BlockSpec((prompt_rows, 2 * kv_count * HEAD_DIM), lambda k, g, n: (0, 0)),
            ],
            scratch_shapes=[pltpu.VMEM((steps, HEAD_DIM), f32)] * 2,
        ),
        compiler_params=pltpu.CompilerParams(
            dimension_semantics=("arbitrary", "arbitrary"),
            vmem_limit_bytes=60 * 1024 * 1024,
        ),
    )(
        length,
        queries,
        queries.T,
        out_grad,
        out_grad.T,
        prompt_kv,
        prompt_kv.T,
        prompt_kv,
        prompt_kv.T,
        keys,
        keys.T,
        values,
        values.T,
        keep,
        keep.reshape(1, steps),
    )


def per_device(
    queries, resp_keys, resp_values, prompt_keys, prompt_values, lengths, loss_mask, out_grad
):
    kv_width = resp_keys.shape[2]
    kv_count = kv_width // HEAD_DIM
    rows_here = prompt_keys.shape[0]
    groups = lax.axis_size("head")
    devices = lax.axis_size("resp") * groups
    both = jnp.concatenate(
        [prompt_keys.reshape(rows_here, groups, kv_width), prompt_values.reshape(rows_here, groups, kv_width)],
        2,
    ).transpose(1, 0, 2)
    outgoing = jnp.broadcast_to(both[None], (devices // groups,) + both.shape).reshape(
        devices, rows_here, 2 * kv_width
    )
    gathered = lax.all_to_all(outgoing, ("resp", "head"), split_axis=0, concat_axis=0, tiled=True)
    prompt_kv = gathered.reshape(devices * rows_here, 2 * kv_width)

    steps = queries.shape[1]
    att, dq, dk, dv, prompt_parts = attend(
        lengths,
        queries.reshape(steps, -1),
        out_grad.reshape(steps, -1),
        prompt_kv,
        resp_keys.reshape(steps, kv_width),
        resp_values.reshape(steps, kv_width),
        loss_mask.reshape(steps, 1),
        kv_count,
    )
    arrived = lax.all_to_all(
        prompt_parts.astype(jnp.bfloat16).reshape(devices, rows_here, 2 * kv_width),
        ("resp", "head"),
        split_axis=0,
        concat_axis=0,
        tiled=True,
    )
    summed = arrived.astype(jnp.float32).reshape(devices // groups, groups, rows_here, 2 * kv_width).sum(0)
    summed = summed.transpose(1, 0, 2)
    prompt_key_grad = summed[:, :, :kv_width].reshape(rows_here, groups * kv_width)
    prompt_value_grad = summed[:, :, kv_width:].reshape(rows_here, groups * kv_width)
    return (
        att.reshape(queries.shape),
        dq.reshape(queries.shape),
        dk.reshape(resp_keys.shape),
        dv.reshape(resp_keys.shape),
        prompt_key_grad,
        prompt_value_grad,
    )


def solution(mesh):
    placed = (
        P("resp", None, "head"),
        P("resp", None, "head"),
        P("resp", None, "head"),
        P(("resp", "head"), None),
        P(("resp", "head"), None),
        P("resp"),
        P("resp", None),
        P("resp", None, "head"),
    )
    return jax.shard_map(
        per_device,
        mesh=mesh,
        in_specs=placed,
        out_specs=(
            P("resp", None, "head"),
            P("resp", None, "head"),
            P("resp", None, "head"),
            P("resp", None, "head"),
            P(("resp", "head"), None),
            P(("resp", "head"), None),
        ),
        check_vma=False,
    )
```

```python
import functools

import jax
import jax.numpy as jnp
from jax import lax
from jax.experimental import pallas as pl
from jax.experimental.pallas import tpu as pltpu
from jax.sharding import PartitionSpec as P

HEAD_DIM = 128
NT = (((1,), (1,)), ((), ()))
TN = (((0,), (0,)), ((), ()))


def attention_kernel(
    length_ref, q_ref, qt_ref, do_ref, dot_ref, kp_ref, kpt_ref, vp_ref, vpt_ref,
    ko_ref, kot_ref, vo_ref, vot_ref, keep_col_ref, keep_row_ref,
    att_ref, dq_ref, dko_ref, dvo_ref, pg_out, dko_acc, dvo_acc, pg_ref,
):
    f32, bf16 = jnp.float32, jnp.bfloat16
    k = pl.program_id(0)
    g = pl.program_id(1)
    scale = HEAD_DIM ** (-0.5)
    length = length_ref[0]
    steps = q_ref.shape[0]
    q = q_ref[...]
    qt = qt_ref[...]
    kp = kp_ref[...]
    ko = ko_ref[...]
    vp = vp_ref[...]
    vo = vo_ref[...]
    sp = jnp.dot(kp, qt, preferred_element_type=f32) * scale
    so = jnp.dot(ko, qt, preferred_element_type=f32) * scale
    j = lax.broadcasted_iota(jnp.int32, (steps, 1), 0)
    t = lax.broadcasted_iota(jnp.int32, (1, steps), 1)
    allowed = (j <= t) & (j < length)
    so = jnp.where(allowed, so, -jnp.inf)
    top = jnp.maximum(sp.max(0, keepdims=True), so.max(0, keepdims=True))
    ep = jnp.exp(sp - top)
    eo = jnp.exp(so - top)
    inverse = 1.0 / (ep.sum(0, keepdims=True) + eo.sum(0, keepdims=True))
    pp = ep * inverse
    po = eo * inverse
    wp = pp.astype(bf16)
    wo = po.astype(bf16)
    live = t < length
    out = jnp.dot(vpt_ref[...], wp, preferred_element_type=f32) + jnp.dot(
        vot_ref[...], wo, preferred_element_type=f32
    )
    att = jnp.where(live, out, 0.0).astype(bf16).astype(f32)
    att_ref[...] = att.T.astype(bf16)
    live_col = lax.broadcasted_iota(jnp.int32, (steps, 1), 0) < length
    do = do_ref[...] * (keep_col_ref[...] * live_col.astype(jnp.int32)).astype(bf16)
    dot = dot_ref[...] * (keep_row_ref[...] * live.astype(jnp.int32)).astype(bf16)
    delta = (dot.astype(f32) * att).sum(0, keepdims=True)
    dpp = jnp.dot(vp, dot, preferred_element_type=f32)
    dpo = jnp.dot(vo, dot, preferred_element_type=f32)
    dsp = (pp * (dpp - delta)).astype(bf16)
    dso = (po * (dpo - delta)).astype(bf16)
    dq = jnp.dot(kpt_ref[...], dsp, preferred_element_type=f32) + jnp.dot(
        kot_ref[...], dso, preferred_element_type=f32
    )
    dq_ref[...] = (dq * scale).T.astype(bf16)
    dkp = jnp.dot(dsp, q, preferred_element_type=f32) * scale
    dvp = jnp.dot(wp, do, preferred_element_type=f32)
    dko = jnp.dot(dso, q, preferred_element_type=f32) * scale
    dvo = jnp.dot(wo, do, preferred_element_type=f32)
    width = HEAD_DIM
    kcol = pl.ds(pl.multiple_of(k * width, width), width)
    vcol = pl.ds(pl.multiple_of((k + pl.num_programs(0)) * width, width), width)

    @pl.when(g == 0)
    def _():
        dko_acc[...] = dko
        dvo_acc[...] = dvo
        pg_ref[:, kcol] = dkp
        pg_ref[:, vcol] = dvp

    @pl.when(g > 0)
    def _():
        dko_acc[...] += dko
        dvo_acc[...] += dvo
        pg_ref[:, kcol] += dkp
        pg_ref[:, vcol] += dvp

    @pl.when(g == pl.num_programs(1) - 1)
    def _():
        dko_ref[...] = dko_acc[...].astype(bf16)
        dvo_ref[...] = dvo_acc[...].astype(bf16)
        pg_out[:, kcol] = pg_ref[:, kcol].astype(bf16)
        pg_out[:, vcol] = pg_ref[:, vcol].astype(bf16)


def attend(length, queries, out_grad, prompt_kv, keys, values, keep, kv_count):
    steps, width = queries.shape
    group_size = width // (kv_count * HEAD_DIM)
    prompt_rows = prompt_kv.shape[0]
    head_block = lambda k, g, n: (0, k * group_size + g)
    kv_block = lambda k, g, n: (0, k)
    bf16, f32 = jnp.bfloat16, jnp.float32
    return pl.pallas_call(
        attention_kernel,
        out_shape=(
            jax.ShapeDtypeStruct((steps, width), bf16),
            jax.ShapeDtypeStruct((steps, width), bf16),
            jax.ShapeDtypeStruct(keys.shape, bf16),
            jax.ShapeDtypeStruct(keys.shape, bf16),
            jax.ShapeDtypeStruct((prompt_rows, 2 * kv_count * HEAD_DIM), bf16),
        ),
        grid_spec=pltpu.PrefetchScalarGridSpec(
            num_scalar_prefetch=1,
            grid=(kv_count, group_size),
            in_specs=[
                pl.BlockSpec((steps, HEAD_DIM), head_block),
                pl.BlockSpec((HEAD_DIM, steps), lambda k, g, n: (k * group_size + g, 0)),
                pl.BlockSpec((steps, HEAD_DIM), head_block),
                pl.BlockSpec((HEAD_DIM, steps), lambda k, g, n: (k * group_size + g, 0)),
                pl.BlockSpec((prompt_rows, HEAD_DIM), kv_block),
                pl.BlockSpec((HEAD_DIM, prompt_rows), lambda k, g, n: (k, 0)),
                pl.BlockSpec((prompt_rows, HEAD_DIM), lambda k, g, n: (0, k + kv_count)),
                pl.BlockSpec((HEAD_DIM, prompt_rows), lambda k, g, n: (k + kv_count, 0)),
                pl.BlockSpec((steps, HEAD_DIM), kv_block),
                pl.BlockSpec((HEAD_DIM, steps), lambda k, g, n: (k, 0)),
                pl.BlockSpec((steps, HEAD_DIM), kv_block),
                pl.BlockSpec((HEAD_DIM, steps), lambda k, g, n: (k, 0)),
                pl.BlockSpec((steps, 1), lambda k, g, n: (0, 0)),
                pl.BlockSpec((1, steps), lambda k, g, n: (0, 0)),
            ],
            out_specs=[
                pl.BlockSpec((steps, HEAD_DIM), head_block),
                pl.BlockSpec((steps, HEAD_DIM), head_block),
                pl.BlockSpec((steps, HEAD_DIM), kv_block),
                pl.BlockSpec((steps, HEAD_DIM), kv_block),
                pl.BlockSpec((prompt_rows, 2 * kv_count * HEAD_DIM), lambda k, g, n: (0, 0)),
            ],
            scratch_shapes=[pltpu.VMEM((steps, HEAD_DIM), f32)] * 2
            + [pltpu.VMEM((prompt_rows, 2 * kv_count * HEAD_DIM), f32)],
        ),
        compiler_params=pltpu.CompilerParams(
            dimension_semantics=("arbitrary", "arbitrary"),
            vmem_limit_bytes=60 * 1024 * 1024,
        ),
    )(
        length,
        queries,
        queries.T,
        out_grad,
        out_grad.T,
        prompt_kv,
        prompt_kv.T,
        prompt_kv,
        prompt_kv.T,
        keys,
        keys.T,
        values,
        values.T,
        keep,
        keep.reshape(1, steps),
    )


def per_device(
    queries, resp_keys, resp_values, prompt_keys, prompt_values, lengths, loss_mask, out_grad
):
    kv_width = resp_keys.shape[2]
    kv_count = kv_width // HEAD_DIM
    rows_here = prompt_keys.shape[0]
    groups = lax.axis_size("head")
    devices = lax.axis_size("resp") * groups
    both = jnp.concatenate(
        [prompt_keys.reshape(rows_here, groups, kv_width), prompt_values.reshape(rows_here, groups, kv_width)],
        2,
    ).transpose(1, 0, 2)
    outgoing = jnp.broadcast_to(both[None], (devices // groups,) + both.shape).reshape(
        devices, rows_here, 2 * kv_width
    )
    gathered = lax.all_to_all(outgoing, ("resp", "head"), split_axis=0, concat_axis=0, tiled=True)
    prompt_kv = gathered.reshape(devices * rows_here, 2 * kv_width)

    steps = queries.shape[1]
    att, dq, dk, dv, prompt_parts = attend(
        lengths,
        queries.reshape(steps, -1),
        out_grad.reshape(steps, -1),
        prompt_kv,
        resp_keys.reshape(steps, kv_width),
        resp_values.reshape(steps, kv_width),
        loss_mask.reshape(steps, 1),
        kv_count,
    )
    arrived = lax.all_to_all(
        prompt_parts.reshape(devices, rows_here, 2 * kv_width),
        ("resp", "head"),
        split_axis=0,
        concat_axis=0,
        tiled=True,
    )
    summed = arrived.astype(jnp.float32).reshape(devices // groups, groups, rows_here, 2 * kv_width).sum(0)
    summed = summed.transpose(1, 0, 2)
    prompt_key_grad = summed[:, :, :kv_width].reshape(rows_here, groups * kv_width)
    prompt_value_grad = summed[:, :, kv_width:].reshape(rows_here, groups * kv_width)
    return (
        att.reshape(queries.shape),
        dq.reshape(queries.shape),
        dk.reshape(resp_keys.shape),
        dv.reshape(resp_keys.shape),
        prompt_key_grad,
        prompt_value_grad,
    )


def solution(mesh):
    placed = (
        P("resp", None, "head"),
        P("resp", None, "head"),
        P("resp", None, "head"),
        P(("resp", "head"), None),
        P(("resp", "head"), None),
        P("resp"),
        P("resp", None),
        P("resp", None, "head"),
    )
    return jax.shard_map(
        per_device,
        mesh=mesh,
        in_specs=placed,
        out_specs=(
            P("resp", None, "head"),
            P("resp", None, "head"),
            P("resp", None, "head"),
            P("resp", None, "head"),
            P(("resp", "head"), None),
            P(("resp", "head"), None),
        ),
        check_vma=False,
    )
```

```python
import functools

import jax
import jax.numpy as jnp
from jax import lax
from jax.experimental import pallas as pl
from jax.experimental.pallas import tpu as pltpu
from jax.sharding import PartitionSpec as P

HEAD_DIM = 128
NT = (((1,), (1,)), ((), ()))
TN = (((0,), (0,)), ((), ()))


def attention_kernel(
    length_ref, q_ref, qt_ref, do_ref, dot_ref, kp_ref, kpt_ref, vp_ref, vpt_ref,
    ko_ref, kot_ref, vo_ref, vot_ref, keep_col_ref, keep_row_ref,
    att_ref, dq_ref, dko_ref, dvo_ref, pg_out, dko_acc, dvo_acc, pg_ref,
):
    f32, bf16 = jnp.float32, jnp.bfloat16
    scale = HEAD_DIM ** (-0.5)
    length = length_ref[0]
    steps = q_ref.shape[0]
    width = HEAD_DIM
    group_size = q_ref.shape[1] // width
    j = lax.broadcasted_iota(jnp.int32, (steps, 1), 0)
    t = lax.broadcasted_iota(jnp.int32, (1, steps), 1)
    allowed = (j <= t) & (j < length)
    live = t < length
    live_col = j < length
    factor_col = (keep_col_ref[...] * live_col.astype(jnp.int32)).astype(bf16)
    factor_row = (keep_row_ref[...] * live.astype(jnp.int32)).astype(bf16)
    dko_acc[...] = jnp.zeros_like(dko_acc)
    dvo_acc[...] = jnp.zeros_like(dvo_acc)
    pg_ref[...] = jnp.zeros_like(pg_ref)

    def head(h, carry):
        cols = pl.ds(pl.multiple_of(h * width, width), width)
        q = q_ref[:, cols]
        qt = qt_ref[cols, :]
        kp = kp_ref[...]
        ko = ko_ref[...]
        vp = vp_ref[...]
        vo = vo_ref[...]
        sp = jnp.dot(kp, qt, preferred_element_type=f32) * scale
        so = jnp.dot(ko, qt, preferred_element_type=f32) * scale
        so = jnp.where(allowed, so, -jnp.inf)
        top = jnp.maximum(sp.max(0, keepdims=True), so.max(0, keepdims=True))
        ep = jnp.exp(sp - top)
        eo = jnp.exp(so - top)
        inverse = 1.0 / (ep.sum(0, keepdims=True) + eo.sum(0, keepdims=True))
        pp = ep * inverse
        po = eo * inverse
        wp = pp.astype(bf16)
        wo = po.astype(bf16)
        out = jnp.dot(vpt_ref[...], wp, preferred_element_type=f32) + jnp.dot(
            vot_ref[...], wo, preferred_element_type=f32
        )
        att = jnp.where(live, out, 0.0).astype(bf16).astype(f32)
        att_ref[:, cols] = att.T.astype(bf16)
        do = do_ref[:, cols] * factor_col
        dot = dot_ref[cols, :] * factor_row
        delta = (dot.astype(f32) * att).sum(0, keepdims=True)
        dpp = jnp.dot(vp, dot, preferred_element_type=f32)
        dpo = jnp.dot(vo, dot, preferred_element_type=f32)
        dsp = (pp * (dpp - delta)).astype(bf16)
        dso = (po * (dpo - delta)).astype(bf16)
        dq = jnp.dot(kpt_ref[...], dsp, preferred_element_type=f32) + jnp.dot(
            kot_ref[...], dso, preferred_element_type=f32
        )
        dq_ref[:, cols] = (dq * scale).T.astype(bf16)
        pg_ref[:, :width] += jnp.dot(dsp, q, preferred_element_type=f32) * scale
        pg_ref[:, width:] += jnp.dot(wp, do, preferred_element_type=f32)
        dko_acc[...] += jnp.dot(dso, q, preferred_element_type=f32) * scale
        dvo_acc[...] += jnp.dot(wo, do, preferred_element_type=f32)
        return carry

    lax.fori_loop(0, group_size, head, 0)
    dko_ref[...] = dko_acc[...].astype(bf16)
    dvo_ref[...] = dvo_acc[...].astype(bf16)
    pg_out[:, :width] = pg_ref[:, :width].astype(bf16)
    pg_out[:, width:] = pg_ref[:, width:].astype(bf16)


def attend(length, queries, out_grad, prompt_kv, keys, values, keep, kv_count):
    steps, width = queries.shape
    group_size = width // (kv_count * HEAD_DIM)
    prompt_rows = prompt_kv.shape[0]
    heads = group_size * HEAD_DIM
    kv_block = lambda k, n: (0, k)
    kv_block_t = lambda k, n: (k, 0)
    bf16, f32 = jnp.bfloat16, jnp.float32
    return pl.pallas_call(
        attention_kernel,
        out_shape=(
            jax.ShapeDtypeStruct((steps, width), bf16),
            jax.ShapeDtypeStruct((steps, width), bf16),
            jax.ShapeDtypeStruct(keys.shape, bf16),
            jax.ShapeDtypeStruct(keys.shape, bf16),
            jax.ShapeDtypeStruct((prompt_rows, 2 * kv_count * HEAD_DIM), bf16),
        ),
        grid_spec=pltpu.PrefetchScalarGridSpec(
            num_scalar_prefetch=1,
            grid=(kv_count,),
            in_specs=[
                pl.BlockSpec((steps, heads), kv_block),
                pl.BlockSpec((heads, steps), kv_block_t),
                pl.BlockSpec((steps, heads), kv_block),
                pl.BlockSpec((heads, steps), kv_block_t),
                pl.BlockSpec((prompt_rows, HEAD_DIM), kv_block),
                pl.BlockSpec((HEAD_DIM, prompt_rows), kv_block_t),
                pl.BlockSpec((prompt_rows, HEAD_DIM), lambda k, n: (0, k + kv_count)),
                pl.BlockSpec((HEAD_DIM, prompt_rows), lambda k, n: (k + kv_count, 0)),
                pl.BlockSpec((steps, HEAD_DIM), kv_block),
                pl.BlockSpec((HEAD_DIM, steps), kv_block_t),
                pl.BlockSpec((steps, HEAD_DIM), kv_block),
                pl.BlockSpec((HEAD_DIM, steps), kv_block_t),
                pl.BlockSpec((steps, 1), lambda k, n: (0, 0)),
                pl.BlockSpec((1, steps), lambda k, n: (0, 0)),
            ],
            out_specs=[
                pl.BlockSpec((steps, heads), kv_block),
                pl.BlockSpec((steps, heads), kv_block),
                pl.BlockSpec((steps, HEAD_DIM), kv_block),
                pl.BlockSpec((steps, HEAD_DIM), kv_block),
                pl.BlockSpec((prompt_rows, 2 * HEAD_DIM), kv_block),
            ],
            scratch_shapes=[pltpu.VMEM((steps, HEAD_DIM), f32)] * 2
            + [pltpu.VMEM((prompt_rows, 2 * HEAD_DIM), f32)],
        ),
        compiler_params=pltpu.CompilerParams(
            dimension_semantics=("arbitrary",),
            vmem_limit_bytes=60 * 1024 * 1024,
        ),
    )(
        length,
        queries,
        queries.T,
        out_grad,
        out_grad.T,
        prompt_kv,
        prompt_kv.T,
        prompt_kv,
        prompt_kv.T,
        keys,
        keys.T,
        values,
        values.T,
        keep,
        keep.reshape(1, steps),
    )


def per_device(
    queries, resp_keys, resp_values, prompt_keys, prompt_values, lengths, loss_mask, out_grad
):
    kv_width = resp_keys.shape[2]
    kv_count = kv_width // HEAD_DIM
    rows_here = prompt_keys.shape[0]
    groups = lax.axis_size("head")
    devices = lax.axis_size("resp") * groups
    both = jnp.concatenate(
        [prompt_keys.reshape(rows_here, groups, kv_width), prompt_values.reshape(rows_here, groups, kv_width)],
        2,
    ).transpose(1, 0, 2)
    outgoing = jnp.broadcast_to(both[None], (devices // groups,) + both.shape).reshape(
        devices, rows_here, 2 * kv_width
    )
    gathered = lax.all_to_all(outgoing, ("resp", "head"), split_axis=0, concat_axis=0, tiled=True)
    prompt_kv = gathered.reshape(devices * rows_here, 2 * kv_width)

    steps = queries.shape[1]
    att, dq, dk, dv, prompt_parts = attend(
        lengths,
        queries.reshape(steps, -1),
        out_grad.reshape(steps, -1),
        prompt_kv,
        resp_keys.reshape(steps, kv_width),
        resp_values.reshape(steps, kv_width),
        loss_mask.reshape(steps, 1),
        kv_count,
    )
    arrived = lax.all_to_all(
        prompt_parts.reshape(devices, rows_here, 2 * kv_width),
        ("resp", "head"),
        split_axis=0,
        concat_axis=0,
        tiled=True,
    )
    summed = arrived.astype(jnp.float32).reshape(devices // groups, groups, rows_here, 2 * kv_width).sum(0)
    summed = summed.reshape(groups, rows_here, kv_count, 2, HEAD_DIM).transpose(3, 1, 0, 2, 4)
    prompt_key_grad = summed[0].reshape(rows_here, groups * kv_width)
    prompt_value_grad = summed[1].reshape(rows_here, groups * kv_width)
    return (
        att.reshape(queries.shape),
        dq.reshape(queries.shape),
        dk.reshape(resp_keys.shape),
        dv.reshape(resp_keys.shape),
        prompt_key_grad,
        prompt_value_grad,
    )


def solution(mesh):
    placed = (
        P("resp", None, "head"),
        P("resp", None, "head"),
        P("resp", None, "head"),
        P(("resp", "head"), None),
        P(("resp", "head"), None),
        P("resp"),
        P("resp", None),
        P("resp", None, "head"),
    )
    return jax.shard_map(
        per_device,
        mesh=mesh,
        in_specs=placed,
        out_specs=(
            P("resp", None, "head"),
            P("resp", None, "head"),
            P("resp", None, "head"),
            P("resp", None, "head"),
            P(("resp", "head"), None),
            P(("resp", "head"), None),
        ),
        check_vma=False,
    )
```

```python
import functools

import jax
import jax.numpy as jnp
from jax import lax
from jax.experimental import pallas as pl
from jax.experimental.pallas import tpu as pltpu
from jax.sharding import PartitionSpec as P

HEAD_DIM = 128
NT = (((1,), (1,)), ((), ()))
TN = (((0,), (0,)), ((), ()))


def attention_kernel(
    length_ref, q_ref, qt_ref, do_ref, dot_ref, kp_ref, kpt_ref, vp_ref, vpt_ref,
    ko_ref, kot_ref, vo_ref, vot_ref, keep_col_ref, keep_row_ref,
    att_ref, dq_ref, dko_ref, dvo_ref, pg_out, dko_acc, dvo_acc, pg_ref,
):
    f32, bf16 = jnp.float32, jnp.bfloat16
    scale = HEAD_DIM ** (-0.5)
    length = length_ref[0]
    steps = q_ref.shape[0]
    width = HEAD_DIM
    group_size = q_ref.shape[1] // width
    j = lax.broadcasted_iota(jnp.int32, (steps, 1), 0)
    t = lax.broadcasted_iota(jnp.int32, (1, steps), 1)
    half = steps // 2
    allowed1 = (j[:half] <= t[:, :half]) & (j[:half] < length)
    allowed2 = (j <= t[:, half:]) & (j < length)
    live = t < length
    live_col = j < length
    factor_col = (keep_col_ref[...] * live_col.astype(jnp.int32)).astype(bf16)
    factor_row = (keep_row_ref[...] * live.astype(jnp.int32)).astype(bf16)
    dko_acc[...] = jnp.zeros_like(dko_acc)
    dvo_acc[...] = jnp.zeros_like(dvo_acc)
    pg_ref[...] = jnp.zeros_like(pg_ref)

    def head(h, carry):
        cols = pl.ds(pl.multiple_of(h * width, width), width)
        q = q_ref[:, cols]
        qt = qt_ref[cols, :]
        kp = kp_ref[...]
        ko = ko_ref[...]
        vp = vp_ref[...]
        vo = vo_ref[...]
        sp = jnp.dot(kp, qt, preferred_element_type=f32) * scale
        so1 = jnp.dot(ko[:half], qt[:, :half], preferred_element_type=f32) * scale
        so2 = jnp.dot(ko, qt[:, half:], preferred_element_type=f32) * scale
        so1 = jnp.where(allowed1, so1, -jnp.inf)
        so2 = jnp.where(allowed2, so2, -jnp.inf)
        top = jnp.maximum(
            sp.max(0, keepdims=True),
            jnp.concatenate([so1.max(0, keepdims=True), so2.max(0, keepdims=True)], 1),
        )
        ep = jnp.exp(sp - top)
        eo1 = jnp.exp(so1 - top[:, :half])
        eo2 = jnp.exp(so2 - top[:, half:])
        inverse = 1.0 / (
            ep.sum(0, keepdims=True)
            + jnp.concatenate([eo1.sum(0, keepdims=True), eo2.sum(0, keepdims=True)], 1)
        )
        pp = ep * inverse
        po1 = eo1 * inverse[:, :half]
        po2 = eo2 * inverse[:, half:]
        wp = pp.astype(bf16)
        wo1 = po1.astype(bf16)
        wo2 = po2.astype(bf16)
        vot = vot_ref[...]
        kot = kot_ref[...]
        out = jnp.dot(vpt_ref[...], wp, preferred_element_type=f32) + jnp.concatenate(
            [
                jnp.dot(vot[:, :half], wo1, preferred_element_type=f32),
                jnp.dot(vot, wo2, preferred_element_type=f32),
            ],
            1,
        )
        att = jnp.where(live, out, 0.0).astype(bf16).astype(f32)
        att_ref[:, cols] = att.T.astype(bf16)
        do = do_ref[:, cols] * factor_col
        dot = dot_ref[cols, :] * factor_row
        delta = (dot.astype(f32) * att).sum(0, keepdims=True)
        dpp = jnp.dot(vp, dot, preferred_element_type=f32)
        dpo1 = jnp.dot(vo[:half], dot[:, :half], preferred_element_type=f32)
        dpo2 = jnp.dot(vo, dot[:, half:], preferred_element_type=f32)
        dsp = (pp * (dpp - delta)).astype(bf16)
        dso1 = (po1 * (dpo1 - delta[:, :half])).astype(bf16)
        dso2 = (po2 * (dpo2 - delta[:, half:])).astype(bf16)
        dq = jnp.dot(kpt_ref[...], dsp, preferred_element_type=f32) + jnp.concatenate(
            [
                jnp.dot(kot[:, :half], dso1, preferred_element_type=f32),
                jnp.dot(kot, dso2, preferred_element_type=f32),
            ],
            1,
        )
        dq_ref[:, cols] = (dq * scale).T.astype(bf16)
        pg_ref[:, :width] += jnp.dot(dsp, q, preferred_element_type=f32) * scale
        pg_ref[:, width:] += jnp.dot(wp, do, preferred_element_type=f32)
        dko_acc[:half, :] += jnp.dot(dso1, q[:half], preferred_element_type=f32) * scale
        dko_acc[...] += jnp.dot(dso2, q[half:], preferred_element_type=f32) * scale
        dvo_acc[:half, :] += jnp.dot(wo1, do[:half], preferred_element_type=f32)
        dvo_acc[...] += jnp.dot(wo2, do[half:], preferred_element_type=f32)
        return carry

    lax.fori_loop(0, group_size, head, 0)
    dko_ref[...] = dko_acc[...].astype(bf16)
    dvo_ref[...] = dvo_acc[...].astype(bf16)
    pg_out[:, :width] = pg_ref[:, :width].astype(bf16)
    pg_out[:, width:] = pg_ref[:, width:].astype(bf16)


def attend(length, queries, out_grad, prompt_kv, keys, values, keep, kv_count):
    steps, width = queries.shape
    group_size = width // (kv_count * HEAD_DIM)
    prompt_rows = prompt_kv.shape[0]
    heads = group_size * HEAD_DIM
    kv_block = lambda k, n: (0, k)
    kv_block_t = lambda k, n: (k, 0)
    bf16, f32 = jnp.bfloat16, jnp.float32
    return pl.pallas_call(
        attention_kernel,
        out_shape=(
            jax.ShapeDtypeStruct((steps, width), bf16),
            jax.ShapeDtypeStruct((steps, width), bf16),
            jax.ShapeDtypeStruct(keys.shape, bf16),
            jax.ShapeDtypeStruct(keys.shape, bf16),
            jax.ShapeDtypeStruct((prompt_rows, 2 * kv_count * HEAD_DIM), bf16),
        ),
        grid_spec=pltpu.PrefetchScalarGridSpec(
            num_scalar_prefetch=1,
            grid=(kv_count,),
            in_specs=[
                pl.BlockSpec((steps, heads), kv_block),
                pl.BlockSpec((heads, steps), kv_block_t),
                pl.BlockSpec((steps, heads), kv_block),
                pl.BlockSpec((heads, steps), kv_block_t),
                pl.BlockSpec((prompt_rows, HEAD_DIM), kv_block),
                pl.BlockSpec((HEAD_DIM, prompt_rows), kv_block_t),
                pl.BlockSpec((prompt_rows, HEAD_DIM), lambda k, n: (0, k + kv_count)),
                pl.BlockSpec((HEAD_DIM, prompt_rows), lambda k, n: (k + kv_count, 0)),
                pl.BlockSpec((steps, HEAD_DIM), kv_block),
                pl.BlockSpec((HEAD_DIM, steps), kv_block_t),
                pl.BlockSpec((steps, HEAD_DIM), kv_block),
                pl.BlockSpec((HEAD_DIM, steps), kv_block_t),
                pl.BlockSpec((steps, 1), lambda k, n: (0, 0)),
                pl.BlockSpec((1, steps), lambda k, n: (0, 0)),
            ],
            out_specs=[
                pl.BlockSpec((steps, heads), kv_block),
                pl.BlockSpec((steps, heads), kv_block),
                pl.BlockSpec((steps, HEAD_DIM), kv_block),
                pl.BlockSpec((steps, HEAD_DIM), kv_block),
                pl.BlockSpec((prompt_rows, 2 * HEAD_DIM), kv_block),
            ],
            scratch_shapes=[pltpu.VMEM((steps, HEAD_DIM), f32)] * 2
            + [pltpu.VMEM((prompt_rows, 2 * HEAD_DIM), f32)],
        ),
        compiler_params=pltpu.CompilerParams(
            dimension_semantics=("arbitrary",),
            vmem_limit_bytes=60 * 1024 * 1024,
        ),
    )(
        length,
        queries,
        queries.T,
        out_grad,
        out_grad.T,
        prompt_kv,
        prompt_kv.T,
        prompt_kv,
        prompt_kv.T,
        keys,
        keys.T,
        values,
        values.T,
        keep,
        keep.reshape(1, steps),
    )


def per_device(
    queries, resp_keys, resp_values, prompt_keys, prompt_values, lengths, loss_mask, out_grad
):
    kv_width = resp_keys.shape[2]
    kv_count = kv_width // HEAD_DIM
    rows_here = prompt_keys.shape[0]
    groups = lax.axis_size("head")
    devices = lax.axis_size("resp") * groups
    both = jnp.concatenate(
        [prompt_keys.reshape(rows_here, groups, kv_width), prompt_values.reshape(rows_here, groups, kv_width)],
        2,
    ).transpose(1, 0, 2)
    outgoing = jnp.broadcast_to(both[None], (devices // groups,) + both.shape).reshape(
        devices, rows_here, 2 * kv_width
    )
    gathered = lax.all_to_all(outgoing, ("resp", "head"), split_axis=0, concat_axis=0, tiled=True)
    prompt_kv = gathered.reshape(devices * rows_here, 2 * kv_width)

    steps = queries.shape[1]
    att, dq, dk, dv, prompt_parts = attend(
        lengths,
        queries.reshape(steps, -1),
        out_grad.reshape(steps, -1),
        prompt_kv,
        resp_keys.reshape(steps, kv_width),
        resp_values.reshape(steps, kv_width),
        loss_mask.reshape(steps, 1),
        kv_count,
    )
    arrived = lax.all_to_all(
        prompt_parts.reshape(devices, rows_here, 2 * kv_width),
        ("resp", "head"),
        split_axis=0,
        concat_axis=0,
        tiled=True,
    )
    summed = arrived.astype(jnp.float32).reshape(devices // groups, groups, rows_here, 2 * kv_width).sum(0)
    summed = summed.reshape(groups, rows_here, kv_count, 2, HEAD_DIM).transpose(3, 1, 0, 2, 4)
    prompt_key_grad = summed[0].reshape(rows_here, groups * kv_width)
    prompt_value_grad = summed[1].reshape(rows_here, groups * kv_width)
    return (
        att.reshape(queries.shape),
        dq.reshape(queries.shape),
        dk.reshape(resp_keys.shape),
        dv.reshape(resp_keys.shape),
        prompt_key_grad,
        prompt_value_grad,
    )


def solution(mesh):
    placed = (
        P("resp", None, "head"),
        P("resp", None, "head"),
        P("resp", None, "head"),
        P(("resp", "head"), None),
        P(("resp", "head"), None),
        P("resp"),
        P("resp", None),
        P("resp", None, "head"),
    )
    return jax.shard_map(
        per_device,
        mesh=mesh,
        in_specs=placed,
        out_specs=(
            P("resp", None, "head"),
            P("resp", None, "head"),
            P("resp", None, "head"),
            P("resp", None, "head"),
            P(("resp", "head"), None),
            P(("resp", "head"), None),
        ),
        check_vma=False,
    )
```

```python
import functools

import jax
import jax.numpy as jnp
from jax import lax
from jax.experimental import pallas as pl
from jax.experimental.pallas import tpu as pltpu
from jax.sharding import PartitionSpec as P

HEAD_DIM = 128
NT = (((1,), (1,)), ((), ()))
TN = (((0,), (0,)), ((), ()))


def attention_kernel(
    length_ref, q_ref, qt_ref, do_ref, dot_ref, kp_ref, vp_ref,
    ko_ref, kot_ref, vo_ref, vot_ref, keep_col_ref, keep_row_ref,
    att_ref, dq_ref, dko_ref, dvo_ref, pg_out, dko_acc, dvo_acc, pg_ref, kpt_ref, vpt_ref,
):
    f32, bf16 = jnp.float32, jnp.bfloat16
    scale = HEAD_DIM ** (-0.5)
    length = length_ref[0]
    steps = q_ref.shape[0]
    width = HEAD_DIM
    group_size = q_ref.shape[1] // width
    j = lax.broadcasted_iota(jnp.int32, (steps, 1), 0)
    t = lax.broadcasted_iota(jnp.int32, (1, steps), 1)
    half = steps // 2
    allowed1 = (j[:half] <= t[:, :half]) & (j[:half] < length)
    allowed2 = (j <= t[:, half:]) & (j < length)
    live = t < length
    live_col = j < length
    factor_col = (keep_col_ref[...] * live_col.astype(jnp.int32)).astype(bf16)
    factor_row = (keep_row_ref[...] * live.astype(jnp.int32)).astype(bf16)
    kpt_ref[...] = kp_ref[...].astype(f32).T.astype(bf16)
    vpt_ref[...] = vp_ref[...].astype(f32).T.astype(bf16)
    dko_acc[...] = jnp.zeros_like(dko_acc)
    dvo_acc[...] = jnp.zeros_like(dvo_acc)
    pg_ref[...] = jnp.zeros_like(pg_ref)

    def head(h, carry):
        cols = pl.ds(pl.multiple_of(h * width, width), width)
        q = q_ref[:, cols]
        qt = qt_ref[cols, :]
        kp = kp_ref[...]
        ko = ko_ref[...]
        vp = vp_ref[...]
        vo = vo_ref[...]
        sp = jnp.dot(kp, qt, preferred_element_type=f32) * scale
        so1 = jnp.dot(ko[:half], qt[:, :half], preferred_element_type=f32) * scale
        so2 = jnp.dot(ko, qt[:, half:], preferred_element_type=f32) * scale
        so1 = jnp.where(allowed1, so1, -jnp.inf)
        so2 = jnp.where(allowed2, so2, -jnp.inf)
        top = jnp.maximum(
            sp.max(0, keepdims=True),
            jnp.concatenate([so1.max(0, keepdims=True), so2.max(0, keepdims=True)], 1),
        )
        ep = jnp.exp(sp - top)
        eo1 = jnp.exp(so1 - top[:, :half])
        eo2 = jnp.exp(so2 - top[:, half:])
        inverse = 1.0 / (
            ep.sum(0, keepdims=True)
            + jnp.concatenate([eo1.sum(0, keepdims=True), eo2.sum(0, keepdims=True)], 1)
        )
        pp = ep * inverse
        po1 = eo1 * inverse[:, :half]
        po2 = eo2 * inverse[:, half:]
        wp = pp.astype(bf16)
        wo1 = po1.astype(bf16)
        wo2 = po2.astype(bf16)
        vot = vot_ref[...]
        kot = kot_ref[...]
        out = jnp.dot(vpt_ref[...], wp, preferred_element_type=f32) + jnp.concatenate(
            [
                jnp.dot(vot[:, :half], wo1, preferred_element_type=f32),
                jnp.dot(vot, wo2, preferred_element_type=f32),
            ],
            1,
        )
        att = jnp.where(live, out, 0.0).astype(bf16).astype(f32)
        att_ref[:, cols] = att.T.astype(bf16)
        do = do_ref[:, cols] * factor_col
        dot = dot_ref[cols, :] * factor_row
        delta = (dot.astype(f32) * att).sum(0, keepdims=True)
        dpp = jnp.dot(vp, dot, preferred_element_type=f32)
        dpo1 = jnp.dot(vo[:half], dot[:, :half], preferred_element_type=f32)
        dpo2 = jnp.dot(vo, dot[:, half:], preferred_element_type=f32)
        dsp = (pp * (dpp - delta)).astype(bf16)
        dso1 = (po1 * (dpo1 - delta[:, :half])).astype(bf16)
        dso2 = (po2 * (dpo2 - delta[:, half:])).astype(bf16)
        dq = jnp.dot(kpt_ref[...], dsp, preferred_element_type=f32) + jnp.concatenate(
            [
                jnp.dot(kot[:, :half], dso1, preferred_element_type=f32),
                jnp.dot(kot, dso2, preferred_element_type=f32),
            ],
            1,
        )
        dq_ref[:, cols] = (dq * scale).T.astype(bf16)
        pg_ref[:, :width] += jnp.dot(dsp, q, preferred_element_type=f32) * scale
        pg_ref[:, width:] += jnp.dot(wp, do, preferred_element_type=f32)
        dko_acc[:half, :] += jnp.dot(dso1, q[:half], preferred_element_type=f32) * scale
        dko_acc[...] += jnp.dot(dso2, q[half:], preferred_element_type=f32) * scale
        dvo_acc[:half, :] += jnp.dot(wo1, do[:half], preferred_element_type=f32)
        dvo_acc[...] += jnp.dot(wo2, do[half:], preferred_element_type=f32)
        return carry

    lax.fori_loop(0, group_size, head, 0)
    dko_ref[...] = dko_acc[...].astype(bf16)
    dvo_ref[...] = dvo_acc[...].astype(bf16)
    pg_out[:, :width] = pg_ref[:, :width].astype(bf16)
    pg_out[:, width:] = pg_ref[:, width:].astype(bf16)


def attend(length, queries, out_grad, prompt_kv, keys, values, keep, kv_count):
    steps, width = queries.shape
    group_size = width // (kv_count * HEAD_DIM)
    prompt_rows = prompt_kv.shape[0]
    heads = group_size * HEAD_DIM
    kv_block = lambda k, n: (0, k)
    kv_block_t = lambda k, n: (k, 0)
    bf16, f32 = jnp.bfloat16, jnp.float32
    return pl.pallas_call(
        attention_kernel,
        out_shape=(
            jax.ShapeDtypeStruct((steps, width), bf16),
            jax.ShapeDtypeStruct((steps, width), bf16),
            jax.ShapeDtypeStruct(keys.shape, bf16),
            jax.ShapeDtypeStruct(keys.shape, bf16),
            jax.ShapeDtypeStruct((prompt_rows, 2 * kv_count * HEAD_DIM), bf16),
        ),
        grid_spec=pltpu.PrefetchScalarGridSpec(
            num_scalar_prefetch=1,
            grid=(kv_count,),
            in_specs=[
                pl.BlockSpec((steps, heads), kv_block),
                pl.BlockSpec((heads, steps), kv_block_t),
                pl.BlockSpec((steps, heads), kv_block),
                pl.BlockSpec((heads, steps), kv_block_t),
                pl.BlockSpec((prompt_rows, HEAD_DIM), kv_block),
                pl.BlockSpec((prompt_rows, HEAD_DIM), lambda k, n: (0, k + kv_count)),
                pl.BlockSpec((steps, HEAD_DIM), kv_block),
                pl.BlockSpec((HEAD_DIM, steps), kv_block_t),
                pl.BlockSpec((steps, HEAD_DIM), kv_block),
                pl.BlockSpec((HEAD_DIM, steps), kv_block_t),
                pl.BlockSpec((steps, 1), lambda k, n: (0, 0)),
                pl.BlockSpec((1, steps), lambda k, n: (0, 0)),
            ],
            out_specs=[
                pl.BlockSpec((steps, heads), kv_block),
                pl.BlockSpec((steps, heads), kv_block),
                pl.BlockSpec((steps, HEAD_DIM), kv_block),
                pl.BlockSpec((steps, HEAD_DIM), kv_block),
                pl.BlockSpec((prompt_rows, 2 * HEAD_DIM), kv_block),
            ],
            scratch_shapes=[pltpu.VMEM((steps, HEAD_DIM), f32)] * 2
            + [pltpu.VMEM((prompt_rows, 2 * HEAD_DIM), f32)]
            + [pltpu.VMEM((HEAD_DIM, prompt_rows), bf16)] * 2,
        ),
        compiler_params=pltpu.CompilerParams(
            dimension_semantics=("arbitrary",),
            vmem_limit_bytes=60 * 1024 * 1024,
        ),
    )(
        length,
        queries,
        queries.T,
        out_grad,
        out_grad.T,
        prompt_kv,
        prompt_kv,
        keys,
        keys.T,
        values,
        values.T,
        keep,
        keep.reshape(1, steps),
    )


def per_device(
    queries, resp_keys, resp_values, prompt_keys, prompt_values, lengths, loss_mask, out_grad
):
    kv_width = resp_keys.shape[2]
    kv_count = kv_width // HEAD_DIM
    rows_here = prompt_keys.shape[0]
    groups = lax.axis_size("head")
    devices = lax.axis_size("resp") * groups
    both = jnp.concatenate(
        [prompt_keys.reshape(rows_here, groups, kv_width), prompt_values.reshape(rows_here, groups, kv_width)],
        2,
    ).transpose(1, 0, 2)
    outgoing = jnp.broadcast_to(both[None], (devices // groups,) + both.shape).reshape(
        devices, rows_here, 2 * kv_width
    )
    gathered = lax.all_to_all(outgoing, ("resp", "head"), split_axis=0, concat_axis=0, tiled=True)
    prompt_kv = gathered.reshape(devices * rows_here, 2 * kv_width)

    steps = queries.shape[1]
    att, dq, dk, dv, prompt_parts = attend(
        lengths,
        queries.reshape(steps, -1),
        out_grad.reshape(steps, -1),
        prompt_kv,
        resp_keys.reshape(steps, kv_width),
        resp_values.reshape(steps, kv_width),
        loss_mask.reshape(steps, 1),
        kv_count,
    )
    arrived = lax.all_to_all(
        prompt_parts.reshape(devices, rows_here, 2 * kv_width),
        ("resp", "head"),
        split_axis=0,
        concat_axis=0,
        tiled=True,
    )
    summed = arrived.astype(jnp.float32).reshape(devices // groups, groups, rows_here, 2 * kv_width).sum(0)
    summed = summed.reshape(groups, rows_here, kv_count, 2, HEAD_DIM).transpose(3, 1, 0, 2, 4)
    prompt_key_grad = summed[0].reshape(rows_here, groups * kv_width)
    prompt_value_grad = summed[1].reshape(rows_here, groups * kv_width)
    return (
        att.reshape(queries.shape),
        dq.reshape(queries.shape),
        dk.reshape(resp_keys.shape),
        dv.reshape(resp_keys.shape),
        prompt_key_grad,
        prompt_value_grad,
    )


def solution(mesh):
    placed = (
        P("resp", None, "head"),
        P("resp", None, "head"),
        P("resp", None, "head"),
        P(("resp", "head"), None),
        P(("resp", "head"), None),
        P("resp"),
        P("resp", None),
        P("resp", None, "head"),
    )
    return jax.shard_map(
        per_device,
        mesh=mesh,
        in_specs=placed,
        out_specs=(
            P("resp", None, "head"),
            P("resp", None, "head"),
            P("resp", None, "head"),
            P("resp", None, "head"),
            P(("resp", "head"), None),
            P(("resp", "head"), None),
        ),
        check_vma=False,
    )
```

```python
import functools

import jax
import jax.numpy as jnp
from jax import lax
from jax.experimental import pallas as pl
from jax.experimental.pallas import tpu as pltpu
from jax.sharding import PartitionSpec as P

HEAD_DIM = 128
NT = (((1,), (1,)), ((), ()))
TN = (((0,), (0,)), ((), ()))


def attention_kernel(
    length_ref, q_ref, qt_ref, do_ref, dot_ref, kp_ref, kpt_ref, vp_ref, vpt_ref,
    ko_ref, kot_ref, vo_ref, vot_ref, keep_col_ref, keep_row_ref,
    att_ref, dq_ref, dko_ref, dvo_ref, pg_out, dko_acc, dvo_acc, pg_ref,
):
    f32, bf16 = jnp.float32, jnp.bfloat16
    scale = HEAD_DIM ** (-0.5)
    length = length_ref[0]
    steps = q_ref.shape[0]
    width = HEAD_DIM
    group_size = q_ref.shape[1] // width
    j = lax.broadcasted_iota(jnp.int32, (steps, 1), 0)
    t = lax.broadcasted_iota(jnp.int32, (1, steps), 1)
    half = steps // 2
    allowed1 = (j[:half] <= t[:, :half]) & (j[:half] < length)
    allowed2 = (j <= t[:, half:]) & (j < length)
    live = t < length
    live_col = j < length
    factor_col = (keep_col_ref[...] * live_col.astype(jnp.int32)).astype(bf16)
    factor_row = (keep_row_ref[...] * live.astype(jnp.int32)).astype(bf16)
    dko_acc[...] = jnp.zeros_like(dko_acc)
    dvo_acc[...] = jnp.zeros_like(dvo_acc)
    pg_ref[...] = jnp.zeros_like(pg_ref)

    def head(h, carry):
        cols = pl.ds(pl.multiple_of(h * width, width), width)
        q = q_ref[:, cols]
        qt = qt_ref[cols, :]
        kp = kp_ref[...]
        ko = ko_ref[...]
        vp = vp_ref[...]
        vo = vo_ref[...]
        sp = jnp.dot(kp, qt, preferred_element_type=f32) * scale
        so1 = jnp.dot(ko[:half], qt[:, :half], preferred_element_type=f32) * scale
        so2 = jnp.dot(ko, qt[:, half:], preferred_element_type=f32) * scale
        so1 = jnp.where(allowed1, so1, -jnp.inf)
        so2 = jnp.where(allowed2, so2, -jnp.inf)
        top = jnp.maximum(
            sp.max(0, keepdims=True),
            jnp.concatenate([so1.max(0, keepdims=True), so2.max(0, keepdims=True)], 1),
        )
        ep = jnp.exp(sp - top)
        eo1 = jnp.exp(so1 - top[:, :half])
        eo2 = jnp.exp(so2 - top[:, half:])
        inverse = 1.0 / (
            ep.sum(0, keepdims=True)
            + jnp.concatenate([eo1.sum(0, keepdims=True), eo2.sum(0, keepdims=True)], 1)
        )
        pp = ep * inverse
        po1 = eo1 * inverse[:, :half]
        po2 = eo2 * inverse[:, half:]
        wp = pp.astype(bf16)
        wo1 = po1.astype(bf16)
        wo2 = po2.astype(bf16)
        vot = vot_ref[...]
        kot = kot_ref[...]
        out = lax.dot_general(wp, vp, TN, preferred_element_type=f32) + jnp.concatenate(
            [
                lax.dot_general(wo1, vo[:half], TN, preferred_element_type=f32),
                lax.dot_general(wo2, vo, TN, preferred_element_type=f32),
            ],
            0,
        )
        att = jnp.where(live_col, out, 0.0).astype(bf16)
        att_ref[:, cols] = att
        do = do_ref[:, cols] * factor_col
        dot = dot_ref[cols, :] * factor_row
        delta = (dot.astype(f32) * att.astype(f32).T).sum(0, keepdims=True)
        dpp = jnp.dot(vp, dot, preferred_element_type=f32)
        dpo1 = jnp.dot(vo[:half], dot[:, :half], preferred_element_type=f32)
        dpo2 = jnp.dot(vo, dot[:, half:], preferred_element_type=f32)
        dsp = (pp * (dpp - delta)).astype(bf16)
        dso1 = (po1 * (dpo1 - delta[:, :half])).astype(bf16)
        dso2 = (po2 * (dpo2 - delta[:, half:])).astype(bf16)
        dq = lax.dot_general(dsp, kp, TN, preferred_element_type=f32) + jnp.concatenate(
            [
                lax.dot_general(dso1, ko[:half], TN, preferred_element_type=f32),
                lax.dot_general(dso2, ko, TN, preferred_element_type=f32),
            ],
            0,
        )
        dq_ref[:, cols] = (dq * scale).astype(bf16)
        pg_ref[:, :width] += jnp.dot(dsp, q, preferred_element_type=f32) * scale
        pg_ref[:, width:] += jnp.dot(wp, do, preferred_element_type=f32)
        dko_acc[:half, :] += jnp.dot(dso1, q[:half], preferred_element_type=f32) * scale
        dko_acc[...] += jnp.dot(dso2, q[half:], preferred_element_type=f32) * scale
        dvo_acc[:half, :] += jnp.dot(wo1, do[:half], preferred_element_type=f32)
        dvo_acc[...] += jnp.dot(wo2, do[half:], preferred_element_type=f32)
        return carry

    lax.fori_loop(0, group_size, head, 0)
    dko_ref[...] = dko_acc[...].astype(bf16)
    dvo_ref[...] = dvo_acc[...].astype(bf16)
    pg_out[:, :width] = pg_ref[:, :width].astype(bf16)
    pg_out[:, width:] = pg_ref[:, width:].astype(bf16)


def attend(length, queries, out_grad, prompt_kv, keys, values, keep, kv_count):
    steps, width = queries.shape
    group_size = width // (kv_count * HEAD_DIM)
    prompt_rows = prompt_kv.shape[0]
    heads = group_size * HEAD_DIM
    kv_block = lambda k, n: (0, k)
    kv_block_t = lambda k, n: (k, 0)
    bf16, f32 = jnp.bfloat16, jnp.float32
    return pl.pallas_call(
        attention_kernel,
        out_shape=(
            jax.ShapeDtypeStruct((steps, width), bf16),
            jax.ShapeDtypeStruct((steps, width), bf16),
            jax.ShapeDtypeStruct(keys.shape, bf16),
            jax.ShapeDtypeStruct(keys.shape, bf16),
            jax.ShapeDtypeStruct((prompt_rows, 2 * kv_count * HEAD_DIM), bf16),
        ),
        grid_spec=pltpu.PrefetchScalarGridSpec(
            num_scalar_prefetch=1,
            grid=(kv_count,),
            in_specs=[
                pl.BlockSpec((steps, heads), kv_block),
                pl.BlockSpec((heads, steps), kv_block_t),
                pl.BlockSpec((steps, heads), kv_block),
                pl.BlockSpec((heads, steps), kv_block_t),
                pl.BlockSpec((prompt_rows, HEAD_DIM), kv_block),
                pl.BlockSpec((HEAD_DIM, prompt_rows), kv_block_t),
                pl.BlockSpec((prompt_rows, HEAD_DIM), lambda k, n: (0, k + kv_count)),
                pl.BlockSpec((HEAD_DIM, prompt_rows), lambda k, n: (k + kv_count, 0)),
                pl.BlockSpec((steps, HEAD_DIM), kv_block),
                pl.BlockSpec((HEAD_DIM, steps), kv_block_t),
                pl.BlockSpec((steps, HEAD_DIM), kv_block),
                pl.BlockSpec((HEAD_DIM, steps), kv_block_t),
                pl.BlockSpec((steps, 1), lambda k, n: (0, 0)),
                pl.BlockSpec((1, steps), lambda k, n: (0, 0)),
            ],
            out_specs=[
                pl.BlockSpec((steps, heads), kv_block),
                pl.BlockSpec((steps, heads), kv_block),
                pl.BlockSpec((steps, HEAD_DIM), kv_block),
                pl.BlockSpec((steps, HEAD_DIM), kv_block),
                pl.BlockSpec((prompt_rows, 2 * HEAD_DIM), kv_block),
            ],
            scratch_shapes=[pltpu.VMEM((steps, HEAD_DIM), f32)] * 2
            + [pltpu.VMEM((prompt_rows, 2 * HEAD_DIM), f32)],
        ),
        compiler_params=pltpu.CompilerParams(
            dimension_semantics=("arbitrary",),
            vmem_limit_bytes=60 * 1024 * 1024,
        ),
    )(
        length,
        queries,
        queries.T,
        out_grad,
        out_grad.T,
        prompt_kv,
        prompt_kv.T,
        prompt_kv,
        prompt_kv.T,
        keys,
        keys.T,
        values,
        values.T,
        keep,
        keep.reshape(1, steps),
    )


def per_device(
    queries, resp_keys, resp_values, prompt_keys, prompt_values, lengths, loss_mask, out_grad
):
    kv_width = resp_keys.shape[2]
    kv_count = kv_width // HEAD_DIM
    rows_here = prompt_keys.shape[0]
    groups = lax.axis_size("head")
    devices = lax.axis_size("resp") * groups
    both = jnp.concatenate(
        [prompt_keys.reshape(rows_here, groups, kv_width), prompt_values.reshape(rows_here, groups, kv_width)],
        2,
    ).transpose(1, 0, 2)
    outgoing = jnp.broadcast_to(both[None], (devices // groups,) + both.shape).reshape(
        devices, rows_here, 2 * kv_width
    )
    gathered = lax.all_to_all(outgoing, ("resp", "head"), split_axis=0, concat_axis=0, tiled=True)
    prompt_kv = gathered.reshape(devices * rows_here, 2 * kv_width)

    steps = queries.shape[1]
    att, dq, dk, dv, prompt_parts = attend(
        lengths,
        queries.reshape(steps, -1),
        out_grad.reshape(steps, -1),
        prompt_kv,
        resp_keys.reshape(steps, kv_width),
        resp_values.reshape(steps, kv_width),
        loss_mask.reshape(steps, 1),
        kv_count,
    )
    arrived = lax.all_to_all(
        prompt_parts.reshape(devices, rows_here, 2 * kv_width),
        ("resp", "head"),
        split_axis=0,
        concat_axis=0,
        tiled=True,
    )
    summed = arrived.astype(jnp.float32).reshape(devices // groups, groups, rows_here, 2 * kv_width).sum(0)
    summed = summed.reshape(groups, rows_here, kv_count, 2, HEAD_DIM).transpose(3, 1, 0, 2, 4)
    prompt_key_grad = summed[0].reshape(rows_here, groups * kv_width)
    prompt_value_grad = summed[1].reshape(rows_here, groups * kv_width)
    return (
        att.reshape(queries.shape),
        dq.reshape(queries.shape),
        dk.reshape(resp_keys.shape),
        dv.reshape(resp_keys.shape),
        prompt_key_grad,
        prompt_value_grad,
    )


def solution(mesh):
    placed = (
        P("resp", None, "head"),
        P("resp", None, "head"),
        P("resp", None, "head"),
        P(("resp", "head"), None),
        P(("resp", "head"), None),
        P("resp"),
        P("resp", None),
        P("resp", None, "head"),
    )
    return jax.shard_map(
        per_device,
        mesh=mesh,
        in_specs=placed,
        out_specs=(
            P("resp", None, "head"),
            P("resp", None, "head"),
            P("resp", None, "head"),
            P("resp", None, "head"),
            P(("resp", "head"), None),
            P(("resp", "head"), None),
        ),
        check_vma=False,
    )
```

```python
import functools

import jax
import jax.numpy as jnp
from jax import lax
from jax.experimental import pallas as pl
from jax.experimental.pallas import tpu as pltpu
from jax.sharding import PartitionSpec as P

HEAD_DIM = 128
NT = (((1,), (1,)), ((), ()))
TN = (((0,), (0,)), ((), ()))


def attention_kernel(
    length_ref, q_ref, qt_ref, do_ref, dot_ref, kp_ref, kpt_ref, vp_ref, vpt_ref,
    ko_ref, kot_ref, vo_ref, vot_ref, keep_col_ref, keep_row_ref,
    att_ref, dq_ref, dko_ref, dvo_ref, pg_out, dko_acc, dvo_acc, pg_ref, e_scr, dp_scr, w_scr, ds_scr,
):
    f32, bf16 = jnp.float32, jnp.bfloat16
    scale = HEAD_DIM ** (-0.5)
    length = length_ref[0]
    steps = q_ref.shape[0]
    width = HEAD_DIM
    group_size = q_ref.shape[1] // width
    j = lax.broadcasted_iota(jnp.int32, (steps, 1), 0)
    t = lax.broadcasted_iota(jnp.int32, (1, steps), 1)
    half = steps // 2
    chunk = 64
    chunks = kp_ref.shape[0] // chunk
    allowed1 = (j[:half] <= t[:, :half]) & (j[:half] < length)
    allowed2 = (j <= t[:, half:]) & (j < length)
    live = t < length
    live_col = j < length
    factor_col = (keep_col_ref[...] * live_col.astype(jnp.int32)).astype(bf16)
    factor_row = (keep_row_ref[...] * live.astype(jnp.int32)).astype(bf16)
    dko_acc[...] = jnp.zeros_like(dko_acc)
    dvo_acc[...] = jnp.zeros_like(dvo_acc)
    pg_ref[...] = jnp.zeros_like(pg_ref)

    def head(h, carry):
        cols = pl.ds(pl.multiple_of(h * width, width), width)
        q = q_ref[:, cols]
        qt = qt_ref[cols, :]
        kp = kp_ref[...]
        ko = ko_ref[...]
        vp = vp_ref[...]
        vo = vo_ref[...]
        e_scr[...] = jnp.dot(kp, qt, preferred_element_type=f32)
        so1 = jnp.dot(ko[:half], qt[:, :half], preferred_element_type=f32) * scale
        so2 = jnp.dot(ko, qt[:, half:], preferred_element_type=f32) * scale
        so1 = jnp.where(allowed1, so1, -jnp.inf)
        so2 = jnp.where(allowed2, so2, -jnp.inf)
        top = jnp.maximum(
            e_scr[...].max(0, keepdims=True) * scale,
            jnp.concatenate([so1.max(0, keepdims=True), so2.max(0, keepdims=True)], 1),
        )

        def exps(c, total):
            rows = pl.ds(pl.multiple_of(c * chunk, chunk), chunk)
            e = jnp.exp(e_scr[rows, :] * scale - top)
            e_scr[rows, :] = e
            return total + e.sum(0, keepdims=True)

        prompt_total = lax.fori_loop(0, chunks, exps, jnp.zeros((1, steps), f32))
        eo1 = jnp.exp(so1 - top[:, :half])
        eo2 = jnp.exp(so2 - top[:, half:])
        inverse = 1.0 / (
            prompt_total
            + jnp.concatenate([eo1.sum(0, keepdims=True), eo2.sum(0, keepdims=True)], 1)
        )

        def weights(c, carry):
            rows = pl.ds(pl.multiple_of(c * chunk, chunk), chunk)
            w_scr[rows, :] = (e_scr[rows, :] * inverse).astype(bf16)
            return carry

        lax.fori_loop(0, chunks, weights, 0)
        po1 = eo1 * inverse[:, :half]
        po2 = eo2 * inverse[:, half:]
        wo1 = po1.astype(bf16)
        wo2 = po2.astype(bf16)
        vot = vot_ref[...]
        kot = kot_ref[...]
        out = jnp.dot(vpt_ref[...], w_scr[...], preferred_element_type=f32) + jnp.concatenate(
            [
                jnp.dot(vot[:, :half], wo1, preferred_element_type=f32),
                jnp.dot(vot, wo2, preferred_element_type=f32),
            ],
            1,
        )
        att = jnp.where(live, out, 0.0).astype(bf16).astype(f32)
        att_ref[:, cols] = att.T.astype(bf16)
        do = do_ref[:, cols] * factor_col
        dot = dot_ref[cols, :] * factor_row
        delta = (dot.astype(f32) * att).sum(0, keepdims=True)
        dp_scr[...] = jnp.dot(vp, dot, preferred_element_type=f32)
        dpo1 = jnp.dot(vo[:half], dot[:, :half], preferred_element_type=f32)
        dpo2 = jnp.dot(vo, dot[:, half:], preferred_element_type=f32)

        def grads(c, carry):
            rows = pl.ds(pl.multiple_of(c * chunk, chunk), chunk)
            ds_scr[rows, :] = (e_scr[rows, :] * inverse * (dp_scr[rows, :] - delta)).astype(bf16)
            return carry

        lax.fori_loop(0, chunks, grads, 0)
        dso1 = (po1 * (dpo1 - delta[:, :half])).astype(bf16)
        dso2 = (po2 * (dpo2 - delta[:, half:])).astype(bf16)
        dq = jnp.dot(kpt_ref[...], ds_scr[...], preferred_element_type=f32) + jnp.concatenate(
            [
                jnp.dot(kot[:, :half], dso1, preferred_element_type=f32),
                jnp.dot(kot, dso2, preferred_element_type=f32),
            ],
            1,
        )
        dq_ref[:, cols] = (dq * scale).T.astype(bf16)
        pg_ref[:, :width] += jnp.dot(ds_scr[...], q, preferred_element_type=f32) * scale
        pg_ref[:, width:] += jnp.dot(w_scr[...], do, preferred_element_type=f32)
        dko_acc[:half, :] += jnp.dot(dso1, q[:half], preferred_element_type=f32) * scale
        dko_acc[...] += jnp.dot(dso2, q[half:], preferred_element_type=f32) * scale
        dvo_acc[:half, :] += jnp.dot(wo1, do[:half], preferred_element_type=f32)
        dvo_acc[...] += jnp.dot(wo2, do[half:], preferred_element_type=f32)
        return carry

    lax.fori_loop(0, group_size, head, 0)
    dko_ref[...] = dko_acc[...].astype(bf16)
    dvo_ref[...] = dvo_acc[...].astype(bf16)
    pg_out[:, :width] = pg_ref[:, :width].astype(bf16)
    pg_out[:, width:] = pg_ref[:, width:].astype(bf16)


def attend(length, queries, out_grad, prompt_kv, keys, values, keep, kv_count):
    steps, width = queries.shape
    group_size = width // (kv_count * HEAD_DIM)
    prompt_rows = prompt_kv.shape[0]
    heads = group_size * HEAD_DIM
    kv_block = lambda k, n: (0, k)
    kv_block_t = lambda k, n: (k, 0)
    bf16, f32 = jnp.bfloat16, jnp.float32
    return pl.pallas_call(
        attention_kernel,
        out_shape=(
            jax.ShapeDtypeStruct((steps, width), bf16),
            jax.ShapeDtypeStruct((steps, width), bf16),
            jax.ShapeDtypeStruct(keys.shape, bf16),
            jax.ShapeDtypeStruct(keys.shape, bf16),
            jax.ShapeDtypeStruct((prompt_rows, 2 * kv_count * HEAD_DIM), bf16),
        ),
        grid_spec=pltpu.PrefetchScalarGridSpec(
            num_scalar_prefetch=1,
            grid=(kv_count,),
            in_specs=[
                pl.BlockSpec((steps, heads), kv_block),
                pl.BlockSpec((heads, steps), kv_block_t),
                pl.BlockSpec((steps, heads), kv_block),
                pl.BlockSpec((heads, steps), kv_block_t),
                pl.BlockSpec((prompt_rows, HEAD_DIM), kv_block),
                pl.BlockSpec((HEAD_DIM, prompt_rows), kv_block_t),
                pl.BlockSpec((prompt_rows, HEAD_DIM), lambda k, n: (0, k + kv_count)),
                pl.BlockSpec((HEAD_DIM, prompt_rows), lambda k, n: (k + kv_count, 0)),
                pl.BlockSpec((steps, HEAD_DIM), kv_block),
                pl.BlockSpec((HEAD_DIM, steps), kv_block_t),
                pl.BlockSpec((steps, HEAD_DIM), kv_block),
                pl.BlockSpec((HEAD_DIM, steps), kv_block_t),
                pl.BlockSpec((steps, 1), lambda k, n: (0, 0)),
                pl.BlockSpec((1, steps), lambda k, n: (0, 0)),
            ],
            out_specs=[
                pl.BlockSpec((steps, heads), kv_block),
                pl.BlockSpec((steps, heads), kv_block),
                pl.BlockSpec((steps, HEAD_DIM), kv_block),
                pl.BlockSpec((steps, HEAD_DIM), kv_block),
                pl.BlockSpec((prompt_rows, 2 * HEAD_DIM), kv_block),
            ],
            scratch_shapes=[pltpu.VMEM((steps, HEAD_DIM), f32)] * 2
            + [pltpu.VMEM((prompt_rows, 2 * HEAD_DIM), f32)]
            + [pltpu.VMEM((prompt_rows, steps), f32)] * 2
            + [pltpu.VMEM((prompt_rows, steps), bf16)] * 2,
        ),
        compiler_params=pltpu.CompilerParams(
            dimension_semantics=("arbitrary",),
            vmem_limit_bytes=60 * 1024 * 1024,
        ),
    )(
        length,
        queries,
        queries.T,
        out_grad,
        out_grad.T,
        prompt_kv,
        prompt_kv.T,
        prompt_kv,
        prompt_kv.T,
        keys,
        keys.T,
        values,
        values.T,
        keep,
        keep.reshape(1, steps),
    )


def per_device(
    queries, resp_keys, resp_values, prompt_keys, prompt_values, lengths, loss_mask, out_grad
):
    kv_width = resp_keys.shape[2]
    kv_count = kv_width // HEAD_DIM
    rows_here = prompt_keys.shape[0]
    groups = lax.axis_size("head")
    devices = lax.axis_size("resp") * groups
    both = jnp.concatenate(
        [prompt_keys.reshape(rows_here, groups, kv_width), prompt_values.reshape(rows_here, groups, kv_width)],
        2,
    ).transpose(1, 0, 2)
    outgoing = jnp.broadcast_to(both[None], (devices // groups,) + both.shape).reshape(
        devices, rows_here, 2 * kv_width
    )
    gathered = lax.all_to_all(outgoing, ("resp", "head"), split_axis=0, concat_axis=0, tiled=True)
    prompt_kv = gathered.reshape(devices * rows_here, 2 * kv_width)

    steps = queries.shape[1]
    att, dq, dk, dv, prompt_parts = attend(
        lengths,
        queries.reshape(steps, -1),
        out_grad.reshape(steps, -1),
        prompt_kv,
        resp_keys.reshape(steps, kv_width),
        resp_values.reshape(steps, kv_width),
        loss_mask.reshape(steps, 1),
        kv_count,
    )
    arrived = lax.all_to_all(
        prompt_parts.reshape(devices, rows_here, 2 * kv_width),
        ("resp", "head"),
        split_axis=0,
        concat_axis=0,
        tiled=True,
    )
    summed = arrived.astype(jnp.float32).reshape(devices // groups, groups, rows_here, 2 * kv_width).sum(0)
    summed = summed.reshape(groups, rows_here, kv_count, 2, HEAD_DIM).transpose(3, 1, 0, 2, 4)
    prompt_key_grad = summed[0].reshape(rows_here, groups * kv_width)
    prompt_value_grad = summed[1].reshape(rows_here, groups * kv_width)
    return (
        att.reshape(queries.shape),
        dq.reshape(queries.shape),
        dk.reshape(resp_keys.shape),
        dv.reshape(resp_keys.shape),
        prompt_key_grad,
        prompt_value_grad,
    )


def solution(mesh):
    placed = (
        P("resp", None, "head"),
        P("resp", None, "head"),
        P("resp", None, "head"),
        P(("resp", "head"), None),
        P(("resp", "head"), None),
        P("resp"),
        P("resp", None),
        P("resp", None, "head"),
    )
    return jax.shard_map(
        per_device,
        mesh=mesh,
        in_specs=placed,
        out_specs=(
            P("resp", None, "head"),
            P("resp", None, "head"),
            P("resp", None, "head"),
            P("resp", None, "head"),
            P(("resp", "head"), None),
            P(("resp", "head"), None),
        ),
        check_vma=False,
    )
```

```python
import functools

import jax
import jax.numpy as jnp
from jax import lax
from jax.experimental import pallas as pl
from jax.experimental.pallas import tpu as pltpu
from jax.sharding import PartitionSpec as P

HEAD_DIM = 128
NT = (((1,), (1,)), ((), ()))
TN = (((0,), (0,)), ((), ()))


def attention_kernel(
    length_ref, q_ref, qt_ref, do_ref, dot_ref, kp_ref, kpt_ref, vp_ref, vpt_ref,
    ko_ref, kot_ref, vo_ref, vot_ref, keep_col_ref, keep_row_ref,
    att_ref, dq_ref, dko_ref, dvo_ref, pg_out, dko_acc, dvo_acc, pg_ref,
):
    f32, bf16 = jnp.float32, jnp.bfloat16
    scale = HEAD_DIM ** (-0.5)
    length = length_ref[0]
    steps = q_ref.shape[0]
    width = HEAD_DIM
    group_size = q_ref.shape[1] // width
    j = lax.broadcasted_iota(jnp.int32, (steps, 1), 0)
    t = lax.broadcasted_iota(jnp.int32, (1, steps), 1)
    half = steps // 2
    allowed1 = (j[:half] <= t[:, :half]) & (j[:half] < length)
    allowed2 = (j <= t[:, half:]) & (j < length)
    live = t < length
    live_col = j < length
    factor_col = (keep_col_ref[...] * live_col.astype(jnp.int32)).astype(bf16)
    factor_row = (keep_row_ref[...] * live.astype(jnp.int32)).astype(bf16)
    dko_acc[...] = jnp.zeros_like(dko_acc)
    dvo_acc[...] = jnp.zeros_like(dvo_acc)
    pg_ref[...] = jnp.zeros_like(pg_ref)

    def head(h, carry):
        cols = pl.ds(pl.multiple_of(h * width, width), width)
        q = q_ref[:, cols]
        qt = qt_ref[cols, :]
        kp = kp_ref[...]
        ko = ko_ref[...]
        vp = vp_ref[...]
        vo = vo_ref[...]
        sp = jnp.dot(kp, qt, preferred_element_type=f32) * scale
        so1 = jnp.dot(ko[:half], qt[:, :half], preferred_element_type=f32) * scale
        so2 = jnp.dot(ko, qt[:, half:], preferred_element_type=f32) * scale
        so1 = jnp.where(allowed1, so1, -jnp.inf)
        so2 = jnp.where(allowed2, so2, -jnp.inf)
        top = jnp.maximum(
            sp.max(0, keepdims=True),
            jnp.concatenate([so1.max(0, keepdims=True), so2.max(0, keepdims=True)], 1),
        )
        ep = jnp.exp(sp - top)
        eo1 = jnp.exp(so1 - top[:, :half])
        eo2 = jnp.exp(so2 - top[:, half:])
        inverse = 1.0 / (
            ep.sum(0, keepdims=True)
            + jnp.concatenate([eo1.sum(0, keepdims=True), eo2.sum(0, keepdims=True)], 1)
        )
        wp = (ep * inverse).astype(bf16)
        wo1 = (eo1 * inverse[:, :half]).astype(bf16)
        wo2 = (eo2 * inverse[:, half:]).astype(bf16)
        vot = vot_ref[...]
        kot = kot_ref[...]
        out = jnp.dot(vpt_ref[...], wp, preferred_element_type=f32) + jnp.concatenate(
            [
                jnp.dot(vot[:, :half], wo1, preferred_element_type=f32),
                jnp.dot(vot, wo2, preferred_element_type=f32),
            ],
            1,
        )
        att = jnp.where(live, out, 0.0).astype(bf16).astype(f32)
        att_ref[:, cols] = att.T.astype(bf16)
        do = do_ref[:, cols] * factor_col
        dot = dot_ref[cols, :] * factor_row
        delta = (dot.astype(f32) * att).sum(0, keepdims=True)
        dpp = jnp.dot(vp, dot, preferred_element_type=f32)
        dpo1 = jnp.dot(vo[:half], dot[:, :half], preferred_element_type=f32)
        dpo2 = jnp.dot(vo, dot[:, half:], preferred_element_type=f32)
        dsp = (ep * inverse * (dpp - delta)).astype(bf16)
        dso1 = (eo1 * inverse[:, :half] * (dpo1 - delta[:, :half])).astype(bf16)
        dso2 = (eo2 * inverse[:, half:] * (dpo2 - delta[:, half:])).astype(bf16)
        dq = jnp.dot(kpt_ref[...], dsp, preferred_element_type=f32) + jnp.concatenate(
            [
                jnp.dot(kot[:, :half], dso1, preferred_element_type=f32),
                jnp.dot(kot, dso2, preferred_element_type=f32),
            ],
            1,
        )
        dq_ref[:, cols] = (dq * scale).T.astype(bf16)
        pg_ref[:, :width] += jnp.dot(dsp, q, preferred_element_type=f32) * scale
        pg_ref[:, width:] += jnp.dot(wp, do, preferred_element_type=f32)
        dko_acc[:half, :] += jnp.dot(dso1, q[:half], preferred_element_type=f32) * scale
        dko_acc[...] += jnp.dot(dso2, q[half:], preferred_element_type=f32) * scale
        dvo_acc[:half, :] += jnp.dot(wo1, do[:half], preferred_element_type=f32)
        dvo_acc[...] += jnp.dot(wo2, do[half:], preferred_element_type=f32)
        return carry

    lax.fori_loop(0, group_size, head, 0)
    dko_ref[...] = dko_acc[...].astype(bf16)
    dvo_ref[...] = dvo_acc[...].astype(bf16)
    pg_out[:, :width] = pg_ref[:, :width].astype(bf16)
    pg_out[:, width:] = pg_ref[:, width:].astype(bf16)


def attend(length, queries, out_grad, prompt_kv, keys, values, keep, kv_count):
    steps, width = queries.shape
    group_size = width // (kv_count * HEAD_DIM)
    prompt_rows = prompt_kv.shape[0]
    heads = group_size * HEAD_DIM
    kv_block = lambda k, n: (0, k)
    kv_block_t = lambda k, n: (k, 0)
    bf16, f32 = jnp.bfloat16, jnp.float32
    return pl.pallas_call(
        attention_kernel,
        out_shape=(
            jax.ShapeDtypeStruct((steps, width), bf16),
            jax.ShapeDtypeStruct((steps, width), bf16),
            jax.ShapeDtypeStruct(keys.shape, bf16),
            jax.ShapeDtypeStruct(keys.shape, bf16),
            jax.ShapeDtypeStruct((prompt_rows, 2 * kv_count * HEAD_DIM), bf16),
        ),
        grid_spec=pltpu.PrefetchScalarGridSpec(
            num_scalar_prefetch=1,
            grid=(kv_count,),
            in_specs=[
                pl.BlockSpec((steps, heads), kv_block),
                pl.BlockSpec((heads, steps), kv_block_t),
                pl.BlockSpec((steps, heads), kv_block),
                pl.BlockSpec((heads, steps), kv_block_t),
                pl.BlockSpec((prompt_rows, HEAD_DIM), kv_block),
                pl.BlockSpec((HEAD_DIM, prompt_rows), kv_block_t),
                pl.BlockSpec((prompt_rows, HEAD_DIM), lambda k, n: (0, k + kv_count)),
                pl.BlockSpec((HEAD_DIM, prompt_rows), lambda k, n: (k + kv_count, 0)),
                pl.BlockSpec((steps, HEAD_DIM), kv_block),
                pl.BlockSpec((HEAD_DIM, steps), kv_block_t),
                pl.BlockSpec((steps, HEAD_DIM), kv_block),
                pl.BlockSpec((HEAD_DIM, steps), kv_block_t),
                pl.BlockSpec((steps, 1), lambda k, n: (0, 0)),
                pl.BlockSpec((1, steps), lambda k, n: (0, 0)),
            ],
            out_specs=[
                pl.BlockSpec((steps, heads), kv_block),
                pl.BlockSpec((steps, heads), kv_block),
                pl.BlockSpec((steps, HEAD_DIM), kv_block),
                pl.BlockSpec((steps, HEAD_DIM), kv_block),
                pl.BlockSpec((prompt_rows, 2 * HEAD_DIM), kv_block),
            ],
            scratch_shapes=[pltpu.VMEM((steps, HEAD_DIM), f32)] * 2
            + [pltpu.VMEM((prompt_rows, 2 * HEAD_DIM), f32)],
        ),
        compiler_params=pltpu.CompilerParams(
            dimension_semantics=("arbitrary",),
            vmem_limit_bytes=60 * 1024 * 1024,
        ),
    )(
        length,
        queries,
        queries.T,
        out_grad,
        out_grad.T,
        prompt_kv,
        prompt_kv.T,
        prompt_kv,
        prompt_kv.T,
        keys,
        keys.T,
        values,
        values.T,
        keep,
        keep.reshape(1, steps),
    )


def per_device(
    queries, resp_keys, resp_values, prompt_keys, prompt_values, lengths, loss_mask, out_grad
):
    kv_width = resp_keys.shape[2]
    kv_count = kv_width // HEAD_DIM
    rows_here = prompt_keys.shape[0]
    groups = lax.axis_size("head")
    devices = lax.axis_size("resp") * groups
    both = jnp.concatenate(
        [prompt_keys.reshape(rows_here, groups, kv_width), prompt_values.reshape(rows_here, groups, kv_width)],
        2,
    ).transpose(1, 0, 2)
    outgoing = jnp.broadcast_to(both[None], (devices // groups,) + both.shape).reshape(
        devices, rows_here, 2 * kv_width
    )
    gathered = lax.all_to_all(outgoing, ("resp", "head"), split_axis=0, concat_axis=0, tiled=True)
    prompt_kv = gathered.reshape(devices * rows_here, 2 * kv_width)

    steps = queries.shape[1]
    att, dq, dk, dv, prompt_parts = attend(
        lengths,
        queries.reshape(steps, -1),
        out_grad.reshape(steps, -1),
        prompt_kv,
        resp_keys.reshape(steps, kv_width),
        resp_values.reshape(steps, kv_width),
        loss_mask.reshape(steps, 1),
        kv_count,
    )
    arrived = lax.all_to_all(
        prompt_parts.reshape(devices, rows_here, 2 * kv_width),
        ("resp", "head"),
        split_axis=0,
        concat_axis=0,
        tiled=True,
    )
    summed = arrived.astype(jnp.float32).reshape(devices // groups, groups, rows_here, 2 * kv_width).sum(0)
    summed = summed.reshape(groups, rows_here, kv_count, 2, HEAD_DIM).transpose(3, 1, 0, 2, 4)
    prompt_key_grad = summed[0].reshape(rows_here, groups * kv_width)
    prompt_value_grad = summed[1].reshape(rows_here, groups * kv_width)
    return (
        att.reshape(queries.shape),
        dq.reshape(queries.shape),
        dk.reshape(resp_keys.shape),
        dv.reshape(resp_keys.shape),
        prompt_key_grad,
        prompt_value_grad,
    )


def solution(mesh):
    placed = (
        P("resp", None, "head"),
        P("resp", None, "head"),
        P("resp", None, "head"),
        P(("resp", "head"), None),
        P(("resp", "head"), None),
        P("resp"),
        P("resp", None),
        P("resp", None, "head"),
    )
    return jax.shard_map(
        per_device,
        mesh=mesh,
        in_specs=placed,
        out_specs=(
            P("resp", None, "head"),
            P("resp", None, "head"),
            P("resp", None, "head"),
            P("resp", None, "head"),
            P(("resp", "head"), None),
            P(("resp", "head"), None),
        ),
        check_vma=False,
    )
```

```python
import functools

import jax
import jax.numpy as jnp
from jax import lax
from jax.experimental import pallas as pl
from jax.experimental.pallas import tpu as pltpu
from jax.sharding import PartitionSpec as P

HEAD_DIM = 128
NT = (((1,), (1,)), ((), ()))
TN = (((0,), (0,)), ((), ()))


def attention_kernel(
    length_ref, q_ref, qt_ref, do_ref, dot_ref, kp_ref, kpt_ref, vp_ref, vpt_ref,
    ko_ref, kot_ref, vo_ref, vot_ref, keep_col_ref, keep_row_ref,
    att_ref, dq_ref, dko_ref, dvo_ref, pg_out, dko_acc, dvo_acc, pg_ref,
):
    f32, bf16 = jnp.float32, jnp.bfloat16
    scale = HEAD_DIM ** (-0.5)
    length = length_ref[0]
    steps = q_ref.shape[0]
    width = HEAD_DIM
    group_size = q_ref.shape[1] // width
    j = lax.broadcasted_iota(jnp.int32, (steps, 1), 0)
    t = lax.broadcasted_iota(jnp.int32, (1, steps), 1)
    blocks = 4
    part = steps // blocks
    allowed = [
        (j[: (b + 1) * part] <= t[:, b * part : (b + 1) * part]) & (j[: (b + 1) * part] < length)
        for b in range(blocks)
    ]
    live = t < length
    live_col = j < length
    factor_col = (keep_col_ref[...] * live_col.astype(jnp.int32)).astype(bf16)
    factor_row = (keep_row_ref[...] * live.astype(jnp.int32)).astype(bf16)
    dko_acc[...] = jnp.zeros_like(dko_acc)
    dvo_acc[...] = jnp.zeros_like(dvo_acc)
    pg_ref[...] = jnp.zeros_like(pg_ref)

    def head(h, carry):
        cols = pl.ds(pl.multiple_of(h * width, width), width)
        q = q_ref[:, cols]
        qt = qt_ref[cols, :]
        kp = kp_ref[...]
        ko = ko_ref[...]
        vp = vp_ref[...]
        vo = vo_ref[...]
        sp = jnp.dot(kp, qt, preferred_element_type=f32) * scale
        so = [
            jnp.where(
                allowed[b],
                jnp.dot(ko[: (b + 1) * part], qt[:, b * part : (b + 1) * part], preferred_element_type=f32)
                * scale,
                -jnp.inf,
            )
            for b in range(blocks)
        ]
        top = jnp.maximum(
            sp.max(0, keepdims=True), jnp.concatenate([s.max(0, keepdims=True) for s in so], 1)
        )
        ep = jnp.exp(sp - top)
        eo = [jnp.exp(s - top[:, b * part : (b + 1) * part]) for b, s in enumerate(so)]
        inverse = 1.0 / (
            ep.sum(0, keepdims=True) + jnp.concatenate([e.sum(0, keepdims=True) for e in eo], 1)
        )
        pp = ep * inverse
        po = [e * inverse[:, b * part : (b + 1) * part] for b, e in enumerate(eo)]
        wp = pp.astype(bf16)
        wo = [p.astype(bf16) for p in po]
        vot = vot_ref[...]
        kot = kot_ref[...]
        out = jnp.dot(vpt_ref[...], wp, preferred_element_type=f32) + jnp.concatenate(
            [jnp.dot(vot[:, : (b + 1) * part], w, preferred_element_type=f32) for b, w in enumerate(wo)], 1
        )
        att = jnp.where(live, out, 0.0).astype(bf16).astype(f32)
        att_ref[:, cols] = att.T.astype(bf16)
        do = do_ref[:, cols] * factor_col
        dot = dot_ref[cols, :] * factor_row
        delta = (dot.astype(f32) * att).sum(0, keepdims=True)
        dpp = jnp.dot(vp, dot, preferred_element_type=f32)
        dsp = (pp * (dpp - delta)).astype(bf16)
        dso = [
            (
                p
                * (
                    jnp.dot(vo[: (b + 1) * part], dot[:, b * part : (b + 1) * part], preferred_element_type=f32)
                    - delta[:, b * part : (b + 1) * part]
                )
            ).astype(bf16)
            for b, p in enumerate(po)
        ]
        dq = jnp.dot(kpt_ref[...], dsp, preferred_element_type=f32) + jnp.concatenate(
            [jnp.dot(kot[:, : (b + 1) * part], d, preferred_element_type=f32) for b, d in enumerate(dso)], 1
        )
        dq_ref[:, cols] = (dq * scale).T.astype(bf16)
        pg_ref[:, :width] += jnp.dot(dsp, q, preferred_element_type=f32) * scale
        pg_ref[:, width:] += jnp.dot(wp, do, preferred_element_type=f32)
        for b in range(blocks):
            rows = slice(0, (b + 1) * part)
            tb = slice(b * part, (b + 1) * part)
            dko_acc[rows, :] += jnp.dot(dso[b], q[tb], preferred_element_type=f32) * scale
            dvo_acc[rows, :] += jnp.dot(wo[b], do[tb], preferred_element_type=f32)
        return carry

    lax.fori_loop(0, group_size, head, 0)
    dko_ref[...] = dko_acc[...].astype(bf16)
    dvo_ref[...] = dvo_acc[...].astype(bf16)
    pg_out[:, :width] = pg_ref[:, :width].astype(bf16)
    pg_out[:, width:] = pg_ref[:, width:].astype(bf16)


def attend(length, queries, out_grad, prompt_kv, keys, values, keep, kv_count):
    steps, width = queries.shape
    group_size = width // (kv_count * HEAD_DIM)
    prompt_rows = prompt_kv.shape[0]
    heads = group_size * HEAD_DIM
    kv_block = lambda k, n: (0, k)
    kv_block_t = lambda k, n: (k, 0)
    bf16, f32 = jnp.bfloat16, jnp.float32
    return pl.pallas_call(
        attention_kernel,
        out_shape=(
            jax.ShapeDtypeStruct((steps, width), bf16),
            jax.ShapeDtypeStruct((steps, width), bf16),
            jax.ShapeDtypeStruct(keys.shape, bf16),
            jax.ShapeDtypeStruct(keys.shape, bf16),
            jax.ShapeDtypeStruct((prompt_rows, 2 * kv_count * HEAD_DIM), bf16),
        ),
        grid_spec=pltpu.PrefetchScalarGridSpec(
            num_scalar_prefetch=1,
            grid=(kv_count,),
            in_specs=[
                pl.BlockSpec((steps, heads), kv_block),
                pl.BlockSpec((heads, steps), kv_block_t),
                pl.BlockSpec((steps, heads), kv_block),
                pl.BlockSpec((heads, steps), kv_block_t),
                pl.BlockSpec((prompt_rows, HEAD_DIM), kv_block),
                pl.BlockSpec((HEAD_DIM, prompt_rows), kv_block_t),
                pl.BlockSpec((prompt_rows, HEAD_DIM), lambda k, n: (0, k + kv_count)),
                pl.BlockSpec((HEAD_DIM, prompt_rows), lambda k, n: (k + kv_count, 0)),
                pl.BlockSpec((steps, HEAD_DIM), kv_block),
                pl.BlockSpec((HEAD_DIM, steps), kv_block_t),
                pl.BlockSpec((steps, HEAD_DIM), kv_block),
                pl.BlockSpec((HEAD_DIM, steps), kv_block_t),
                pl.BlockSpec((steps, 1), lambda k, n: (0, 0)),
                pl.BlockSpec((1, steps), lambda k, n: (0, 0)),
            ],
            out_specs=[
                pl.BlockSpec((steps, heads), kv_block),
                pl.BlockSpec((steps, heads), kv_block),
                pl.BlockSpec((steps, HEAD_DIM), kv_block),
                pl.BlockSpec((steps, HEAD_DIM), kv_block),
                pl.BlockSpec((prompt_rows, 2 * HEAD_DIM), kv_block),
            ],
            scratch_shapes=[pltpu.VMEM((steps, HEAD_DIM), f32)] * 2
            + [pltpu.VMEM((prompt_rows, 2 * HEAD_DIM), f32)],
        ),
        compiler_params=pltpu.CompilerParams(
            dimension_semantics=("arbitrary",),
            vmem_limit_bytes=60 * 1024 * 1024,
        ),
    )(
        length,
        queries,
        queries.T,
        out_grad,
        out_grad.T,
        prompt_kv,
        prompt_kv.T,
        prompt_kv,
        prompt_kv.T,
        keys,
        keys.T,
        values,
        values.T,
        keep,
        keep.reshape(1, steps),
    )


def per_device(
    queries, resp_keys, resp_values, prompt_keys, prompt_values, lengths, loss_mask, out_grad
):
    kv_width = resp_keys.shape[2]
    kv_count = kv_width // HEAD_DIM
    rows_here = prompt_keys.shape[0]
    groups = lax.axis_size("head")
    devices = lax.axis_size("resp") * groups
    both = jnp.concatenate(
        [prompt_keys.reshape(rows_here, groups, kv_width), prompt_values.reshape(rows_here, groups, kv_width)],
        2,
    ).transpose(1, 0, 2)
    outgoing = jnp.broadcast_to(both[None], (devices // groups,) + both.shape).reshape(
        devices, rows_here, 2 * kv_width
    )
    gathered = lax.all_to_all(outgoing, ("resp", "head"), split_axis=0, concat_axis=0, tiled=True)
    prompt_kv = gathered.reshape(devices * rows_here, 2 * kv_width)

    steps = queries.shape[1]
    att, dq, dk, dv, prompt_parts = attend(
        lengths,
        queries.reshape(steps, -1),
        out_grad.reshape(steps, -1),
        prompt_kv,
        resp_keys.reshape(steps, kv_width),
        resp_values.reshape(steps, kv_width),
        loss_mask.reshape(steps, 1),
        kv_count,
    )
    arrived = lax.all_to_all(
        prompt_parts.reshape(devices, rows_here, 2 * kv_width),
        ("resp", "head"),
        split_axis=0,
        concat_axis=0,
        tiled=True,
    )
    summed = arrived.astype(jnp.float32).reshape(devices // groups, groups, rows_here, 2 * kv_width).sum(0)
    summed = summed.reshape(groups, rows_here, kv_count, 2, HEAD_DIM).transpose(3, 1, 0, 2, 4)
    prompt_key_grad = summed[0].reshape(rows_here, groups * kv_width)
    prompt_value_grad = summed[1].reshape(rows_here, groups * kv_width)
    return (
        att.reshape(queries.shape),
        dq.reshape(queries.shape),
        dk.reshape(resp_keys.shape),
        dv.reshape(resp_keys.shape),
        prompt_key_grad,
        prompt_value_grad,
    )


def solution(mesh):
    placed = (
        P("resp", None, "head"),
        P("resp", None, "head"),
        P("resp", None, "head"),
        P(("resp", "head"), None),
        P(("resp", "head"), None),
        P("resp"),
        P("resp", None),
        P("resp", None, "head"),
    )
    return jax.shard_map(
        per_device,
        mesh=mesh,
        in_specs=placed,
        out_specs=(
            P("resp", None, "head"),
            P("resp", None, "head"),
            P("resp", None, "head"),
            P("resp", None, "head"),
            P(("resp", "head"), None),
            P(("resp", "head"), None),
        ),
        check_vma=False,
    )
```

```python
import functools

import jax
import jax.numpy as jnp
from jax import lax
from jax.experimental import pallas as pl
from jax.experimental.pallas import tpu as pltpu
from jax.sharding import PartitionSpec as P

HEAD_DIM = 128
NT = (((1,), (1,)), ((), ()))
TN = (((0,), (0,)), ((), ()))


def attention_kernel(
    length_ref, q_ref, qt_ref, do_ref, dot_ref, pkv_ref,
    ko_ref, kot_ref, vo_ref, vot_ref, keep_col_ref, keep_row_ref,
    att_ref, dq_ref, dko_ref, dvo_ref, pg_out, dko_acc, dvo_acc, pg_ref, kpt_ref, vpt_ref,
):
    f32, bf16 = jnp.float32, jnp.bfloat16
    scale = HEAD_DIM ** (-0.5)
    length = length_ref[0]
    steps = q_ref.shape[0]
    width = HEAD_DIM
    group_size = q_ref.shape[1] // width
    j = lax.broadcasted_iota(jnp.int32, (steps, 1), 0)
    t = lax.broadcasted_iota(jnp.int32, (1, steps), 1)
    half = steps // 2
    allowed1 = (j[:half] <= t[:, :half]) & (j[:half] < length)
    allowed2 = (j <= t[:, half:]) & (j < length)
    live = t < length
    live_col = j < length
    factor_col = (keep_col_ref[...] * live_col.astype(jnp.int32)).astype(bf16)
    factor_row = (keep_row_ref[...] * live.astype(jnp.int32)).astype(bf16)
    k = pl.program_id(0)
    kp_ref = pkv_ref.at[:, pl.ds(pl.multiple_of(k * width, width), width)]
    vp_ref = pkv_ref.at[:, pl.ds(pl.multiple_of((k + pl.num_programs(0)) * width, width), width)]
    kpt_ref[...] = kp_ref[...].astype(f32).T.astype(bf16)
    vpt_ref[...] = vp_ref[...].astype(f32).T.astype(bf16)
    dko_acc[...] = jnp.zeros_like(dko_acc)
    dvo_acc[...] = jnp.zeros_like(dvo_acc)
    pg_ref[...] = jnp.zeros_like(pg_ref)

    def head(h, carry):
        cols = pl.ds(pl.multiple_of(h * width, width), width)
        q = q_ref[:, cols]
        qt = qt_ref[cols, :]
        kp = kp_ref[...]
        ko = ko_ref[...]
        vp = vp_ref[...]
        vo = vo_ref[...]
        sp = jnp.dot(kp, qt, preferred_element_type=f32) * scale
        so1 = jnp.dot(ko[:half], qt[:, :half], preferred_element_type=f32) * scale
        so2 = jnp.dot(ko, qt[:, half:], preferred_element_type=f32) * scale
        so1 = jnp.where(allowed1, so1, -jnp.inf)
        so2 = jnp.where(allowed2, so2, -jnp.inf)
        top = jnp.maximum(
            sp.max(0, keepdims=True),
            jnp.concatenate([so1.max(0, keepdims=True), so2.max(0, keepdims=True)], 1),
        )
        ep = jnp.exp(sp - top)
        eo1 = jnp.exp(so1 - top[:, :half])
        eo2 = jnp.exp(so2 - top[:, half:])
        inverse = 1.0 / (
            ep.sum(0, keepdims=True)
            + jnp.concatenate([eo1.sum(0, keepdims=True), eo2.sum(0, keepdims=True)], 1)
        )
        pp = ep * inverse
        po1 = eo1 * inverse[:, :half]
        po2 = eo2 * inverse[:, half:]
        wp = pp.astype(bf16)
        wo1 = po1.astype(bf16)
        wo2 = po2.astype(bf16)
        vot = vot_ref[...]
        kot = kot_ref[...]
        out = jnp.dot(vpt_ref[...], wp, preferred_element_type=f32) + jnp.concatenate(
            [
                jnp.dot(vot[:, :half], wo1, preferred_element_type=f32),
                jnp.dot(vot, wo2, preferred_element_type=f32),
            ],
            1,
        )
        att = jnp.where(live, out, 0.0).astype(bf16).astype(f32)
        att_ref[:, cols] = att.T.astype(bf16)
        do = do_ref[:, cols] * factor_col
        dot = dot_ref[cols, :] * factor_row
        delta = (dot.astype(f32) * att).sum(0, keepdims=True)
        dpp = jnp.dot(vp, dot, preferred_element_type=f32)
        dpo1 = jnp.dot(vo[:half], dot[:, :half], preferred_element_type=f32)
        dpo2 = jnp.dot(vo, dot[:, half:], preferred_element_type=f32)
        dsp = (pp * (dpp - delta)).astype(bf16)
        dso1 = (po1 * (dpo1 - delta[:, :half])).astype(bf16)
        dso2 = (po2 * (dpo2 - delta[:, half:])).astype(bf16)
        dq = jnp.dot(kpt_ref[...], dsp, preferred_element_type=f32) + jnp.concatenate(
            [
                jnp.dot(kot[:, :half], dso1, preferred_element_type=f32),
                jnp.dot(kot, dso2, preferred_element_type=f32),
            ],
            1,
        )
        dq_ref[:, cols] = (dq * scale).T.astype(bf16)
        pg_ref[:, :width] += jnp.dot(dsp, q, preferred_element_type=f32) * scale
        pg_ref[:, width:] += jnp.dot(wp, do, preferred_element_type=f32)
        dko_acc[:half, :] += jnp.dot(dso1, q[:half], preferred_element_type=f32) * scale
        dko_acc[...] += jnp.dot(dso2, q[half:], preferred_element_type=f32) * scale
        dvo_acc[:half, :] += jnp.dot(wo1, do[:half], preferred_element_type=f32)
        dvo_acc[...] += jnp.dot(wo2, do[half:], preferred_element_type=f32)
        return carry

    lax.fori_loop(0, group_size, head, 0)
    dko_ref[...] = dko_acc[...].astype(bf16)
    dvo_ref[...] = dvo_acc[...].astype(bf16)
    pg_out[:, :width] = pg_ref[:, :width].astype(bf16)
    pg_out[:, width:] = pg_ref[:, width:].astype(bf16)


def attend(length, queries, out_grad, prompt_kv, keys, values, keep, kv_count):
    steps, width = queries.shape
    group_size = width // (kv_count * HEAD_DIM)
    prompt_rows = prompt_kv.shape[0]
    heads = group_size * HEAD_DIM
    kv_block = lambda k, n: (0, k)
    kv_block_t = lambda k, n: (k, 0)
    bf16, f32 = jnp.bfloat16, jnp.float32
    return pl.pallas_call(
        attention_kernel,
        out_shape=(
            jax.ShapeDtypeStruct((steps, width), bf16),
            jax.ShapeDtypeStruct((steps, width), bf16),
            jax.ShapeDtypeStruct(keys.shape, bf16),
            jax.ShapeDtypeStruct(keys.shape, bf16),
            jax.ShapeDtypeStruct((prompt_rows, 2 * kv_count * HEAD_DIM), bf16),
        ),
        grid_spec=pltpu.PrefetchScalarGridSpec(
            num_scalar_prefetch=1,
            grid=(kv_count,),
            in_specs=[
                pl.BlockSpec((steps, heads), kv_block),
                pl.BlockSpec((heads, steps), kv_block_t),
                pl.BlockSpec((steps, heads), kv_block),
                pl.BlockSpec((heads, steps), kv_block_t),
                pl.BlockSpec(memory_space=pltpu.VMEM),
                pl.BlockSpec((steps, HEAD_DIM), kv_block),
                pl.BlockSpec((HEAD_DIM, steps), kv_block_t),
                pl.BlockSpec((steps, HEAD_DIM), kv_block),
                pl.BlockSpec((HEAD_DIM, steps), kv_block_t),
                pl.BlockSpec((steps, 1), lambda k, n: (0, 0)),
                pl.BlockSpec((1, steps), lambda k, n: (0, 0)),
            ],
            out_specs=[
                pl.BlockSpec((steps, heads), kv_block),
                pl.BlockSpec((steps, heads), kv_block),
                pl.BlockSpec((steps, HEAD_DIM), kv_block),
                pl.BlockSpec((steps, HEAD_DIM), kv_block),
                pl.BlockSpec((prompt_rows, 2 * HEAD_DIM), kv_block),
            ],
            scratch_shapes=[pltpu.VMEM((steps, HEAD_DIM), f32)] * 2
            + [pltpu.VMEM((prompt_rows, 2 * HEAD_DIM), f32)]
            + [pltpu.VMEM((HEAD_DIM, prompt_rows), bf16)] * 2,
        ),
        compiler_params=pltpu.CompilerParams(
            dimension_semantics=("arbitrary",),
            vmem_limit_bytes=60 * 1024 * 1024,
        ),
    )(
        length,
        queries,
        queries.T,
        out_grad,
        out_grad.T,
        prompt_kv,
        keys,
        keys.T,
        values,
        values.T,
        keep,
        keep.reshape(1, steps),
    )


def per_device(
    queries, resp_keys, resp_values, prompt_keys, prompt_values, lengths, loss_mask, out_grad
):
    kv_width = resp_keys.shape[2]
    kv_count = kv_width // HEAD_DIM
    rows_here = prompt_keys.shape[0]
    groups = lax.axis_size("head")
    devices = lax.axis_size("resp") * groups
    both = jnp.concatenate(
        [prompt_keys.reshape(rows_here, groups, kv_width), prompt_values.reshape(rows_here, groups, kv_width)],
        2,
    ).transpose(1, 0, 2)
    outgoing = jnp.broadcast_to(both[None], (devices // groups,) + both.shape).reshape(
        devices, rows_here, 2 * kv_width
    )
    gathered = lax.all_to_all(outgoing, ("resp", "head"), split_axis=0, concat_axis=0, tiled=True)
    prompt_kv = gathered.reshape(devices * rows_here, 2 * kv_width)

    steps = queries.shape[1]
    att, dq, dk, dv, prompt_parts = attend(
        lengths,
        queries.reshape(steps, -1),
        out_grad.reshape(steps, -1),
        prompt_kv,
        resp_keys.reshape(steps, kv_width),
        resp_values.reshape(steps, kv_width),
        loss_mask.reshape(steps, 1),
        kv_count,
    )
    arrived = lax.all_to_all(
        prompt_parts.reshape(devices, rows_here, 2 * kv_width),
        ("resp", "head"),
        split_axis=0,
        concat_axis=0,
        tiled=True,
    )
    summed = arrived.astype(jnp.float32).reshape(devices // groups, groups, rows_here, 2 * kv_width).sum(0)
    summed = summed.reshape(groups, rows_here, kv_count, 2, HEAD_DIM).transpose(3, 1, 0, 2, 4)
    prompt_key_grad = summed[0].reshape(rows_here, groups * kv_width)
    prompt_value_grad = summed[1].reshape(rows_here, groups * kv_width)
    return (
        att.reshape(queries.shape),
        dq.reshape(queries.shape),
        dk.reshape(resp_keys.shape),
        dv.reshape(resp_keys.shape),
        prompt_key_grad,
        prompt_value_grad,
    )


def solution(mesh):
    placed = (
        P("resp", None, "head"),
        P("resp", None, "head"),
        P("resp", None, "head"),
        P(("resp", "head"), None),
        P(("resp", "head"), None),
        P("resp"),
        P("resp", None),
        P("resp", None, "head"),
    )
    return jax.shard_map(
        per_device,
        mesh=mesh,
        in_specs=placed,
        out_specs=(
            P("resp", None, "head"),
            P("resp", None, "head"),
            P("resp", None, "head"),
            P("resp", None, "head"),
            P(("resp", "head"), None),
            P(("resp", "head"), None),
        ),
        check_vma=False,
    )
```

```python
import functools

import jax
import jax.numpy as jnp
from jax import lax
from jax.experimental import pallas as pl
from jax.experimental.pallas import tpu as pltpu
from jax.sharding import PartitionSpec as P

HEAD_DIM = 128
NT = (((1,), (1,)), ((), ()))
TN = (((0,), (0,)), ((), ()))


def attention_kernel(
    length_ref, q_all, qt_all, do_all, dot_all, pkv_ref,
    ko_ref, kot_ref, vo_ref, vot_ref, keep_col_ref, keep_row_ref,
    att_ref, dq_ref, dko_ref, dvo_ref, pg_out, dko_acc, dvo_acc, pg_ref, kpt_ref, vpt_ref,
):
    f32, bf16 = jnp.float32, jnp.bfloat16
    scale = HEAD_DIM ** (-0.5)
    length = length_ref[0]
    steps = q_all.shape[0]
    width = HEAD_DIM
    group_size = att_ref.shape[1] // width
    heads = pl.ds(pl.multiple_of(pl.program_id(0) * group_size * width, width), group_size * width)
    q_ref = q_all.at[:, heads]
    qt_ref = qt_all.at[heads, :]
    do_ref = do_all.at[:, heads]
    dot_ref = dot_all.at[heads, :]
    j = lax.broadcasted_iota(jnp.int32, (steps, 1), 0)
    t = lax.broadcasted_iota(jnp.int32, (1, steps), 1)
    half = steps // 2
    allowed1 = (j[:half] <= t[:, :half]) & (j[:half] < length)
    allowed2 = (j <= t[:, half:]) & (j < length)
    live = t < length
    live_col = j < length
    factor_col = (keep_col_ref[...] * live_col.astype(jnp.int32)).astype(bf16)
    factor_row = (keep_row_ref[...] * live.astype(jnp.int32)).astype(bf16)
    k = pl.program_id(0)
    kp_ref = pkv_ref.at[:, pl.ds(pl.multiple_of(k * width, width), width)]
    vp_ref = pkv_ref.at[:, pl.ds(pl.multiple_of((k + pl.num_programs(0)) * width, width), width)]
    kpt_ref[...] = kp_ref[...].astype(f32).T.astype(bf16)
    vpt_ref[...] = vp_ref[...].astype(f32).T.astype(bf16)
    dko_acc[...] = jnp.zeros_like(dko_acc)
    dvo_acc[...] = jnp.zeros_like(dvo_acc)
    pg_ref[...] = jnp.zeros_like(pg_ref)

    def head(h, carry):
        cols = pl.ds(pl.multiple_of(h * width, width), width)
        q = q_ref[:, cols]
        qt = qt_ref[cols, :]
        kp = kp_ref[...]
        ko = ko_ref[...]
        vp = vp_ref[...]
        vo = vo_ref[...]
        sp = jnp.dot(kp, qt, preferred_element_type=f32) * scale
        so1 = jnp.dot(ko[:half], qt[:, :half], preferred_element_type=f32) * scale
        so2 = jnp.dot(ko, qt[:, half:], preferred_element_type=f32) * scale
        so1 = jnp.where(allowed1, so1, -jnp.inf)
        so2 = jnp.where(allowed2, so2, -jnp.inf)
        top = jnp.maximum(
            sp.max(0, keepdims=True),
            jnp.concatenate([so1.max(0, keepdims=True), so2.max(0, keepdims=True)], 1),
        )
        ep = jnp.exp(sp - top)
        eo1 = jnp.exp(so1 - top[:, :half])
        eo2 = jnp.exp(so2 - top[:, half:])
        inverse = 1.0 / (
            ep.sum(0, keepdims=True)
            + jnp.concatenate([eo1.sum(0, keepdims=True), eo2.sum(0, keepdims=True)], 1)
        )
        pp = ep * inverse
        po1 = eo1 * inverse[:, :half]
        po2 = eo2 * inverse[:, half:]
        wp = pp.astype(bf16)
        wo1 = po1.astype(bf16)
        wo2 = po2.astype(bf16)
        vot = vot_ref[...]
        kot = kot_ref[...]
        out = jnp.dot(vpt_ref[...], wp, preferred_element_type=f32) + jnp.concatenate(
            [
                jnp.dot(vot[:, :half], wo1, preferred_element_type=f32),
                jnp.dot(vot, wo2, preferred_element_type=f32),
            ],
            1,
        )
        att = jnp.where(live, out, 0.0).astype(bf16).astype(f32)
        att_ref[:, cols] = att.T.astype(bf16)
        do = do_ref[:, cols] * factor_col
        dot = dot_ref[cols, :] * factor_row
        delta = (dot.astype(f32) * att).sum(0, keepdims=True)
        dpp = jnp.dot(vp, dot, preferred_element_type=f32)
        dpo1 = jnp.dot(vo[:half], dot[:, :half], preferred_element_type=f32)
        dpo2 = jnp.dot(vo, dot[:, half:], preferred_element_type=f32)
        dsp = (pp * (dpp - delta)).astype(bf16)
        dso1 = (po1 * (dpo1 - delta[:, :half])).astype(bf16)
        dso2 = (po2 * (dpo2 - delta[:, half:])).astype(bf16)
        dq = jnp.dot(kpt_ref[...], dsp, preferred_element_type=f32) + jnp.concatenate(
            [
                jnp.dot(kot[:, :half], dso1, preferred_element_type=f32),
                jnp.dot(kot, dso2, preferred_element_type=f32),
            ],
            1,
        )
        dq_ref[:, cols] = (dq * scale).T.astype(bf16)
        pg_ref[:, :width] += jnp.dot(dsp, q, preferred_element_type=f32) * scale
        pg_ref[:, width:] += jnp.dot(wp, do, preferred_element_type=f32)
        dko_acc[:half, :] += jnp.dot(dso1, q[:half], preferred_element_type=f32) * scale
        dko_acc[...] += jnp.dot(dso2, q[half:], preferred_element_type=f32) * scale
        dvo_acc[:half, :] += jnp.dot(wo1, do[:half], preferred_element_type=f32)
        dvo_acc[...] += jnp.dot(wo2, do[half:], preferred_element_type=f32)
        return carry

    lax.fori_loop(0, group_size, head, 0)
    dko_ref[...] = dko_acc[...].astype(bf16)
    dvo_ref[...] = dvo_acc[...].astype(bf16)
    pg_out[:, :width] = pg_ref[:, :width].astype(bf16)
    pg_out[:, width:] = pg_ref[:, width:].astype(bf16)


def attend(length, queries, out_grad, prompt_kv, keys, values, keep, kv_count):
    steps, width = queries.shape
    group_size = width // (kv_count * HEAD_DIM)
    prompt_rows = prompt_kv.shape[0]
    heads = group_size * HEAD_DIM
    kv_block = lambda k, n: (0, k)
    kv_block_t = lambda k, n: (k, 0)
    bf16, f32 = jnp.bfloat16, jnp.float32
    return pl.pallas_call(
        attention_kernel,
        out_shape=(
            jax.ShapeDtypeStruct((steps, width), bf16),
            jax.ShapeDtypeStruct((steps, width), bf16),
            jax.ShapeDtypeStruct(keys.shape, bf16),
            jax.ShapeDtypeStruct(keys.shape, bf16),
            jax.ShapeDtypeStruct((prompt_rows, 2 * kv_count * HEAD_DIM), bf16),
        ),
        grid_spec=pltpu.PrefetchScalarGridSpec(
            num_scalar_prefetch=1,
            grid=(kv_count,),
            in_specs=[
                pl.BlockSpec(memory_space=pltpu.VMEM),
                pl.BlockSpec(memory_space=pltpu.VMEM),
                pl.BlockSpec(memory_space=pltpu.VMEM),
                pl.BlockSpec(memory_space=pltpu.VMEM),
                pl.BlockSpec(memory_space=pltpu.VMEM),
                pl.BlockSpec((steps, HEAD_DIM), kv_block),
                pl.BlockSpec((HEAD_DIM, steps), kv_block_t),
                pl.BlockSpec((steps, HEAD_DIM), kv_block),
                pl.BlockSpec((HEAD_DIM, steps), kv_block_t),
                pl.BlockSpec((steps, 1), lambda k, n: (0, 0)),
                pl.BlockSpec((1, steps), lambda k, n: (0, 0)),
            ],
            out_specs=[
                pl.BlockSpec((steps, heads), kv_block),
                pl.BlockSpec((steps, heads), kv_block),
                pl.BlockSpec((steps, HEAD_DIM), kv_block),
                pl.BlockSpec((steps, HEAD_DIM), kv_block),
                pl.BlockSpec((prompt_rows, 2 * HEAD_DIM), kv_block),
            ],
            scratch_shapes=[pltpu.VMEM((steps, HEAD_DIM), f32)] * 2
            + [pltpu.VMEM((prompt_rows, 2 * HEAD_DIM), f32)]
            + [pltpu.VMEM((HEAD_DIM, prompt_rows), bf16)] * 2,
        ),
        compiler_params=pltpu.CompilerParams(
            dimension_semantics=("arbitrary",),
            vmem_limit_bytes=60 * 1024 * 1024,
        ),
    )(
        length,
        queries,
        queries.T,
        out_grad,
        out_grad.T,
        prompt_kv,
        keys,
        keys.T,
        values,
        values.T,
        keep,
        keep.reshape(1, steps),
    )


def per_device(
    queries, resp_keys, resp_values, prompt_keys, prompt_values, lengths, loss_mask, out_grad
):
    kv_width = resp_keys.shape[2]
    kv_count = kv_width // HEAD_DIM
    rows_here = prompt_keys.shape[0]
    groups = lax.axis_size("head")
    devices = lax.axis_size("resp") * groups
    both = jnp.concatenate(
        [prompt_keys.reshape(rows_here, groups, kv_width), prompt_values.reshape(rows_here, groups, kv_width)],
        2,
    ).transpose(1, 0, 2)
    outgoing = jnp.broadcast_to(both[None], (devices // groups,) + both.shape).reshape(
        devices, rows_here, 2 * kv_width
    )
    gathered = lax.all_to_all(outgoing, ("resp", "head"), split_axis=0, concat_axis=0, tiled=True)
    prompt_kv = gathered.reshape(devices * rows_here, 2 * kv_width)

    steps = queries.shape[1]
    att, dq, dk, dv, prompt_parts = attend(
        lengths,
        queries.reshape(steps, -1),
        out_grad.reshape(steps, -1),
        prompt_kv,
        resp_keys.reshape(steps, kv_width),
        resp_values.reshape(steps, kv_width),
        loss_mask.reshape(steps, 1),
        kv_count,
    )
    arrived = lax.all_to_all(
        prompt_parts.reshape(devices, rows_here, 2 * kv_width),
        ("resp", "head"),
        split_axis=0,
        concat_axis=0,
        tiled=True,
    )
    summed = arrived.astype(jnp.float32).reshape(devices // groups, groups, rows_here, 2 * kv_width).sum(0)
    summed = summed.reshape(groups, rows_here, kv_count, 2, HEAD_DIM).transpose(3, 1, 0, 2, 4)
    prompt_key_grad = summed[0].reshape(rows_here, groups * kv_width)
    prompt_value_grad = summed[1].reshape(rows_here, groups * kv_width)
    return (
        att.reshape(queries.shape),
        dq.reshape(queries.shape),
        dk.reshape(resp_keys.shape),
        dv.reshape(resp_keys.shape),
        prompt_key_grad,
        prompt_value_grad,
    )


def solution(mesh):
    placed = (
        P("resp", None, "head"),
        P("resp", None, "head"),
        P("resp", None, "head"),
        P(("resp", "head"), None),
        P(("resp", "head"), None),
        P("resp"),
        P("resp", None),
        P("resp", None, "head"),
    )
    return jax.shard_map(
        per_device,
        mesh=mesh,
        in_specs=placed,
        out_specs=(
            P("resp", None, "head"),
            P("resp", None, "head"),
            P("resp", None, "head"),
            P("resp", None, "head"),
            P(("resp", "head"), None),
            P(("resp", "head"), None),
        ),
        check_vma=False,
    )
```

```python
import functools

import jax
import jax.numpy as jnp
from jax import lax
from jax.experimental import pallas as pl
from jax.experimental.pallas import tpu as pltpu
from jax.sharding import PartitionSpec as P

HEAD_DIM = 128
NT = (((1,), (1,)), ((), ()))
TN = (((0,), (0,)), ((), ()))


def attention_kernel(
    length_ref, q_ref, qt_ref, do_ref, dot_ref, pkv_ref,
    ko_ref, kot_ref, vo_ref, vot_ref, keep_col_ref, keep_row_ref,
    att_ref, dq_ref, dko_ref, dvo_ref, pg_out, dko_acc, dvo_acc, pg_ref, kpt_ref, vpt_ref,
):
    f32, bf16 = jnp.float32, jnp.bfloat16
    scale = HEAD_DIM ** (-0.5)
    length = length_ref[0]
    steps = q_ref.shape[0]
    width = HEAD_DIM
    group_size = q_ref.shape[1] // width
    j = lax.broadcasted_iota(jnp.int32, (steps, 1), 0)
    t = lax.broadcasted_iota(jnp.int32, (1, steps), 1)
    half = steps // 2
    allowed1 = (j[:half] <= t[:, :half]) & (j[:half] < length)
    allowed2 = (j <= t[:, half:]) & (j < length)
    live = t < length
    live_col = j < length
    factor_col = (keep_col_ref[...] * live_col.astype(jnp.int32)).astype(bf16)
    factor_row = (keep_row_ref[...] * live.astype(jnp.int32)).astype(bf16)
    k = pl.program_id(0)
    kp_ref = pkv_ref.at[:, pl.ds(pl.multiple_of(k * width, width), width)]
    vp_ref = pkv_ref.at[:, pl.ds(pl.multiple_of((k + pl.num_programs(0)) * width, width), width)]
    kpt_ref[...] = kp_ref[...].astype(f32).T.astype(bf16)
    vpt_ref[...] = vp_ref[...].astype(f32).T.astype(bf16)
    dko_acc[...] = jnp.zeros_like(dko_acc)
    dvo_acc[...] = jnp.zeros_like(dvo_acc)
    pg_ref[...] = jnp.zeros_like(pg_ref)

    def head(h, carry):
        cols = pl.ds(pl.multiple_of(h * width, width), width)
        q = q_ref[:, cols]
        qt = qt_ref[cols, :]
        kp = kp_ref[...]
        ko = ko_ref[...]
        vp = vp_ref[...]
        vo = vo_ref[...]
        sp = jnp.dot(kp, qt, preferred_element_type=f32) * scale
        so1 = jnp.dot(ko[:half], qt[:, :half], preferred_element_type=f32) * scale
        so2 = jnp.dot(ko, qt[:, half:], preferred_element_type=f32) * scale
        so1 = jnp.where(allowed1, so1, -jnp.inf)
        so2 = jnp.where(allowed2, so2, -jnp.inf)
        top = jnp.maximum(
            sp.max(0, keepdims=True),
            jnp.concatenate([so1.max(0, keepdims=True), so2.max(0, keepdims=True)], 1),
        )
        ep = jnp.exp(sp - top)
        eo1 = jnp.exp(so1 - top[:, :half])
        eo2 = jnp.exp(so2 - top[:, half:])
        inverse = 1.0 / (
            ep.sum(0, keepdims=True)
            + jnp.concatenate([eo1.sum(0, keepdims=True), eo2.sum(0, keepdims=True)], 1)
        )
        pp = ep * inverse
        po1 = eo1 * inverse[:, :half]
        po2 = eo2 * inverse[:, half:]
        wp = pp.astype(bf16)
        wo1 = po1.astype(bf16)
        wo2 = po2.astype(bf16)
        vot = vot_ref[...]
        kot = kot_ref[...]
        out = jnp.dot(vpt_ref[...], wp, preferred_element_type=f32) + jnp.concatenate(
            [
                jnp.dot(vot[:, :half], wo1, preferred_element_type=f32),
                jnp.dot(vot, wo2, preferred_element_type=f32),
            ],
            1,
        )
        att = jnp.where(live, out, 0.0).astype(bf16).astype(f32)
        att_ref[:, cols] = att.T.astype(bf16)
        do = do_ref[:, cols] * factor_col
        dot = dot_ref[cols, :] * factor_row
        delta = (dot.astype(f32) * att).sum(0, keepdims=True)
        dpp = jnp.dot(vp, dot, preferred_element_type=f32)
        dpo1 = jnp.dot(vo[:half], dot[:, :half], preferred_element_type=f32)
        dpo2 = jnp.dot(vo, dot[:, half:], preferred_element_type=f32)
        dsp = (pp * (dpp - delta)).astype(bf16)
        dso1 = (po1 * (dpo1 - delta[:, :half])).astype(bf16)
        dso2 = (po2 * (dpo2 - delta[:, half:])).astype(bf16)
        dq = jnp.dot(kpt_ref[...], dsp, preferred_element_type=f32) + jnp.concatenate(
            [
                jnp.dot(kot[:, :half], dso1, preferred_element_type=f32),
                jnp.dot(kot, dso2, preferred_element_type=f32),
            ],
            1,
        )
        dq_ref[:, cols] = (dq * scale).T.astype(bf16)
        pg_ref[:, :width] += jnp.dot(dsp, q, preferred_element_type=f32) * scale
        pg_ref[:, width:] += jnp.dot(wp, do, preferred_element_type=f32)
        dko_acc[:half, :] += jnp.dot(dso1, q[:half], preferred_element_type=f32) * scale
        dko_acc[...] += jnp.dot(dso2, q[half:], preferred_element_type=f32) * scale
        dvo_acc[:half, :] += jnp.dot(wo1, do[:half], preferred_element_type=f32)
        dvo_acc[...] += jnp.dot(wo2, do[half:], preferred_element_type=f32)
        return carry

    lax.fori_loop(0, group_size, head, 0)
    dko_ref[...] = dko_acc[...].astype(bf16)
    dvo_ref[...] = dvo_acc[...].astype(bf16)
    window = pl.ds(pl.multiple_of(pl.program_id(0) * 2 * width, width), 2 * width)
    pg_out[:, window] = pg_ref[...].astype(bf16)


def attend(length, queries, out_grad, prompt_kv, keys, values, keep, kv_count):
    steps, width = queries.shape
    group_size = width // (kv_count * HEAD_DIM)
    prompt_rows = prompt_kv.shape[0]
    heads = group_size * HEAD_DIM
    kv_block = lambda k, n: (0, k)
    kv_block_t = lambda k, n: (k, 0)
    bf16, f32 = jnp.bfloat16, jnp.float32
    return pl.pallas_call(
        attention_kernel,
        out_shape=(
            jax.ShapeDtypeStruct((steps, width), bf16),
            jax.ShapeDtypeStruct((steps, width), bf16),
            jax.ShapeDtypeStruct(keys.shape, bf16),
            jax.ShapeDtypeStruct(keys.shape, bf16),
            jax.ShapeDtypeStruct((prompt_rows, 2 * kv_count * HEAD_DIM), bf16),
        ),
        grid_spec=pltpu.PrefetchScalarGridSpec(
            num_scalar_prefetch=1,
            grid=(kv_count,),
            in_specs=[
                pl.BlockSpec((steps, heads), kv_block),
                pl.BlockSpec((heads, steps), kv_block_t),
                pl.BlockSpec((steps, heads), kv_block),
                pl.BlockSpec((heads, steps), kv_block_t),
                pl.BlockSpec(memory_space=pltpu.VMEM),
                pl.BlockSpec((steps, HEAD_DIM), kv_block),
                pl.BlockSpec((HEAD_DIM, steps), kv_block_t),
                pl.BlockSpec((steps, HEAD_DIM), kv_block),
                pl.BlockSpec((HEAD_DIM, steps), kv_block_t),
                pl.BlockSpec((steps, 1), lambda k, n: (0, 0)),
                pl.BlockSpec((1, steps), lambda k, n: (0, 0)),
            ],
            out_specs=[
                pl.BlockSpec((steps, heads), kv_block),
                pl.BlockSpec((steps, heads), kv_block),
                pl.BlockSpec((steps, HEAD_DIM), kv_block),
                pl.BlockSpec((steps, HEAD_DIM), kv_block),
                pl.BlockSpec(memory_space=pltpu.VMEM),
            ],
            scratch_shapes=[pltpu.VMEM((steps, HEAD_DIM), f32)] * 2
            + [pltpu.VMEM((prompt_rows, 2 * HEAD_DIM), f32)]
            + [pltpu.VMEM((HEAD_DIM, prompt_rows), bf16)] * 2,
        ),
        compiler_params=pltpu.CompilerParams(
            dimension_semantics=("arbitrary",),
            vmem_limit_bytes=60 * 1024 * 1024,
        ),
    )(
        length,
        queries,
        queries.T,
        out_grad,
        out_grad.T,
        prompt_kv,
        keys,
        keys.T,
        values,
        values.T,
        keep,
        keep.reshape(1, steps),
    )


def per_device(
    queries, resp_keys, resp_values, prompt_keys, prompt_values, lengths, loss_mask, out_grad
):
    kv_width = resp_keys.shape[2]
    kv_count = kv_width // HEAD_DIM
    rows_here = prompt_keys.shape[0]
    groups = lax.axis_size("head")
    devices = lax.axis_size("resp") * groups
    both = jnp.concatenate(
        [prompt_keys.reshape(rows_here, groups, kv_width), prompt_values.reshape(rows_here, groups, kv_width)],
        2,
    ).transpose(1, 0, 2)
    outgoing = jnp.broadcast_to(both[None], (devices // groups,) + both.shape).reshape(
        devices, rows_here, 2 * kv_width
    )
    gathered = lax.all_to_all(outgoing, ("resp", "head"), split_axis=0, concat_axis=0, tiled=True)
    prompt_kv = gathered.reshape(devices * rows_here, 2 * kv_width)

    steps = queries.shape[1]
    att, dq, dk, dv, prompt_parts = attend(
        lengths,
        queries.reshape(steps, -1),
        out_grad.reshape(steps, -1),
        prompt_kv,
        resp_keys.reshape(steps, kv_width),
        resp_values.reshape(steps, kv_width),
        loss_mask.reshape(steps, 1),
        kv_count,
    )
    arrived = lax.all_to_all(
        prompt_parts.reshape(devices, rows_here, 2 * kv_width),
        ("resp", "head"),
        split_axis=0,
        concat_axis=0,
        tiled=True,
    )
    summed = arrived.astype(jnp.float32).reshape(devices // groups, groups, rows_here, 2 * kv_width).sum(0)
    summed = summed.reshape(groups, rows_here, kv_count, 2, HEAD_DIM).transpose(3, 1, 0, 2, 4)
    prompt_key_grad = summed[0].reshape(rows_here, groups * kv_width)
    prompt_value_grad = summed[1].reshape(rows_here, groups * kv_width)
    return (
        att.reshape(queries.shape),
        dq.reshape(queries.shape),
        dk.reshape(resp_keys.shape),
        dv.reshape(resp_keys.shape),
        prompt_key_grad,
        prompt_value_grad,
    )


def solution(mesh):
    placed = (
        P("resp", None, "head"),
        P("resp", None, "head"),
        P("resp", None, "head"),
        P(("resp", "head"), None),
        P(("resp", "head"), None),
        P("resp"),
        P("resp", None),
        P("resp", None, "head"),
    )
    return jax.shard_map(
        per_device,
        mesh=mesh,
        in_specs=placed,
        out_specs=(
            P("resp", None, "head"),
            P("resp", None, "head"),
            P("resp", None, "head"),
            P("resp", None, "head"),
            P(("resp", "head"), None),
            P(("resp", "head"), None),
        ),
        check_vma=False,
    )
```

```python
import functools

import jax
import jax.numpy as jnp
from jax import lax
from jax.experimental import pallas as pl
from jax.experimental.pallas import tpu as pltpu
from jax.sharding import PartitionSpec as P

HEAD_DIM = 128
NT = (((1,), (1,)), ((), ()))
TN = (((0,), (0,)), ((), ()))


def attention_kernel(
    length_ref, q_ref, qt_ref, do_ref, dot_ref, pkv_ref,
    ko_ref, kot_ref, vo_ref, vot_ref, keep_col_ref, keep_row_ref,
    att_ref, dq_ref, dko_ref, dvo_ref, pg_out, dko_acc, dvo_acc, pg_ref, kpt_ref, vpt_ref,
):
    f32, bf16 = jnp.float32, jnp.bfloat16
    scale = HEAD_DIM ** (-0.5)
    length = length_ref[0]
    steps = q_ref.shape[0]
    width = HEAD_DIM
    group_size = q_ref.shape[1] // width
    j = lax.broadcasted_iota(jnp.int32, (steps, 1), 0)
    t = lax.broadcasted_iota(jnp.int32, (1, steps), 1)
    half = steps // 2
    allowed1 = (j[:half] <= t[:, :half]) & (j[:half] < length)
    allowed2 = (j <= t[:, half:]) & (j < length)
    live = t < length
    live_col = j < length
    factor_col = (keep_col_ref[...] * live_col.astype(jnp.int32)).astype(bf16)
    factor_row = (keep_row_ref[...] * live.astype(jnp.int32)).astype(bf16)
    k = pl.program_id(0)
    kp_ref = pkv_ref.at[:, pl.ds(pl.multiple_of(k * width, width), width)]
    vp_ref = pkv_ref.at[:, pl.ds(pl.multiple_of((k + pl.num_programs(0)) * width, width), width)]
    kpt_ref[...] = kp_ref[...].astype(f32).T.astype(bf16)
    vpt_ref[...] = vp_ref[...].astype(f32).T.astype(bf16)
    dko_acc[...] = jnp.zeros_like(dko_acc)
    dvo_acc[...] = jnp.zeros_like(dvo_acc)
    pg_ref[...] = jnp.zeros_like(pg_ref)

    def head(h, carry):
        cols = pl.ds(pl.multiple_of(h * width, width), width)
        q = q_ref[:, cols]
        qt = qt_ref[cols, :]
        kp = kp_ref[...]
        ko = ko_ref[...]
        vp = vp_ref[...]
        vo = vo_ref[...]
        sp = jnp.dot(kp, qt, preferred_element_type=f32) * scale
        so1 = jnp.dot(ko[:half], qt[:, :half], preferred_element_type=f32) * scale
        so2 = jnp.dot(ko, qt[:, half:], preferred_element_type=f32) * scale
        so1 = jnp.where(allowed1, so1, -jnp.inf)
        so2 = jnp.where(allowed2, so2, -jnp.inf)
        top = jnp.maximum(
            sp.max(0, keepdims=True),
            jnp.concatenate([so1.max(0, keepdims=True), so2.max(0, keepdims=True)], 1),
        )
        ep = jnp.exp(sp - top)
        eo1 = jnp.exp(so1 - top[:, :half])
        eo2 = jnp.exp(so2 - top[:, half:])
        inverse = 1.0 / (
            ep.sum(0, keepdims=True)
            + jnp.concatenate([eo1.sum(0, keepdims=True), eo2.sum(0, keepdims=True)], 1)
        )
        pp = ep * inverse
        po1 = eo1 * inverse[:, :half]
        po2 = eo2 * inverse[:, half:]
        wp = pp.astype(bf16)
        wo1 = po1.astype(bf16)
        wo2 = po2.astype(bf16)
        vot = vot_ref[...]
        kot = kot_ref[...]
        out = jnp.dot(vpt_ref[...], wp, preferred_element_type=f32) + jnp.concatenate(
            [
                jnp.dot(vot[:, :half], wo1, preferred_element_type=f32),
                jnp.dot(vot, wo2, preferred_element_type=f32),
            ],
            1,
        )
        att = jnp.where(live, out, 0.0).astype(bf16).astype(f32)
        att_ref[:, cols] = att.T.astype(bf16)
        do = do_ref[:, cols] * factor_col
        dot = dot_ref[cols, :] * factor_row
        delta = (dot.astype(f32) * att).sum(0, keepdims=True)
        dpp = jnp.dot(vp, dot, preferred_element_type=f32)
        dpo1 = jnp.dot(vo[:half], dot[:, :half], preferred_element_type=f32)
        dpo2 = jnp.dot(vo, dot[:, half:], preferred_element_type=f32)
        dsp = (pp * (dpp - delta)).astype(bf16)
        dso1 = (po1 * (dpo1 - delta[:, :half])).astype(bf16)
        dso2 = (po2 * (dpo2 - delta[:, half:])).astype(bf16)
        dq = jnp.dot(kpt_ref[...], dsp, preferred_element_type=f32) + jnp.concatenate(
            [
                jnp.dot(kot[:, :half], dso1, preferred_element_type=f32),
                jnp.dot(kot, dso2, preferred_element_type=f32),
            ],
            1,
        )
        dq_ref[:, cols] = (dq * scale).T.astype(bf16)
        pg_ref[:, :width] += jnp.dot(dsp, q, preferred_element_type=f32)
        pg_ref[:, width:] += jnp.dot(wp, do, preferred_element_type=f32)
        dko_acc[:half, :] += jnp.dot(dso1, q[:half], preferred_element_type=f32)
        dko_acc[...] += jnp.dot(dso2, q[half:], preferred_element_type=f32)
        dvo_acc[:half, :] += jnp.dot(wo1, do[:half], preferred_element_type=f32)
        dvo_acc[...] += jnp.dot(wo2, do[half:], preferred_element_type=f32)
        return carry

    lax.fori_loop(0, group_size, head, 0)
    dko_ref[...] = (dko_acc[...] * scale).astype(bf16)
    dvo_ref[...] = dvo_acc[...].astype(bf16)
    pg_out[:, :width] = (pg_ref[:, :width] * scale).astype(bf16)
    pg_out[:, width:] = pg_ref[:, width:].astype(bf16)


def attend(length, queries, out_grad, prompt_kv, keys, values, keep, kv_count):
    steps, width = queries.shape
    group_size = width // (kv_count * HEAD_DIM)
    prompt_rows = prompt_kv.shape[0]
    heads = group_size * HEAD_DIM
    kv_block = lambda k, n: (0, k)
    kv_block_t = lambda k, n: (k, 0)
    bf16, f32 = jnp.bfloat16, jnp.float32
    return pl.pallas_call(
        attention_kernel,
        out_shape=(
            jax.ShapeDtypeStruct((steps, width), bf16),
            jax.ShapeDtypeStruct((steps, width), bf16),
            jax.ShapeDtypeStruct(keys.shape, bf16),
            jax.ShapeDtypeStruct(keys.shape, bf16),
            jax.ShapeDtypeStruct((prompt_rows, 2 * kv_count * HEAD_DIM), bf16),
        ),
        grid_spec=pltpu.PrefetchScalarGridSpec(
            num_scalar_prefetch=1,
            grid=(kv_count,),
            in_specs=[
                pl.BlockSpec((steps, heads), kv_block),
                pl.BlockSpec((heads, steps), kv_block_t),
                pl.BlockSpec((steps, heads), kv_block),
                pl.BlockSpec((heads, steps), kv_block_t),
                pl.BlockSpec(memory_space=pltpu.VMEM),
                pl.BlockSpec((steps, HEAD_DIM), kv_block),
                pl.BlockSpec((HEAD_DIM, steps), kv_block_t),
                pl.BlockSpec((steps, HEAD_DIM), kv_block),
                pl.BlockSpec((HEAD_DIM, steps), kv_block_t),
                pl.BlockSpec((steps, 1), lambda k, n: (0, 0)),
                pl.BlockSpec((1, steps), lambda k, n: (0, 0)),
            ],
            out_specs=[
                pl.BlockSpec((steps, heads), kv_block),
                pl.BlockSpec((steps, heads), kv_block),
                pl.BlockSpec((steps, HEAD_DIM), kv_block),
                pl.BlockSpec((steps, HEAD_DIM), kv_block),
                pl.BlockSpec((prompt_rows, 2 * HEAD_DIM), kv_block),
            ],
            scratch_shapes=[pltpu.VMEM((steps, HEAD_DIM), f32)] * 2
            + [pltpu.VMEM((prompt_rows, 2 * HEAD_DIM), f32)]
            + [pltpu.VMEM((HEAD_DIM, prompt_rows), bf16)] * 2,
        ),
        compiler_params=pltpu.CompilerParams(
            dimension_semantics=("arbitrary",),
            vmem_limit_bytes=60 * 1024 * 1024,
        ),
    )(
        length,
        queries,
        queries.T,
        out_grad,
        out_grad.T,
        prompt_kv,
        keys,
        keys.T,
        values,
        values.T,
        keep,
        keep.reshape(1, steps),
    )


def per_device(
    queries, resp_keys, resp_values, prompt_keys, prompt_values, lengths, loss_mask, out_grad
):
    kv_width = resp_keys.shape[2]
    kv_count = kv_width // HEAD_DIM
    rows_here = prompt_keys.shape[0]
    groups = lax.axis_size("head")
    devices = lax.axis_size("resp") * groups
    both = jnp.concatenate(
        [prompt_keys.reshape(rows_here, groups, kv_width), prompt_values.reshape(rows_here, groups, kv_width)],
        2,
    ).transpose(1, 0, 2)
    outgoing = jnp.broadcast_to(both[None], (devices // groups,) + both.shape).reshape(
        devices, rows_here, 2 * kv_width
    )
    gathered = lax.all_to_all(outgoing, ("resp", "head"), split_axis=0, concat_axis=0, tiled=True)
    prompt_kv = gathered.reshape(devices * rows_here, 2 * kv_width)

    steps = queries.shape[1]
    att, dq, dk, dv, prompt_parts = attend(
        lengths,
        queries.reshape(steps, -1),
        out_grad.reshape(steps, -1),
        prompt_kv,
        resp_keys.reshape(steps, kv_width),
        resp_values.reshape(steps, kv_width),
        loss_mask.reshape(steps, 1),
        kv_count,
    )
    arrived = lax.all_to_all(
        prompt_parts.reshape(devices, rows_here, 2 * kv_width),
        ("resp", "head"),
        split_axis=0,
        concat_axis=0,
        tiled=True,
    )
    summed = arrived.astype(jnp.float32).reshape(devices // groups, groups, rows_here, 2 * kv_width).sum(0)
    summed = summed.reshape(groups, rows_here, kv_count, 2, HEAD_DIM).transpose(3, 1, 0, 2, 4)
    prompt_key_grad = summed[0].reshape(rows_here, groups * kv_width)
    prompt_value_grad = summed[1].reshape(rows_here, groups * kv_width)
    return (
        att.reshape(queries.shape),
        dq.reshape(queries.shape),
        dk.reshape(resp_keys.shape),
        dv.reshape(resp_keys.shape),
        prompt_key_grad,
        prompt_value_grad,
    )


def solution(mesh):
    placed = (
        P("resp", None, "head"),
        P("resp", None, "head"),
        P("resp", None, "head"),
        P(("resp", "head"), None),
        P(("resp", "head"), None),
        P("resp"),
        P("resp", None),
        P("resp", None, "head"),
    )
    return jax.shard_map(
        per_device,
        mesh=mesh,
        in_specs=placed,
        out_specs=(
            P("resp", None, "head"),
            P("resp", None, "head"),
            P("resp", None, "head"),
            P("resp", None, "head"),
            P(("resp", "head"), None),
            P(("resp", "head"), None),
        ),
        check_vma=False,
    )
```
